32 devices in a mesh: src: 4 (over y, core), rcv: 8 (over z, x).
Axes of the slice: x: 2, y: 2, z: 4, core: 2. Of those that a mesh axis runs over, the one named last changes fastest.
Arguments:
- data: bfloat16 [2, 4096, 4096], P(None, ('src', 'rcv')), may hold values from -0.8984375 to 0.8984375
- fill_mask: int32 [4096, 4096], P(('src', 'rcv')), may hold values 0 or 1
- obliquity: float32 [4096], replicated, may hold values from 0.25 to 4
- aperture: int32 [8, 8, 8], P('src'), may hold values from 0 to 7, as said below
- lengths: int32 [8, 8], P('src', 'rcv'), may hold values from 1 to 8, as said below
Outputs:
- predicted: float32 [2, 4096, 4096], P(None, 'src', 'rcv')
The draws below stay inside these ranges and needn't reach their ends.
Inputs may be any that keep to these rules, and one draw needn't show every extreme that they name: `aperture`: every entry is a tile index; the 8 entries of one output tile are distinct; only the first lengths entries of a list are used. `lengths`: some output tile uses all 8 entries of its list.
All inputs are finite; a program needn't handle non-finite values. No bound on the sum of `fill_mask` on one device may be relied on, other than what follows from the above.
Results may differ from the reference program's by a relative error of at most 0.0028.
Values may be sent and summed in bfloat16 or wider, within the bound.
No kernel may reach another device: no remote copies, remote signals or barrier semaphores. Data moves between devices by JAX's collectives and lax.ppermute only.
A program may use at most 128 MiB of HBM per device.

```python
import math
import jax
import jax.numpy as jnp
from jax import lax

TILE_SIZE = 512
MAX_SLOTS = 8
TILE_COUNT = 8
STATIONS = 4096


def draw_aperture(key, part):
    local_key = jax.random.fold_in(key, 11)
    scores = jax.random.randint(local_key, (TILE_COUNT, TILE_COUNT, TILE_COUNT), 0, 2 ** 20, dtype=jnp.int32)
    scores = scores * TILE_COUNT + jnp.arange(TILE_COUNT, dtype=jnp.int32)
    ordering = jnp.argsort(scores, axis=-1, stable=True)
    return ordering[:, :, :MAX_SLOTS].astype(jnp.int32)


def draw_lengths(key, part):
    local_key = jax.random.fold_in(key, 23)
    first_key, second_key, third_key = jax.random.split(local_key, 3)
    first_draw = jax.random.randint(first_key, (TILE_COUNT, TILE_COUNT), 0, MAX_SLOTS, dtype=jnp.int32)
    second_draw = jax.random.randint(second_key, (TILE_COUNT, TILE_COUNT), 0, MAX_SLOTS, dtype=jnp.int32)
    counts = MAX_SLOTS - first_draw * second_draw // (MAX_SLOTS - 1)
    forced = jax.random.randint(third_key, (), 0, TILE_COUNT * TILE_COUNT, dtype=jnp.int32)
    counts = counts.reshape(-1).at[forced].set(MAX_SLOTS)
    return counts.reshape(TILE_COUNT, TILE_COUNT).astype(jnp.int32)


def plant(array, own_key, smallest, largest):
    dims = array.shape
    index_at = [jax.random.randint(jax.random.fold_in(own_key, axis), (), 0, dims[axis]) for axis in range(len(dims))]
    array = array.at[tuple(index_at)].set(smallest)
    longest = dims.index(max(dims))
    index_at[longest] = (index_at[longest] + 1) % dims[longest]
    return array.at[tuple(index_at)].set(largest)


def level_of(key, extent, pieces, least, top_value):
    gain, own = 1.0, jax.random.fold_in(key, 6)
    for position, shards_of in pieces:
        draws = jnp.exp(jax.random.uniform(jax.random.fold_in(own, position), (shards_of,), jnp.float32, least / len(pieces), top_value / len(pieces)))
        gain = gain * jnp.repeat(draws, extent[position] // shards_of).reshape([-1 if axis == position else 1 for axis in range(len(extent))])
    return gain


def gaussian(own_key, dims, deviation, most, pieces=(), kind=jnp.bfloat16):
    factor_of = level_of(own_key, dims, pieces, -0.22, 0.18) if pieces else 1.0
    result = jax.random.normal(own_key, dims, jnp.float32) * deviation * factor_of
    return jnp.minimum(jnp.maximum(result, -most), most).astype(kind)


def setup_inputs(seed: int = 0) -> dict:
    keys = jax.random.split(jax.random.key(seed), 6)
    return {
        "data": gaussian(keys[0], (2, STATIONS, STATIONS), 0.15, 0.8984375, ((1, 32),)),
        "fill_mask": plant((jax.random.randint(keys[1], (STATIONS, STATIONS), 0, 3) < 2).astype(jnp.int32), jax.random.fold_in(keys[1], 1), 0, 1),
        "obliquity": jnp.clip(jnp.exp(jax.random.uniform(keys[2], (STATIONS,), jnp.float32, math.log(0.25), math.log(4.0))), 0.25, 4.0),
        "aperture": draw_aperture(jax.random.fold_in(keys[5], 71), 0),
        "lengths": draw_lengths(jax.random.fold_in(keys[5], 71), 0),
    }


def complex_product(left_pair, right_pair):
    left_wide = jnp.concatenate([left_pair[0], left_pair[1]], axis=1)
    upper = jnp.concatenate([right_pair[0], right_pair[1]], axis=1)
    lower = jnp.concatenate([-right_pair[1], right_pair[0]], axis=1)
    right_wide = jnp.concatenate([upper, lower], axis=0)
    return jnp.dot(left_wide, right_wide, preferred_element_type=jnp.float32)


def reference(data, fill_mask, obliquity, aperture, lengths):
    transposed = jnp.swapaxes(data, 1, 2)
    filled = jnp.where(fill_mask[None] == 1, data, transposed)
    weighted = (filled.astype(jnp.float32) * obliquity[None, :, None]).astype(jnp.bfloat16)

    def predict_tile(flat_index):
        tile_row = (flat_index // TILE_COUNT).astype(jnp.int32)
        tile_col = (flat_index % TILE_COUNT).astype(jnp.int32)

        def add_slot(slot_index, summed):
            inner_tile = aperture[tile_row, tile_col, slot_index].astype(jnp.int32)
            left_pair = lax.dynamic_slice(filled, (jnp.int32(0), tile_row * TILE_SIZE, inner_tile * TILE_SIZE), (2, TILE_SIZE, TILE_SIZE))
            right_pair = lax.dynamic_slice(weighted, (jnp.int32(0), inner_tile * TILE_SIZE, tile_col * TILE_SIZE), (2, TILE_SIZE, TILE_SIZE))
            return summed + complex_product(left_pair, right_pair)

        initial = jnp.zeros((TILE_SIZE, 2 * TILE_SIZE), jnp.float32)
        return -lax.fori_loop(0, lengths[tile_row, tile_col], add_slot, initial)

    results = lax.map(predict_tile, jnp.arange(TILE_COUNT * TILE_COUNT, dtype=jnp.int32))
    results = results.reshape(TILE_COUNT, TILE_COUNT, TILE_SIZE, 2, TILE_SIZE)
    results = jnp.transpose(results, (3, 0, 2, 1, 4))
    return results.reshape(2, STATIONS, STATIONS)
```

```python
import functools

import jax
import jax.numpy as jnp
from jax import lax
from jax.experimental import pallas as pl
from jax.experimental.pallas import tpu as pltpu
from jax.sharding import PartitionSpec as P

TILE_SIZE = 512


def ring_order(count):
    return list(range(0, count, 2)) + list(range(1, count, 2))[::-1]


def split_kernel(data_ref, out_ref):
    rows = data_ref.shape[1]
    for block in range(out_ref.shape[0]):
        for part in range(2):
            piece = data_ref[part, :, block * rows : (block + 1) * rows]
            out_ref[block, part] = piece.T


def transposed_blocks(data, devices):
    _, rows, total = data.shape
    if rows % 128:
        return jnp.transpose(data.reshape(2, rows, devices, rows), (2, 0, 3, 1))
    group = 4
    return pl.pallas_call(
        split_kernel,
        out_shape=jax.ShapeDtypeStruct((devices, 2, rows, rows), data.dtype),
        grid=(devices // group,),
        in_specs=[pl.BlockSpec((2, rows, group * rows), lambda i: (0, 0, i))],
        out_specs=pl.BlockSpec((group, 2, rows, rows), lambda i: (i, 0, 0, 0)),
    )(data)


def fill_kernel(data_ref, mask_ref, arrived_ref, first_ref, second_ref):
    rows = data_ref.shape[1]
    for block in range(arrived_ref.shape[0]):
        span = slice(block * rows, (block + 1) * rows)
        keep = mask_ref[:, span] == 1
        for part, out_ref in enumerate((first_ref, second_ref)):
            out_ref[:, span] = jnp.where(keep, data_ref[part, :, span], arrived_ref[block, part])


def fill(data, mask, arrived):
    _, rows, total = data.shape
    devices = arrived.shape[0]
    if rows % 128:
        transposed = jnp.transpose(arrived, (1, 2, 0, 3)).reshape(2, rows, total)
        filled = jnp.where(mask[None] == 1, data, transposed)
        return filled[0], filled[1]
    group = 4
    plane = jax.ShapeDtypeStruct((rows, total), data.dtype)
    return pl.pallas_call(
        fill_kernel,
        out_shape=(plane, plane),
        grid=(devices // group,),
        in_specs=[
            pl.BlockSpec((2, rows, group * rows), lambda i: (0, 0, i)),
            pl.BlockSpec((rows, group * rows), lambda i: (0, i)),
            pl.BlockSpec((group, 2, rows, rows), lambda i: (i, 0, 0, 0)),
        ],
        out_specs=(pl.BlockSpec((rows, group * rows), lambda i: (0, i)),) * 2,
    )(data, mask, arrived)


def product_kernel(rows, src_count, plan_ref, used_ref, *refs):
    (row_refs, piece_refs), out_ref, scratch = refs[0], refs[1], refs[2:]
    left, right, row_sem, piece_sem = scratch
    inner_tiles = right.shape[0]
    out_tiles = out_ref.shape[1] // TILE_SIZE

    def piece_copies():
        copies = []
        at = len(row_refs)
        for ref in piece_refs:
            for index in range(ref.shape[0]):
                first = plan_ref[at]
                tile, offset = first // TILE_SIZE, first % TILE_SIZE
                for part in range(2):
                    row = pl.multiple_of(offset + (1 - part) * TILE_SIZE, rows)
                    copies.append(
                        pltpu.make_async_copy(
                            ref.at[index, part],
                            right.at[tile, pl.ds(row, rows), :],
                            piece_sem,
                        )
                    )
                at += 1
        return copies

    def start_rows(tile):
        for index, (ref, part) in enumerate(row_refs):
            row = pl.multiple_of(plan_ref[index], rows)
            column = pl.multiple_of(tile * 2 * TILE_SIZE + part * TILE_SIZE, TILE_SIZE)
            pltpu.make_async_copy(
                ref.at[:, pl.ds(pl.multiple_of(tile * TILE_SIZE, TILE_SIZE), TILE_SIZE)],
                left.at[pl.ds(row, rows), pl.ds(column, TILE_SIZE)],
                row_sem.at[tile],
            ).start()

    for copy in piece_copies():
        copy.start()

    @pl.loop(0, inner_tiles)
    def _(tile):
        start_rows(tile)

    out_ref[...] = jnp.zeros_like(out_ref)
    pltpu.make_async_copy(
        right.at[:, pl.ds(0, 2 * TILE_SIZE), :], right.at[:, pl.ds(0, 2 * TILE_SIZE), :], piece_sem
    ).wait()

    @pl.loop(0, inner_tiles)
    def _(tile):
        columns = pl.ds(pl.multiple_of(tile * 2 * TILE_SIZE, 2 * TILE_SIZE), 2 * TILE_SIZE)
        pltpu.make_async_copy(left.at[:, columns], left.at[:, columns], row_sem.at[tile]).wait()
        right[tile, 2 * TILE_SIZE :, :] = -right[tile, :TILE_SIZE, :]

        @pl.loop(0, out_tiles)
        def _(out_tile):
            @pl.when(used_ref[out_tile, tile] == 1)
            def _():
                span = pl.ds(pl.multiple_of(out_tile * TILE_SIZE, TILE_SIZE), TILE_SIZE)
                lhs = left[span, columns]
                for part in range(2):
                    rhs = right[tile, pl.ds((1 - part) * TILE_SIZE, 2 * TILE_SIZE), :]
                    out_ref[part, span, :] += jnp.dot(lhs, rhs, preferred_element_type=jnp.float32)


def product(row_buffers, row_starts, pieces, piece_starts, used, span, total):
    rows = row_buffers[0][0].shape[0]
    parts = [part for _, part in row_buffers]
    arrays = [array for array, _ in row_buffers] + list(pieces)
    plan = jnp.stack(row_starts + piece_starts).astype(jnp.int32)

    def kernel(plan_ref, used_ref, *refs):
        ins = refs[: len(arrays)]
        row_refs = list(zip(ins[: len(parts)], parts))
        product_kernel(
            rows, None, plan_ref, used_ref, (row_refs, ins[len(parts) :]), *refs[len(arrays) :]
        )

    inner_tiles = total // TILE_SIZE
    return pl.pallas_call(
        kernel,
        out_shape=jax.ShapeDtypeStruct((2, span, TILE_SIZE), jnp.float32),
        grid_spec=pltpu.PrefetchScalarGridSpec(
            num_scalar_prefetch=2,
            grid=(1,),
            in_specs=[pl.BlockSpec(memory_space=pl.ANY)] * len(arrays),
            out_specs=pl.BlockSpec((2, span, TILE_SIZE), lambda i, *_: (0, 0, 0), pipeline_mode=pl.Buffered(1)),
            scratch_shapes=[
                pltpu.VMEM((span, 2 * total), jnp.bfloat16),
                pltpu.VMEM((inner_tiles, 3 * TILE_SIZE, TILE_SIZE), jnp.bfloat16),
                pltpu.SemaphoreType.DMA((inner_tiles,)),
                pltpu.SemaphoreType.DMA,
            ],
        ),
        compiler_params=pltpu.CompilerParams(vmem_limit_bytes=67_000_000),
    )(plan, used, *arrays)


def local(data, fill_mask, obliquity, aperture, lengths):
    _, rows, total = data.shape
    src_count = lax.axis_size("src")
    rcv_count = lax.axis_size("rcv")
    src_index = lax.axis_index("src")
    rcv_index = lax.axis_index("rcv")
    devices = src_count * rcv_count
    span = rows * rcv_count

    arrived = lax.all_to_all(
        transposed_blocks(data, devices), ("src", "rcv"), split_axis=0, concat_axis=0, tiled=True
    )
    own = fill(data, fill_mask, arrived)

    order = ring_order(rcv_count)
    forward = [(order[i], order[(i + 1) % rcv_count]) for i in range(rcv_count)]
    backward = [(b, a) for a, b in forward]
    position = jnp.asarray([order.index(i) for i in range(rcv_count)], jnp.int32)[rcv_index]
    table = jnp.asarray(order, jnp.int32)

    def origin(offset):
        return table[(position + offset) % rcv_count]

    def cut(planes, first):
        gains = -lax.dynamic_slice_in_dim(obliquity, src_index * span + first * rows, rows)
        tiles = [lax.dynamic_slice_in_dim(p, rcv_index * TILE_SIZE, TILE_SIZE, axis=1) for p in planes]
        return (jnp.stack(tiles).astype(jnp.float32) * gains[None, :, None]).astype(jnp.bfloat16)

    row_buffers, row_starts, pieces, piece_starts = [], [], [], []

    def collect(blocks):
        for planes, first in blocks:
            for part in range(2):
                row_buffers.append((planes[part], part))
                row_starts.append(first * rows)
        held = jnp.stack([cut(planes, first) for planes, first in blocks])
        starts = [src_index * span + first * rows for _, first in blocks]
        masks = [0]
        bit = src_count // 2
        while bit:
            swap = [(i, i ^ bit) for i in range(src_count)]
            other = lax.ppermute(held, "src", swap)
            held = jnp.concatenate([held, other])
            masks = masks + [mask ^ bit for mask in masks]
            bit //= 2
        pieces.append(held)
        for mask in masks:
            for _, first in blocks:
                piece_starts.append((src_index ^ mask) * span + first * rows)

    collect([(own, origin(0))])
    ahead, behind = own, own
    for step in range(1, (rcv_count - 1) // 2 + 1):
        ahead = tuple(lax.ppermute(p, "rcv", forward) for p in ahead)
        behind = tuple(lax.ppermute(p, "rcv", backward) for p in behind)
        collect([(ahead, origin(-step)), (behind, origin(step))])
    if rcv_count % 2 == 0:
        last = (lax.ppermute(ahead[0], "rcv", forward), lax.ppermute(behind[1], "rcv", backward))
        collect([(last, origin(rcv_count // 2))])

    lists = lax.dynamic_index_in_dim(aperture, rcv_index, 1, keepdims=False)
    slot = jnp.arange(lists.shape[1], dtype=jnp.int32)
    wanted = (slot[None, :] < lengths)[:, :, None]
    tiles = jnp.arange(total // TILE_SIZE, dtype=jnp.int32)
    used = jnp.any(wanted & (lists[:, :, None] == tiles), axis=1).astype(jnp.int32)
    return product(row_buffers, row_starts, pieces, piece_starts, used, span, total)


def solution(mesh):
    placed = (
        P(None, ("src", "rcv"), None),
        P(("src", "rcv"), None),
        P(),
        P("src", None, None),
        P("src", "rcv"),
    )
    return jax.shard_map(
        local, mesh=mesh, in_specs=placed, out_specs=P(None, "src", "rcv"), check_vma=False
    )
```

```python
import functools

import jax
import jax.numpy as jnp
from jax import lax
from jax.experimental import pallas as pl
from jax.experimental.pallas import tpu as pltpu
from jax.sharding import PartitionSpec as P

TILE_SIZE = 512


def ring_order(count):
    return list(range(0, count, 2)) + list(range(1, count, 2))[::-1]


def split_kernel(data_ref, *out_refs):
    rows = data_ref.shape[1]
    for part, out_ref in enumerate(out_refs):
        for block in range(out_ref.shape[0]):
            out_ref[block] = data_ref[part, :, block * rows : (block + 1) * rows].T


def transposed_blocks(data, devices):
    _, rows, total = data.shape
    if rows % 128:
        return tuple(jnp.transpose(p.reshape(rows, devices, rows), (1, 0, 2)) for p in data)
    group = 8
    return pl.pallas_call(
        split_kernel,
        out_shape=(jax.ShapeDtypeStruct((devices, rows, rows), data.dtype),) * 2,
        grid=(devices // group,),
        in_specs=[pl.BlockSpec((2, rows, group * rows), lambda i: (0, 0, i))],
        out_specs=(pl.BlockSpec((group, rows, rows), lambda i: (i, 0, 0)),) * 2,
    )(data)


def fill_kernel(data_ref, mask_ref, arrived_ref, out_ref):
    rows = data_ref.shape[0]
    for block in range(arrived_ref.shape[0]):
        span = slice(block * rows, (block + 1) * rows)
        out_ref[:, span] = jnp.where(
            mask_ref[:, span] == 1, data_ref[:, span], arrived_ref[block]
        )


def fill(data, mask, arrived, part):
    _, rows, total = data.shape
    devices = arrived.shape[0]
    if rows % 128:
        transposed = jnp.transpose(arrived, (2, 0, 1)).reshape(rows, total)
        return jnp.where(mask == 1, data[part], transposed)
    group = 8
    return pl.pallas_call(
        fill_kernel,
        out_shape=jax.ShapeDtypeStruct((rows, total), data.dtype),
        grid=(devices // group,),
        in_specs=[
            pl.BlockSpec((None, rows, group * rows), lambda i: (part, 0, i)),
            pl.BlockSpec((rows, group * rows), lambda i: (0, i)),
            pl.BlockSpec((group, rows, rows), lambda i: (i, 0, 0)),
        ],
        out_specs=pl.BlockSpec((rows, group * rows), lambda i: (0, i)),
    )(data, mask, arrived)


def product_kernel(rows, src_count, plan_ref, used_ref, *refs):
    (row_refs, piece_refs), out_ref, scratch = refs[0], refs[1], refs[2:]
    left, right, row_sem, piece_sem = scratch
    inner_tiles = right.shape[0]
    out_tiles = out_ref.shape[1] // TILE_SIZE

    def piece_copies():
        copies = []
        at = len(row_refs)
        for ref in piece_refs:
            for index in range(ref.shape[0]):
                first = plan_ref[at]
                tile, offset = first // TILE_SIZE, first % TILE_SIZE
                for part in range(2):
                    row = pl.multiple_of(offset + (1 - part) * TILE_SIZE, rows)
                    copies.append(
                        pltpu.make_async_copy(
                            ref.at[index, part],
                            right.at[tile, pl.ds(row, rows), :],
                            piece_sem,
                        )
                    )
                at += 1
        return copies

    def start_rows(tile):
        for index, (ref, part) in enumerate(row_refs):
            row = pl.multiple_of(plan_ref[index], rows)
            column = pl.multiple_of(tile * 2 * TILE_SIZE + part * TILE_SIZE, TILE_SIZE)
            pltpu.make_async_copy(
                ref.at[:, pl.ds(pl.multiple_of(tile * TILE_SIZE, TILE_SIZE), TILE_SIZE)],
                left.at[pl.ds(row, rows), pl.ds(column, TILE_SIZE)],
                row_sem.at[tile],
            ).start()

    for copy in piece_copies():
        copy.start()

    @pl.loop(0, inner_tiles)
    def _(tile):
        start_rows(tile)

    out_ref[...] = jnp.zeros_like(out_ref)
    pltpu.make_async_copy(
        right.at[:, pl.ds(0, 2 * TILE_SIZE), :], right.at[:, pl.ds(0, 2 * TILE_SIZE), :], piece_sem
    ).wait()

    @pl.loop(0, inner_tiles)
    def _(tile):
        columns = pl.ds(pl.multiple_of(tile * 2 * TILE_SIZE, 2 * TILE_SIZE), 2 * TILE_SIZE)
        pltpu.make_async_copy(left.at[:, columns], left.at[:, columns], row_sem.at[tile]).wait()
        right[tile, 2 * TILE_SIZE :, :] = -right[tile, :TILE_SIZE, :]

        @pl.loop(0, out_tiles)
        def _(out_tile):
            @pl.when(used_ref[out_tile, tile] == 1)
            def _():
                span = pl.ds(pl.multiple_of(out_tile * TILE_SIZE, TILE_SIZE), TILE_SIZE)
                lhs = left[span, columns]
                for part in range(2):
                    rhs = right[tile, pl.ds((1 - part) * TILE_SIZE, 2 * TILE_SIZE), :]
                    out_ref[part, span, :] += jnp.dot(lhs, rhs, preferred_element_type=jnp.float32)


def product(row_buffers, row_starts, pieces, piece_starts, used, span, total):
    rows = row_buffers[0][0].shape[0]
    parts = [part for _, part in row_buffers]
    arrays = [array for array, _ in row_buffers] + list(pieces)
    plan = jnp.stack(row_starts + piece_starts).astype(jnp.int32)

    def kernel(plan_ref, used_ref, *refs):
        ins = refs[: len(arrays)]
        row_refs = list(zip(ins[: len(parts)], parts))
        product_kernel(
            rows, None, plan_ref, used_ref, (row_refs, ins[len(parts) :]), *refs[len(arrays) :]
        )

    inner_tiles = total // TILE_SIZE
    return pl.pallas_call(
        kernel,
        out_shape=jax.ShapeDtypeStruct((2, span, TILE_SIZE), jnp.float32),
        grid_spec=pltpu.PrefetchScalarGridSpec(
            num_scalar_prefetch=2,
            grid=(1,),
            in_specs=[pl.BlockSpec(memory_space=pl.ANY)] * len(arrays),
            out_specs=pl.BlockSpec((2, span, TILE_SIZE), lambda i, *_: (0, 0, 0), pipeline_mode=pl.Buffered(1)),
            scratch_shapes=[
                pltpu.VMEM((span, 2 * total), jnp.bfloat16),
                pltpu.VMEM((inner_tiles, 3 * TILE_SIZE, TILE_SIZE), jnp.bfloat16),
                pltpu.SemaphoreType.DMA((inner_tiles,)),
                pltpu.SemaphoreType.DMA,
            ],
        ),
        compiler_params=pltpu.CompilerParams(vmem_limit_bytes=67_000_000),
    )(plan, used, *arrays)


def cut_kernel(place_ref, *refs):
    planes, out_ref = refs[:-1], refs[-1]
    for block in range(out_ref.shape[0]):
        first, second, gain = planes[3 * block : 3 * block + 3]
        for part, ref in enumerate((first, second)):
            out_ref[block, part] = (ref[...].astype(jnp.float32) * gain[...]).astype(jnp.bfloat16)


def cut(blocks, column, gains):
    rows = blocks[0][0][0].shape[0]
    place = jnp.stack([column] + [first for _, first in blocks]).astype(jnp.int32)
    specs, operands = [], []
    for index, (planes, _) in enumerate(blocks):
        specs += [pl.BlockSpec((rows, TILE_SIZE), lambda i, place: (0, place[0]))] * 2
        specs.append(pl.BlockSpec((None, rows, 1), lambda i, place, at=index + 1: (place[at], 0, 0)))
        operands += [planes[0], planes[1], gains]
    shape = (len(blocks), 2, rows, TILE_SIZE)
    return pl.pallas_call(
        cut_kernel,
        out_shape=jax.ShapeDtypeStruct(shape, jnp.bfloat16),
        grid_spec=pltpu.PrefetchScalarGridSpec(
            num_scalar_prefetch=1,
            grid=(1,),
            in_specs=specs,
            out_specs=pl.BlockSpec(shape, lambda i, place: (0, 0, 0, 0)),
        ),
    )(place, *operands)


def job(base, row_blocks, columns, absent, used, span, total, full, accumulate, choice=()):
    rows = row_blocks[0][0][0].shape[0]
    count, height = len(row_blocks), len(row_blocks) * rows
    chunks = 1 + max(column[3] for column in columns)
    depth = total if full else len(columns) * rows
    span_depth = depth // chunks
    plan = jnp.stack(
        [first for _, first in row_blocks]
        + [column[2] for column in columns]
        + list(absent)
        + list(choice)
    ).astype(jnp.int32)
    planes = [plane for block, _ in row_blocks for plane in block]
    sources, source_at = [], []
    for pieces, *_ in columns:
        if not any(pieces is source for source in sources):
            sources.append(pieces)
        source_at.append([source is pieces for source in sources].index(True))
    given = [] if base is None else [base]

    def kernel(plan_ref, used_ref, *refs):
        plane_refs = refs[: len(planes)]
        source_refs = refs[len(planes) : len(planes) + len(sources)]
        out_ref, left, right, held, left_sem, right_sem, held_sem = refs[-7:]

        def first_of(at):
            return pl.multiple_of(plan_ref[at], rows)

        def held_copy(block, part, out):
            here = held.at[part, pl.ds(block * rows, rows), :]
            there = out_ref.at[part, pl.ds(first_of(block), rows), :]
            pair = (here, there) if out else (there, here)
            return pltpu.make_async_copy(*pair, held_sem)

        if accumulate:
            for block in range(count):
                for part in range(2):
                    held_copy(block, part, False).start()
        else:
            held[...] = jnp.zeros_like(held)
        for at in range(len(absent)):
            row = first_of(count + len(columns) + at)
            right[:, pl.ds(row, rows), :] = jnp.zeros((3, rows, TILE_SIZE), jnp.bfloat16)
        for at, (_, index, _, chunk) in enumerate(columns):
            row = first_of(count + at) if full else at * rows
            for part in range(2):
                pltpu.make_async_copy(
                    source_refs[source_at[at]].at[index, part],
                    right.at[part, pl.ds(row, rows), :],
                    right_sem.at[chunk],
                ).start()
        for block in range(count):
            for part in range(2):
                ref, here = plane_refs[2 * block + part], pl.ds(block * rows, rows)
                if full and choice:
                    for at in range(len(planes) // 2):

                        @pl.when(plan_ref[plan.shape[0] - 1] == at)
                        def _():
                            pltpu.make_async_copy(
                                plane_refs[2 * at + part], left.at[part, here, :], left_sem
                            ).start()

                    continue
                if full:
                    pltpu.make_async_copy(ref, left.at[part, here, :], left_sem).start()
                    continue
                for at in range(len(columns)):
                    pltpu.make_async_copy(
                        ref.at[:, pl.ds(first_of(count + at), rows)],
                        left.at[part, here, pl.ds(at * rows, rows)],
                        left_sem,
                    ).start()
        pltpu.make_async_copy(left, left, left_sem).wait()
        if accumulate:
            pltpu.make_async_copy(held, held, held_sem).wait()

        for chunk in range(chunks):
            members = [at for at, column in enumerate(columns) if column[3] == chunk]
            bytes_view = right.at[pl.ds(0, 2), pl.ds(0, len(members) * rows), :]
            pltpu.make_async_copy(bytes_view, bytes_view, right_sem.at[chunk]).wait()
            if full:
                base_row = plan_ref[count + members[0]] // span_depth * span_depth
                inner = pl.ds(pl.multiple_of(base_row, span_depth), span_depth)
                pieces = [(base_row + t * TILE_SIZE, TILE_SIZE) for t in range(span_depth // TILE_SIZE)]
                spots = [pl.ds(pl.multiple_of(p, TILE_SIZE), n) for p, n in pieces]
            else:
                inner = slice(None)
                pieces = [(plan_ref[count + at], rows) for at in members]
                spots = [pl.ds(at * rows, rows) for at in members]
            for block in range(count):
                own_tile = plan_ref[block] // TILE_SIZE
                for (first, size), spot in zip(pieces, spots):

                    @pl.when(used_ref[own_tile, first // TILE_SIZE] == 0)
                    def _():
                        left[:, block * rows : (block + 1) * rows, spot] = jnp.zeros(
                            (2, rows, size), jnp.bfloat16
                        )

            right[2, inner, :] = -right[1, inner, :]
            lead, trail = left[0, :, inner], left[1, :, inner]
            for part, (upper, lower) in enumerate(((0, 2), (1, 0))):
                held[part] += jnp.dot(
                    lead, right[upper, inner, :], preferred_element_type=jnp.float32
                ) + jnp.dot(trail, right[lower, inner, :], preferred_element_type=jnp.float32)

        for block in range(count):
            for part in range(2):
                held_copy(block, part, True).start()
        pltpu.make_async_copy(held, held, held_sem).wait()

    operands = planes + sources + given
    moved = 4 * height * depth + 4 * depth * TILE_SIZE + 8 * height * TILE_SIZE
    return pl.pallas_call(
        kernel,
        out_shape=jax.ShapeDtypeStruct((2, span, TILE_SIZE), jnp.float32),
        grid_spec=pltpu.PrefetchScalarGridSpec(
            num_scalar_prefetch=2,
            grid=(1,),
            in_specs=[pl.BlockSpec(memory_space=pl.ANY)] * len(operands),
            out_specs=pl.BlockSpec(memory_space=pl.ANY),
            scratch_shapes=[
                pltpu.VMEM((2, height, depth), jnp.bfloat16),
                pltpu.VMEM((3, depth, TILE_SIZE), jnp.bfloat16),
                pltpu.VMEM((2, height, TILE_SIZE), jnp.float32),
                pltpu.SemaphoreType.DMA,
                pltpu.SemaphoreType.DMA((chunks,)),
                pltpu.SemaphoreType.DMA,
            ],
        ),
        input_output_aliases={} if base is None else {2 + len(operands) - 1: 0},
        cost_estimate=pl.CostEstimate(
            flops=8 * height * depth * TILE_SIZE, bytes_accessed=moved, transcendentals=0
        ),
        compiler_params=pltpu.CompilerParams(vmem_limit_bytes=60 * 1024 * 1024),
    )(plan, used, *operands)


def used_tiles(aperture, lengths, rcv_index, total):
    lists = lax.dynamic_index_in_dim(aperture, rcv_index, 1, keepdims=False)
    slot = jnp.arange(lists.shape[1], dtype=jnp.int32)
    wanted = (slot[None, :] < lengths)[:, :, None]
    tiles = jnp.arange(total // TILE_SIZE, dtype=jnp.int32)
    return jnp.any(wanted & (lists[:, :, None] == tiles), axis=1).astype(jnp.int32)


def local(data, fill_mask, obliquity, aperture, lengths):
    _, rows, total = data.shape
    src_count = lax.axis_size("src")
    rcv_count = lax.axis_size("rcv")
    src_index = lax.axis_index("src")
    rcv_index = lax.axis_index("rcv")
    devices = src_count * rcv_count
    span = rows * rcv_count
    phased = rows % 128 == 0 and rcv_count % 4 == 0 and rcv_count > 4

    blocks = transposed_blocks(data, devices)
    arrived = [
        lax.all_to_all(b, ("src", "rcv"), split_axis=0, concat_axis=0, tiled=True) for b in blocks
    ]
    own = tuple(fill(data, fill_mask, a, part) for part, a in enumerate(arrived))
    used = used_tiles(aperture, lengths, rcv_index, total)

    order = ring_order(rcv_count)
    forward = [(order[i], order[(i + 1) % rcv_count]) for i in range(rcv_count)]
    backward = [(b, a) for a, b in forward]
    place = jnp.asarray([order.index(i) for i in range(rcv_count)], jnp.int32)[rcv_index]
    table = jnp.asarray(order + order, jnp.int32)
    half = rcv_count // 2

    def origin(offset):
        return lax.dynamic_index_in_dim(table, place + offset % rcv_count, keepdims=False)

    my_gains = -lax.dynamic_slice_in_dim(obliquity, src_index * span, span)
    gains = my_gains.reshape(rcv_count, rows, 1)

    def tiles_of(blocks, column):
        if rows % 128 == 0:
            return cut(blocks, column, gains)
        out = []
        for planes, first in blocks:
            cuts = [lax.dynamic_slice_in_dim(p, column * TILE_SIZE, TILE_SIZE, 1) for p in planes]
            gain = lax.dynamic_index_in_dim(gains, first, 0, keepdims=True)
            out.append((jnp.stack(cuts).astype(jnp.float32) * gain).astype(jnp.bfloat16))
        return jnp.stack(out)

    columns = []

    def spread(held, origins):
        held_by = [(held, 0)]
        bit = src_count // 2
        while bit:
            swap = [(i, i ^ bit) for i in range(src_count)]
            held_by += [(lax.ppermute(x, "src", swap), mask ^ bit) for x, mask in held_by]
            bit //= 2
        for pieces, mask in held_by:
            for index, first in enumerate(origins):
                columns.append((pieces, index, (src_index ^ mask) * span + first * rows, mask))

    def collect(blocks):
        spread(tiles_of(blocks, rcv_index), [first for _, first in blocks])

    steps = (rcv_count - 1) // 2
    rows_of = {0: (own, origin(0))}
    far = origin(half)
    if phased:
        across = [(order[i], order[(i + half) % rcv_count]) for i in range(rcv_count)]
        spread(lax.ppermute(tiles_of([(own, origin(0))], far), "rcv", across), [far])
    collect([rows_of[0]])
    ahead, behind = own, own
    trail = {}
    for step in range(1, steps + 1):
        ahead = tuple(lax.ppermute(p, "rcv", forward) for p in ahead)
        behind = tuple(lax.ppermute(p, "rcv", backward) for p in behind)
        rows_of[-step], rows_of[step] = (ahead, origin(-step)), (behind, origin(step))
        trail[step] = len(columns)
        collect([rows_of[-step], rows_of[step]])
    if not phased:
        if rcv_count % 2 == 0:
            last = (lax.ppermute(ahead[0], "rcv", forward), lax.ppermute(behind[1], "rcv", backward))
            rows_of[half] = (last, far)
            collect([rows_of[half]])
        row_buffers, row_starts, pieces, starts = [], [], [], []
        for planes, first in rows_of.values():
            row_buffers += [(planes[0], 0), (planes[1], 1)]
            row_starts += [first * rows] * 2
        for array, index, first, _ in columns:
            if index == 0:
                pieces.append(array)
            starts.append(first)
        return product(row_buffers, row_starts, pieces, starts, used, span, total)

    quarter = rcv_count // 4
    near = [quarter - 1, quarter, rcv_count - 1 - quarter, rcv_count - quarter]
    last = [
        lax.ppermute(p, "rcv", [(order[(i + d) % rcv_count], order[i]) for i in range(rcv_count) if i not in near])
        for p, d in ((ahead[0], -1), (behind[1], 1))
    ]
    taken = []
    for offset in (-1, 1):
        pairs = []
        for i in near:
            mate = rcv_count - 1 - i
            if (mate + offset) % rcv_count == (i + half) % rcv_count:
                pairs.append((order[mate], order[i]))
        taken.append([lax.ppermute(p, "rcv", pairs) for p in rows_of[offset][0]])
    is_near = jnp.any(place == jnp.asarray(near, jnp.int32))
    side = jnp.any(jnp.asarray([(rcv_count - 2 - i - i - half) % rcv_count == 0 for i in range(rcv_count)])[None, place])
    chosen = jnp.where(is_near, jnp.where(side, 1, 2), 0)

    def as_rows(offsets):
        return [(rows_of[o][0], rows_of[o][1] * rows) for o in offsets]

    inside = [0] + [o for step in range(1, steps) for o in (-step, step)]
    outside = [-steps, steps]
    early, late = columns[: trail[steps]], columns[trail[steps] :]
    out = job(
        None, as_rows(inside), early, [c[2] for c in late], used, span, total, True, False
    )
    packed = [(array, index, first, 0) for array, index, first, _ in late]
    out = job(out, as_rows(inside), packed, [], used, span, total, False, True)
    out = job(out, as_rows(outside), columns, [], used, span, total, True, False)
    candidates = (*last, *taken[0], *taken[1])
    return job(
        out, [(candidates, far * rows)], columns, [], used, span, total, True, False, [chosen]
    )


def solution(mesh):
    placed = (
        P(None, ("src", "rcv"), None),
        P(("src", "rcv"), None),
        P(),
        P("src", None, None),
        P("src", "rcv"),
    )
    return jax.shard_map(
        local, mesh=mesh, in_specs=placed, out_specs=P(None, "src", "rcv"), check_vma=False
    )
```

```python
import jax
import jax.numpy as jnp
import numpy as np
from jax import lax
from jax.experimental import pallas as pl
from jax.experimental.pallas import tpu as pltpu
from jax.sharding import PartitionSpec as P


TILE_SIZE = 512


def ring_order(count):
    return list(range(0, count, 2)) + list(range(1, count, 2))[::-1]


def split_kernel(data_ref, *out_refs):
    rows = data_ref.shape[1]
    for part, out_ref in enumerate(out_refs):
        for block in range(out_ref.shape[0]):
            out_ref[block] = data_ref[part, :, block * rows : (block + 1) * rows].T


def transposed_blocks(data, devices):
    _, rows, _ = data.shape
    if rows % 128:
        return tuple(jnp.transpose(p.reshape(rows, devices, rows), (1, 0, 2)) for p in data)
    group = 8
    return pl.pallas_call(
        split_kernel,
        out_shape=(jax.ShapeDtypeStruct((devices, rows, rows), data.dtype),) * 2,
        grid=(devices // group,),
        in_specs=[pl.BlockSpec((2, rows, group * rows), lambda i: (0, 0, i))],
        out_specs=(pl.BlockSpec((group, rows, rows), lambda i: (i, 0, 0)),) * 2,
    )(data)


def fill_kernel(data_ref, mask_ref, arrived_ref, out_ref):
    rows = data_ref.shape[0]
    for block in range(arrived_ref.shape[0]):
        span = slice(block * rows, (block + 1) * rows)
        out_ref[:, span] = jnp.where(
            mask_ref[:, span] == 1, data_ref[:, span], arrived_ref[block]
        )


def fill(data, mask, arrived, part):
    _, rows, total = data.shape
    devices = arrived.shape[0]
    if rows % 128:
        transposed = jnp.transpose(arrived, (2, 0, 1)).reshape(rows, total)
        return jnp.where(mask == 1, data[part], transposed)
    group = 8
    return pl.pallas_call(
        fill_kernel,
        out_shape=jax.ShapeDtypeStruct((rows, total), data.dtype),
        grid=(devices // group,),
        in_specs=[
            pl.BlockSpec((None, rows, group * rows), lambda i: (part, 0, i)),
            pl.BlockSpec((rows, group * rows), lambda i: (0, i)),
            pl.BlockSpec((group, rows, rows), lambda i: (i, 0, 0)),
        ],
        out_specs=pl.BlockSpec((rows, group * rows), lambda i: (0, i)),
    )(data, mask, arrived)


def product_kernel(rows, plan_ref, used_ref, *refs):
    (row_refs, piece_refs), out_ref, scratch = refs[0], refs[1], refs[2:]
    left, right, row_sem, piece_sem = scratch
    inner_tiles = right.shape[0]
    out_tiles = out_ref.shape[1] // TILE_SIZE

    def piece_copies():
        copies = []
        at = len(row_refs)
        for ref in piece_refs:
            for index in range(ref.shape[0]):
                first = plan_ref[at]
                tile, offset = first // TILE_SIZE, first % TILE_SIZE
                for part in range(2):
                    row = pl.multiple_of(offset + (1 - part) * TILE_SIZE, rows)
                    copies.append(
                        pltpu.make_async_copy(
                            ref.at[index, part],
                            right.at[tile, pl.ds(row, rows), :],
                            piece_sem,
                        )
                    )
                at += 1
        return copies

    def start_rows(tile):
        for index, (ref, part) in enumerate(row_refs):
            row = pl.multiple_of(plan_ref[index], rows)
            column = pl.multiple_of(tile * 2 * TILE_SIZE + part * TILE_SIZE, TILE_SIZE)
            pltpu.make_async_copy(
                ref.at[:, pl.ds(pl.multiple_of(tile * TILE_SIZE, TILE_SIZE), TILE_SIZE)],
                left.at[pl.ds(row, rows), pl.ds(column, TILE_SIZE)],
                row_sem.at[tile],
            ).start()

    for copy in piece_copies():
        copy.start()

    @pl.loop(0, inner_tiles)
    def _(tile):
        start_rows(tile)

    out_ref[...] = jnp.zeros_like(out_ref)
    pltpu.make_async_copy(
        right.at[:, pl.ds(0, 2 * TILE_SIZE), :], right.at[:, pl.ds(0, 2 * TILE_SIZE), :], piece_sem
    ).wait()

    @pl.loop(0, inner_tiles)
    def _(tile):
        columns = pl.ds(pl.multiple_of(tile * 2 * TILE_SIZE, 2 * TILE_SIZE), 2 * TILE_SIZE)
        pltpu.make_async_copy(left.at[:, columns], left.at[:, columns], row_sem.at[tile]).wait()
        right[tile, 2 * TILE_SIZE :, :] = -right[tile, :TILE_SIZE, :]

        @pl.loop(0, out_tiles)
        def _(out_tile):
            @pl.when(used_ref[out_tile, tile] == 1)
            def _():
                span = pl.ds(pl.multiple_of(out_tile * TILE_SIZE, TILE_SIZE), TILE_SIZE)
                lhs = left[span, columns]
                for part in range(2):
                    rhs = right[tile, pl.ds((1 - part) * TILE_SIZE, 2 * TILE_SIZE), :]
                    out_ref[part, span, :] += jnp.dot(lhs, rhs, preferred_element_type=jnp.float32)


def product(row_buffers, row_starts, pieces, piece_starts, used, span, total):
    rows = row_buffers[0][0].shape[0]
    parts = [part for _, part in row_buffers]
    arrays = [array for array, _ in row_buffers] + list(pieces)
    plan = jnp.stack(row_starts + piece_starts).astype(jnp.int32)

    def kernel(plan_ref, used_ref, *refs):
        ins = refs[: len(arrays)]
        row_refs = list(zip(ins[: len(parts)], parts))
        product_kernel(
            rows, plan_ref, used_ref, (row_refs, ins[len(parts) :]), *refs[len(arrays) :]
        )

    inner_tiles = total // TILE_SIZE
    return pl.pallas_call(
        kernel,
        out_shape=jax.ShapeDtypeStruct((2, span, TILE_SIZE), jnp.float32),
        grid_spec=pltpu.PrefetchScalarGridSpec(
            num_scalar_prefetch=2,
            grid=(1,),
            in_specs=[pl.BlockSpec(memory_space=pl.ANY)] * len(arrays),
            out_specs=pl.BlockSpec((2, span, TILE_SIZE), lambda i, *_: (0, 0, 0), pipeline_mode=pl.Buffered(1)),
            scratch_shapes=[
                pltpu.VMEM((span, 2 * total), jnp.bfloat16),
                pltpu.VMEM((inner_tiles, 3 * TILE_SIZE, TILE_SIZE), jnp.bfloat16),
                pltpu.SemaphoreType.DMA((inner_tiles,)),
                pltpu.SemaphoreType.DMA,
            ],
        ),
        compiler_params=pltpu.CompilerParams(vmem_limit_bytes=67_000_000),
    )(plan, used, *arrays)


def cut_kernel(device_ref, place_ref, *refs):
    planes, out_ref = refs[:-1], refs[-1]
    for block in range(out_ref.shape[0]):
        first, second, gain = planes[3 * block : 3 * block + 3]
        for part, ref in enumerate((first, second)):
            out_ref[block, part] = (ref[...].astype(jnp.float32) * gain[...]).astype(jnp.bfloat16)


def cut(blocks, column, gains, device):
    rows = blocks[0][0][0].shape[0]
    place = np.stack([column] + [first for _, first in blocks], axis=1).astype(np.int32)
    specs, operands = [], []
    for index, (planes, _) in enumerate(blocks):
        specs += [pl.BlockSpec((rows, TILE_SIZE), lambda i, me, place: (0, place[me[0], 0]))] * 2
        specs.append(
            pl.BlockSpec((None, rows, 1), lambda i, me, place, at=index + 1: (place[me[0], at], 0, 0))
        )
        operands += [planes[0], planes[1], gains]
    shape = (len(blocks), 2, rows, TILE_SIZE)
    return pl.pallas_call(
        cut_kernel,
        out_shape=jax.ShapeDtypeStruct(shape, jnp.bfloat16),
        grid_spec=pltpu.PrefetchScalarGridSpec(
            num_scalar_prefetch=2,
            grid=(1,),
            in_specs=specs,
            out_specs=pl.BlockSpec(shape, lambda i, me, place: (0, 0, 0, 0)),
        ),
    )(device, jnp.asarray(place), *operands)


def job(device, base, row_blocks, columns, absent, used, span, total, full, accumulate, choice=()):
    rows = row_blocks[0][0][0].shape[0]
    count, height = len(row_blocks), len(row_blocks) * rows
    chunks = 1 + max(column[3] for column in columns)
    depth = total if full else len(columns) * rows
    span_depth = depth // chunks
    plan = np.stack(
        [first for _, first in row_blocks]
        + [column[2] for column in columns]
        + list(absent)
        + list(choice),
        axis=1,
    ).astype(np.int32)
    planes = [plane for block, _ in row_blocks for plane in block]
    sources, source_at = [], []
    for pieces, *_ in columns:
        if not any(pieces is source for source in sources):
            sources.append(pieces)
        source_at.append([source is pieces for source in sources].index(True))
    given = [] if base is None else [base]

    def kernel(device_ref, plan_ref, used_ref, *refs):
        plane_refs = refs[: len(planes)]
        source_refs = refs[len(planes) : len(planes) + len(sources)]
        out_ref, left, right, held, left_sem, right_sem, held_sem = refs[-7:]
        me = device_ref[0]

        def first_of(at):
            return pl.multiple_of(plan_ref[me, at], rows)

        def held_copy(block, part, out):
            here = held.at[part, pl.ds(block * rows, rows), :]
            there = out_ref.at[part, pl.ds(first_of(block), rows), :]
            pair = (here, there) if out else (there, here)
            return pltpu.make_async_copy(*pair, held_sem)

        if accumulate:
            for block in range(count):
                for part in range(2):
                    held_copy(block, part, False).start()
        else:
            held[...] = jnp.zeros_like(held)
        for at in range(len(absent)):
            row = first_of(count + len(columns) + at)
            right[:, pl.ds(row, rows), :] = jnp.zeros((3, rows, TILE_SIZE), jnp.bfloat16)
        for at, (_, index, _, chunk) in enumerate(columns):
            row = first_of(count + at) if full else at * rows
            for part in range(2):
                pltpu.make_async_copy(
                    source_refs[source_at[at]].at[index, part],
                    right.at[part, pl.ds(row, rows), :],
                    right_sem.at[chunk],
                ).start()
        for block in range(count):
            for part in range(2):
                ref, here = plane_refs[2 * block + part], pl.ds(block * rows, rows)
                if full and choice:
                    for at in range(len(planes) // 2):

                        @pl.when(plan_ref[me, plan.shape[1] - 1] == at)
                        def _():
                            pltpu.make_async_copy(
                                plane_refs[2 * at + part], left.at[part, here, :], left_sem
                            ).start()

                    continue
                if full:
                    pltpu.make_async_copy(ref, left.at[part, here, :], left_sem).start()
                    continue
                for at in range(len(columns)):
                    pltpu.make_async_copy(
                        ref.at[:, pl.ds(first_of(count + at), rows)],
                        left.at[part, here, pl.ds(at * rows, rows)],
                        left_sem,
                    ).start()
        pltpu.make_async_copy(left, left, left_sem).wait()
        if accumulate:
            pltpu.make_async_copy(held, held, held_sem).wait()

        for chunk in range(chunks):
            members = [at for at, column in enumerate(columns) if column[3] == chunk]
            bytes_view = right.at[pl.ds(0, 2), pl.ds(0, len(members) * rows), :]
            pltpu.make_async_copy(bytes_view, bytes_view, right_sem.at[chunk]).wait()
            if full:
                base_row = plan_ref[me, count + members[0]] // span_depth * span_depth
                inner = pl.ds(pl.multiple_of(base_row, span_depth), span_depth)
                pieces = [(base_row + t * TILE_SIZE, TILE_SIZE) for t in range(span_depth // TILE_SIZE)]
                spots = [pl.ds(pl.multiple_of(p, TILE_SIZE), n) for p, n in pieces]
            else:
                inner = slice(None)
                pieces = [(plan_ref[me, count + at], rows) for at in members]
                spots = [pl.ds(at * rows, rows) for at in members]
            for block in range(count):
                own_tile = plan_ref[me, block] // TILE_SIZE
                for (first, size), spot in zip(pieces, spots):

                    @pl.when(used_ref[own_tile, first // TILE_SIZE] == 0)
                    def _():
                        left[:, block * rows : (block + 1) * rows, spot] = jnp.zeros(
                            (2, rows, size), jnp.bfloat16
                        )

            right[2, inner, :] = -right[1, inner, :]
            lead, trail = left[0, :, inner], left[1, :, inner]
            for part, (upper, lower) in enumerate(((0, 2), (1, 0))):
                held[part] += jnp.dot(
                    lead, right[upper, inner, :], preferred_element_type=jnp.float32
                ) + jnp.dot(trail, right[lower, inner, :], preferred_element_type=jnp.float32)

        for block in range(count):
            for part in range(2):
                held_copy(block, part, True).start()
        pltpu.make_async_copy(held, held, held_sem).wait()

    operands = planes + sources + given
    moved = 4 * height * depth + 4 * depth * TILE_SIZE + 8 * height * TILE_SIZE
    return pl.pallas_call(
        kernel,
        out_shape=jax.ShapeDtypeStruct((2, span, TILE_SIZE), jnp.float32),
        grid_spec=pltpu.PrefetchScalarGridSpec(
            num_scalar_prefetch=3,
            grid=(1,),
            in_specs=[pl.BlockSpec(memory_space=pl.ANY)] * len(operands),
            out_specs=pl.BlockSpec(memory_space=pl.ANY),
            scratch_shapes=[
                pltpu.VMEM((2, height, depth), jnp.bfloat16),
                pltpu.VMEM((3, depth, TILE_SIZE), jnp.bfloat16),
                pltpu.VMEM((2, height, TILE_SIZE), jnp.float32),
                pltpu.SemaphoreType.DMA,
                pltpu.SemaphoreType.DMA((chunks,)),
                pltpu.SemaphoreType.DMA,
            ],
        ),
        input_output_aliases={} if base is None else {3 + len(operands) - 1: 0},
        cost_estimate=pl.CostEstimate(
            flops=8 * height * depth * TILE_SIZE, bytes_accessed=moved, transcendentals=0
        ),
        compiler_params=pltpu.CompilerParams(vmem_limit_bytes=60 * 1024 * 1024),
    )(device, jnp.asarray(plan), used, *operands)


def used_tiles(aperture, lengths, rcv_index, total):
    lists = lax.dynamic_index_in_dim(aperture, rcv_index, 1, keepdims=False)
    slot = jnp.arange(lists.shape[1], dtype=jnp.int32)
    wanted = (slot[None, :] < lengths)[:, :, None]
    tiles = jnp.arange(total // TILE_SIZE, dtype=jnp.int32)
    return jnp.any(wanted & (lists[:, :, None] == tiles), axis=1).astype(jnp.int32)


def local(data, fill_mask, obliquity, aperture, lengths):
    _, rows, total = data.shape
    src_count = lax.axis_size("src")
    rcv_count = lax.axis_size("rcv")
    src_index = lax.axis_index("src")
    rcv_index = lax.axis_index("rcv")
    devices = src_count * rcv_count
    span = rows * rcv_count
    device = (src_index * rcv_count + rcv_index).reshape(1)
    phased = rows % 128 == 0 and rcv_count % 4 == 0 and rcv_count > 4

    order = ring_order(rcv_count)
    owner, mine = np.divmod(np.arange(devices), rcv_count)
    place = np.asarray([order.index(i) for i in range(rcv_count)])[mine]
    half = rcv_count // 2
    steps = (rcv_count - 1) // 2

    def origin(offset):
        return np.asarray(order)[(place + offset) % rcv_count]

    def here(numbers):
        return jnp.asarray(numbers, jnp.int32)[device[0]]

    forward = [(order[i], order[(i + 1) % rcv_count]) for i in range(rcv_count)]
    backward = [(b, a) for a, b in forward]

    def hop(planes, pairs):
        return tuple(lax.ppermute(p, "rcv", pairs) for p in planes)

    used = used_tiles(aperture, lengths, rcv_index, total)
    my_gains = -lax.dynamic_slice_in_dim(obliquity, src_index * span, span)
    gains = my_gains.reshape(rcv_count, rows, 1)

    def tiles_of(blocks, column):
        if phased:
            return cut(blocks, column, gains, device)
        out = []
        for planes, first in blocks:
            start = here(column) * TILE_SIZE
            cuts = [lax.dynamic_slice_in_dim(p, start, TILE_SIZE, 1) for p in planes]
            gain = lax.dynamic_index_in_dim(gains, here(first), 0, keepdims=True)
            out.append((jnp.stack(cuts).astype(jnp.float32) * gain).astype(jnp.bfloat16))
        return jnp.stack(out)

    columns = []

    def spread(held, origins):
        held_by = [(held, 0)]
        bit = src_count // 2
        while bit:
            swap = [(i, i ^ bit) for i in range(src_count)]
            held_by += [(lax.ppermute(x, "src", swap), mask ^ bit) for x, mask in held_by]
            bit //= 2
        for pieces, mask in held_by:
            for index, first in enumerate(origins):
                columns.append((pieces, index, (owner ^ mask) * span + first * rows, mask))

    def collect(blocks):
        tiles = tiles_of(blocks, mine)
        spread(tiles, [first for _, first in blocks])

    blocks = transposed_blocks(data, devices)
    arrived = [
        lax.all_to_all(b, ("src", "rcv"), split_axis=0, concat_axis=0, tiled=True) for b in blocks
    ]
    own, ahead, behind = [], [], []
    for part in range(2):
        own.append(fill(data, fill_mask, arrived[part], part))
        ahead.append(lax.ppermute(own[part], "rcv", forward))
        behind.append(lax.ppermute(own[part], "rcv", backward))

    rows_of = {0: (own, origin(0)), -1: (ahead, origin(-1)), 1: (behind, origin(1))}
    far = origin(half)
    if not phased:
        collect([rows_of[0]])
        collect([rows_of[-1], rows_of[1]])
        for step in range(2, steps + 1):
            ahead, behind = hop(ahead, forward), hop(behind, backward)
            rows_of[-step], rows_of[step] = (ahead, origin(-step)), (behind, origin(step))
            collect([rows_of[-step], rows_of[step]])
        if rcv_count % 2 == 0:
            last = hop(ahead[:1], forward) + hop(behind[1:], backward)
            rows_of[half] = (last, far)
            collect([rows_of[half]])
        row_buffers, row_starts, pieces, starts = [], [], [], []
        for planes, first in rows_of.values():
            row_buffers += [(planes[0], 0), (planes[1], 1)]
            row_starts += [here(first * rows)] * 2
        for array, index, first, _ in columns:
            if index == 0:
                pieces.append(array)
            starts.append(here(first))
        return product(row_buffers, row_starts, pieces, starts, used, span, total)

    quarter = rcv_count // 4
    near = [quarter - 1, quarter, rcv_count - 1 - quarter, rcv_count - quarter]

    def from_mate(offset):
        pairs = []
        for i in near:
            mate = rcv_count - 1 - i
            if (mate + offset) % rcv_count == (i + half) % rcv_count:
                pairs.append((order[mate], order[i]))
        return pairs

    across = [(order[i], order[(i + half) % rcv_count]) for i in range(rcv_count)]
    far_pieces = cut([(own, origin(0))], far, gains, device)
    far_pieces = lax.ppermute(far_pieces, "rcv", across)
    spread(far_pieces, [far])
    collect([rows_of[0]])
    inside = [0] + [o for step in range(1, steps) for o in (-step, step)]
    outside = [-steps, steps]

    def as_rows(offsets):
        return [(rows_of[o][0], rows_of[o][1] * rows) for o in offsets]

    for step in range(2, steps + 1):
        collect([rows_of[1 - step], rows_of[step - 1]])
        moved = []
        for part in range(2):
            moved.append(lax.ppermute(ahead[part], "rcv", forward))
            moved.append(lax.ppermute(behind[part], "rcv", backward))
        ahead, behind = moved[0::2], moved[1::2]
        rows_of[-step], rows_of[step] = (ahead, origin(-step)), (behind, origin(step))
    taken = [hop(rows_of[offset][0], from_mate(offset)) for offset in (-1, 1)]
    late_from = len(columns)
    collect([rows_of[-steps], rows_of[steps]])
    early, late = columns[:late_from], columns[late_from:]
    out = job(
        device, None, as_rows(inside), early, [c[2] for c in late], used, span, total, True, False
    )
    turns = [
        [(order[(i + d) % rcv_count], order[i]) for i in range(rcv_count) if i not in near]
        for d in (-1, 1)
    ]
    last = []
    for part, plane in enumerate((ahead[0], behind[1])):
        last.append(lax.ppermute(plane, "rcv", turns[part]))
    packed = [(array, index, first, 0) for array, index, first, _ in late]
    out = job(device, out, as_rows(inside), packed, [], used, span, total, False, True)
    out = job(device, out, as_rows(outside), columns, [], used, span, total, True, False)
    chosen = np.zeros(devices)
    for number, offset in enumerate((-1, 1), start=1):
        for _, target in from_mate(offset):
            chosen[mine == target] = number
    candidates = [(*last, *taken[0], *taken[1])]
    rows_far = [(candidates[0], far * rows)]
    return job(device, out, rows_far, columns, [], used, span, total, True, False, [chosen])


def solution(mesh):
    placed = (
        P(None, ("src", "rcv"), None),
        P(("src", "rcv"), None),
        P(),
        P("src", None, None),
        P("src", "rcv"),
    )

    return jax.shard_map(
        local, mesh=mesh, in_specs=placed, out_specs=P(None, "src", "rcv"), check_vma=False
    )
```

```python
import jax
import jax.numpy as jnp
import numpy as np
from jax import lax
from jax.experimental import pallas as pl
from jax.experimental.pallas import tpu as pltpu
from jax.sharding import PartitionSpec as P


TILE_SIZE = 512


def ring_order(count):
    return list(range(0, count, 2)) + list(range(1, count, 2))[::-1]


def split_kernel(data_ref, *out_refs):
    rows = data_ref.shape[1]
    for part, out_ref in enumerate(out_refs):
        for block in range(out_ref.shape[0]):
            out_ref[block] = data_ref[part, :, block * rows : (block + 1) * rows].T


def transposed_blocks(data, devices):
    _, rows, _ = data.shape
    if rows % 128:
        return tuple(jnp.transpose(p.reshape(rows, devices, rows), (1, 0, 2)) for p in data)
    group = 8
    return pl.pallas_call(
        split_kernel,
        out_shape=(jax.ShapeDtypeStruct((devices, rows, rows), data.dtype),) * 2,
        grid=(devices // group,),
        in_specs=[pl.BlockSpec((2, rows, group * rows), lambda i: (0, 0, i))],
        out_specs=(pl.BlockSpec((group, rows, rows), lambda i: (i, 0, 0)),) * 2,
    )(data)


def fill_kernel(data_ref, mask_ref, arrived_ref, out_ref):
    rows = data_ref.shape[0]
    for block in range(arrived_ref.shape[0]):
        span = slice(block * rows, (block + 1) * rows)
        out_ref[:, span] = jnp.where(
            mask_ref[:, span] == 1, data_ref[:, span], arrived_ref[block]
        )


def fill(data, mask, arrived, part):
    _, rows, total = data.shape
    devices = arrived.shape[0]
    if rows % 128:
        transposed = jnp.transpose(arrived, (2, 0, 1)).reshape(rows, total)
        return jnp.where(mask == 1, data[part], transposed)
    group = 8
    return pl.pallas_call(
        fill_kernel,
        out_shape=jax.ShapeDtypeStruct((rows, total), data.dtype),
        grid=(devices // group,),
        in_specs=[
            pl.BlockSpec((None, rows, group * rows), lambda i: (part, 0, i)),
            pl.BlockSpec((rows, group * rows), lambda i: (0, i)),
            pl.BlockSpec((group, rows, rows), lambda i: (i, 0, 0)),
        ],
        out_specs=pl.BlockSpec((rows, group * rows), lambda i: (0, i)),
    )(data, mask, arrived)


def product_kernel(rows, plan_ref, used_ref, *refs):
    (row_refs, piece_refs), out_ref, scratch = refs[0], refs[1], refs[2:]
    left, right, row_sem, piece_sem = scratch
    inner_tiles = right.shape[0]
    out_tiles = out_ref.shape[1] // TILE_SIZE

    def piece_copies():
        copies = []
        at = len(row_refs)
        for ref in piece_refs:
            for index in range(ref.shape[0]):
                first = plan_ref[at]
                tile, offset = first // TILE_SIZE, first % TILE_SIZE
                for part in range(2):
                    row = pl.multiple_of(offset + (1 - part) * TILE_SIZE, rows)
                    copies.append(
                        pltpu.make_async_copy(
                            ref.at[index, part],
                            right.at[tile, pl.ds(row, rows), :],
                            piece_sem,
                        )
                    )
                at += 1
        return copies

    def start_rows(tile):
        for index, (ref, part) in enumerate(row_refs):
            row = pl.multiple_of(plan_ref[index], rows)
            column = pl.multiple_of(tile * 2 * TILE_SIZE + part * TILE_SIZE, TILE_SIZE)
            pltpu.make_async_copy(
                ref.at[:, pl.ds(pl.multiple_of(tile * TILE_SIZE, TILE_SIZE), TILE_SIZE)],
                left.at[pl.ds(row, rows), pl.ds(column, TILE_SIZE)],
                row_sem.at[tile],
            ).start()

    for copy in piece_copies():
        copy.start()

    @pl.loop(0, inner_tiles)
    def _(tile):
        start_rows(tile)

    out_ref[...] = jnp.zeros_like(out_ref)
    pltpu.make_async_copy(
        right.at[:, pl.ds(0, 2 * TILE_SIZE), :], right.at[:, pl.ds(0, 2 * TILE_SIZE), :], piece_sem
    ).wait()

    @pl.loop(0, inner_tiles)
    def _(tile):
        columns = pl.ds(pl.multiple_of(tile * 2 * TILE_SIZE, 2 * TILE_SIZE), 2 * TILE_SIZE)
        pltpu.make_async_copy(left.at[:, columns], left.at[:, columns], row_sem.at[tile]).wait()
        right[tile, 2 * TILE_SIZE :, :] = -right[tile, :TILE_SIZE, :]

        @pl.loop(0, out_tiles)
        def _(out_tile):
            @pl.when(used_ref[out_tile, tile] == 1)
            def _():
                span = pl.ds(pl.multiple_of(out_tile * TILE_SIZE, TILE_SIZE), TILE_SIZE)
                lhs = left[span, columns]
                for part in range(2):
                    rhs = right[tile, pl.ds((1 - part) * TILE_SIZE, 2 * TILE_SIZE), :]
                    out_ref[part, span, :] += jnp.dot(lhs, rhs, preferred_element_type=jnp.float32)


def product(row_buffers, row_starts, pieces, piece_starts, used, span, total):
    rows = row_buffers[0][0].shape[0]
    parts = [part for _, part in row_buffers]
    arrays = [array for array, _ in row_buffers] + list(pieces)
    plan = jnp.stack(row_starts + piece_starts).astype(jnp.int32)

    def kernel(plan_ref, used_ref, *refs):
        ins = refs[: len(arrays)]
        row_refs = list(zip(ins[: len(parts)], parts))
        product_kernel(
            rows, plan_ref, used_ref, (row_refs, ins[len(parts) :]), *refs[len(arrays) :]
        )

    inner_tiles = total // TILE_SIZE
    return pl.pallas_call(
        kernel,
        out_shape=jax.ShapeDtypeStruct((2, span, TILE_SIZE), jnp.float32),
        grid_spec=pltpu.PrefetchScalarGridSpec(
            num_scalar_prefetch=2,
            grid=(1,),
            in_specs=[pl.BlockSpec(memory_space=pl.ANY)] * len(arrays),
            out_specs=pl.BlockSpec((2, span, TILE_SIZE), lambda i, *_: (0, 0, 0), pipeline_mode=pl.Buffered(1)),
            scratch_shapes=[
                pltpu.VMEM((span, 2 * total), jnp.bfloat16),
                pltpu.VMEM((inner_tiles, 3 * TILE_SIZE, TILE_SIZE), jnp.bfloat16),
                pltpu.SemaphoreType.DMA((inner_tiles,)),
                pltpu.SemaphoreType.DMA,
            ],
        ),
        compiler_params=pltpu.CompilerParams(vmem_limit_bytes=67_000_000),
    )(plan, used, *arrays)


def cut_kernel(device_ref, place_ref, *refs):
    planes, out_ref = refs[:-1], refs[-1]
    for block in range(out_ref.shape[0]):
        first, second, gain = planes[3 * block : 3 * block + 3]
        for part, ref in enumerate((first, second)):
            out_ref[block, part] = (ref[...].astype(jnp.float32) * gain[...]).astype(jnp.bfloat16)


def cut(blocks, column, gains, device):
    rows = blocks[0][0][0].shape[0]
    place = np.stack([column] + [first for _, first in blocks], axis=1).astype(np.int32)
    specs, operands = [], []
    for index, (planes, _) in enumerate(blocks):
        specs += [pl.BlockSpec((rows, TILE_SIZE), lambda i, me, place: (0, place[me[0], 0]))] * 2
        specs.append(
            pl.BlockSpec((None, rows, 1), lambda i, me, place, at=index + 1: (place[me[0], at], 0, 0))
        )
        operands += [planes[0], planes[1], gains]
    shape = (len(blocks), 2, rows, TILE_SIZE)
    return pl.pallas_call(
        cut_kernel,
        out_shape=jax.ShapeDtypeStruct(shape, jnp.bfloat16),
        grid_spec=pltpu.PrefetchScalarGridSpec(
            num_scalar_prefetch=2,
            grid=(1,),
            in_specs=specs,
            out_specs=pl.BlockSpec(shape, lambda i, me, place: (0, 0, 0, 0)),
        ),
    )(device, jnp.asarray(place), *operands)


def job(device, base, row_blocks, columns, absent, used, span, total, full, accumulate, choice=(), groups=1):
    rows = row_blocks[0][0][0].shape[0]
    count, height = len(row_blocks), len(row_blocks) * rows
    chunks = 1 + max(column[3] for column in columns)
    depth = total if full else len(columns) * rows
    chunk_depth = depth // chunks
    plan = np.stack(
        [first for _, first in row_blocks]
        + [column[2] for column in columns]
        + list(absent)
        + list(choice),
        axis=1,
    ).astype(np.int32)
    planes = [plane for block, _ in row_blocks for plane in block]
    sources, source_at = [], []
    for pieces, *_ in columns:
        if not any(pieces is source for source in sources):
            sources.append(pieces)
        source_at.append([source is pieces for source in sources].index(True))
    given = [] if base is None else [base]
    bounds = [count * turn // groups for turn in range(groups + 1)]
    turns = list(zip(bounds[:-1], bounds[1:]))
    members = [[at for at, column in enumerate(columns) if column[3] == c] for c in range(chunks)]

    def kernel(device_ref, plan_ref, used_ref, *refs):
        plane_refs = refs[: len(planes)]
        source_refs = refs[len(planes) : len(planes) + len(sources)]
        out_ref, left, right, held, left_sem, right_sem, held_sem = refs[-7:]
        me = device_ref[0]

        def first_of(at):
            return pl.multiple_of(plan_ref[me, at], rows)

        def inner_of(chunk):
            if not full:
                return slice(None)
            start = plan_ref[me, count + members[chunk][0]] // chunk_depth * chunk_depth
            return pl.ds(pl.multiple_of(start, chunk_depth), chunk_depth)

        def held_copy(block, part, out, sem):
            here = held.at[part, pl.ds(block * rows, rows), :]
            there = out_ref.at[part, pl.ds(first_of(block), rows), :]
            pair = (here, there) if out else (there, here)
            return pltpu.make_async_copy(*pair, sem)

        def start_left(turn, chunk):
            sem, inner = left_sem.at[turn, chunk], inner_of(chunk)
            for block in range(*turns[turn]):
                for part in range(2):
                    here = pl.ds(block * rows, rows)
                    if not full:
                        for at in range(len(columns)):
                            pltpu.make_async_copy(
                                plane_refs[2 * block + part].at[:, pl.ds(first_of(count + at), rows)],
                                left.at[part, here, pl.ds(at * rows, rows)],
                                sem,
                            ).start()
                        continue
                    for at in range(len(planes) // 2 if choice else 1):
                        ref = plane_refs[2 * (block + at) + part]
                        copy = pltpu.make_async_copy(ref.at[:, inner], left.at[part, here, inner], sem)
                        if choice:
                            pl.when(plan_ref[me, plan.shape[1] - 1] == at)(copy.start)
                        else:
                            copy.start()

        def start_right(chunk):
            for at in members[chunk]:
                row = first_of(count + at) if full else at * rows
                for part in range(2):
                    pltpu.make_async_copy(
                        source_refs[source_at[at]].at[columns[at][1], part],
                        right.at[part, pl.ds(row, rows), :],
                        right_sem.at[chunk],
                    ).start()

        for chunk in range(chunks):
            start_right(chunk)
            start_left(0, chunk)
        for turn in range(1, groups):
            for chunk in range(chunks):
                start_left(turn, chunk)
        if accumulate:
            for turn in range(groups):
                for block in range(*turns[turn]):
                    for part in range(2):
                        held_copy(block, part, False, held_sem.at[turn]).start()
        for at in range(len(absent)):
            row = first_of(count + len(columns) + at)
            right[:, pl.ds(row, rows), :] = jnp.zeros((3, rows, TILE_SIZE), jnp.bfloat16)

        for turn, (first, end) in enumerate(turns):
            band = slice(first * rows, end * rows)
            if accumulate:
                view = held.at[:, pl.ds(first * rows, (end - first) * rows), :]
                pltpu.make_async_copy(view, view, held_sem.at[turn]).wait()
            for chunk in range(chunks):
                inner = inner_of(chunk)
                if turn == 0:
                    view = right.at[pl.ds(0, 2), pl.ds(0, len(members[chunk]) * rows), :]
                    pltpu.make_async_copy(view, view, right_sem.at[chunk]).wait()
                    right[2, inner, :] = -right[1, inner, :]
                view = left.at[:, pl.ds(0, (end - first) * rows), pl.ds(0, chunk_depth)]
                pltpu.make_async_copy(view, view, left_sem.at[turn, chunk]).wait()
                if full:
                    start = plan_ref[me, count + members[chunk][0]] // chunk_depth * chunk_depth
                    tiles = [(start + t, TILE_SIZE) for t in range(0, chunk_depth, TILE_SIZE)]
                    spots = [pl.ds(pl.multiple_of(p, TILE_SIZE), n) for p, n in tiles]
                else:
                    tiles = [(plan_ref[me, count + at], rows) for at in members[chunk]]
                    spots = [pl.ds(at * rows, rows) for at in members[chunk]]
                for block in range(first, end):
                    own_tile = plan_ref[me, block] // TILE_SIZE
                    for (inner_row, size), spot in zip(tiles, spots):

                        @pl.when(used_ref[own_tile, inner_row // TILE_SIZE] == 0)
                        def _():
                            left[:, block * rows : (block + 1) * rows, spot] = jnp.zeros(
                                (2, rows, size), jnp.bfloat16
                            )

                lead, trail = left[0, band, inner], left[1, band, inner]
                for part, (upper, lower) in enumerate(((0, 2), (1, 0))):
                    both = jnp.dot(
                        lead, right[upper, inner, :], preferred_element_type=jnp.float32
                    ) + jnp.dot(trail, right[lower, inner, :], preferred_element_type=jnp.float32)
                    if chunk == 0 and not accumulate:
                        held[part, band] = both
                    else:
                        held[part, band] += both
                    if chunk == chunks - 1:
                        for block in range(first, end):
                            held_copy(block, part, True, held_sem.at[groups]).start()
        pltpu.make_async_copy(held, held, held_sem.at[groups]).wait()

    operands = planes + sources + given
    moved = 4 * height * depth + 4 * depth * TILE_SIZE + 8 * height * TILE_SIZE
    return pl.pallas_call(
        kernel,
        out_shape=jax.ShapeDtypeStruct((2, span, TILE_SIZE), jnp.float32),
        grid_spec=pltpu.PrefetchScalarGridSpec(
            num_scalar_prefetch=3,
            grid=(1,),
            in_specs=[pl.BlockSpec(memory_space=pl.ANY)] * len(operands),
            out_specs=pl.BlockSpec(memory_space=pl.ANY),
            scratch_shapes=[
                pltpu.VMEM((2, height, depth), jnp.bfloat16),
                pltpu.VMEM((3, depth, TILE_SIZE), jnp.bfloat16),
                pltpu.VMEM((2, height, TILE_SIZE), jnp.float32),
                pltpu.SemaphoreType.DMA((groups, chunks)),
                pltpu.SemaphoreType.DMA((chunks,)),
                pltpu.SemaphoreType.DMA((groups + 1,)),
            ],
        ),
        input_output_aliases={} if base is None else {3 + len(operands) - 1: 0},
        cost_estimate=pl.CostEstimate(
            flops=8 * height * depth * TILE_SIZE, bytes_accessed=moved, transcendentals=0
        ),
        compiler_params=pltpu.CompilerParams(vmem_limit_bytes=60 * 1024 * 1024),
    )(device, jnp.asarray(plan), used, *operands)


def used_tiles(aperture, lengths, rcv_index, total):
    lists = lax.dynamic_index_in_dim(aperture, rcv_index, 1, keepdims=False)
    slot = jnp.arange(lists.shape[1], dtype=jnp.int32)
    wanted = (slot[None, :] < lengths)[:, :, None]
    tiles = jnp.arange(total // TILE_SIZE, dtype=jnp.int32)
    return jnp.any(wanted & (lists[:, :, None] == tiles), axis=1).astype(jnp.int32)


def local(data, fill_mask, obliquity, aperture, lengths):
    _, rows, total = data.shape
    src_count = lax.axis_size("src")
    rcv_count = lax.axis_size("rcv")
    src_index = lax.axis_index("src")
    rcv_index = lax.axis_index("rcv")
    devices = src_count * rcv_count
    span = rows * rcv_count
    device = (src_index * rcv_count + rcv_index).reshape(1)
    phased = rows % 128 == 0 and rcv_count % 4 == 0 and rcv_count > 4

    order = ring_order(rcv_count)
    owner, mine = np.divmod(np.arange(devices), rcv_count)
    place = np.asarray([order.index(i) for i in range(rcv_count)])[mine]
    half = rcv_count // 2
    steps = (rcv_count - 1) // 2

    def origin(offset):
        return np.asarray(order)[(place + offset) % rcv_count]

    def here(numbers):
        return jnp.asarray(numbers, jnp.int32)[device[0]]

    forward = [(order[i], order[(i + 1) % rcv_count]) for i in range(rcv_count)]
    backward = [(b, a) for a, b in forward]

    def hop(planes, pairs):
        return tuple(lax.ppermute(p, "rcv", pairs) for p in planes)

    used = used_tiles(aperture, lengths, rcv_index, total)
    my_gains = -lax.dynamic_slice_in_dim(obliquity, src_index * span, span)
    gains = my_gains.reshape(rcv_count, rows, 1)

    def tiles_of(blocks, column):
        if phased:
            return cut(blocks, column, gains, device)
        out = []
        for planes, first in blocks:
            start = here(column) * TILE_SIZE
            cuts = [lax.dynamic_slice_in_dim(p, start, TILE_SIZE, 1) for p in planes]
            gain = lax.dynamic_index_in_dim(gains, here(first), 0, keepdims=True)
            out.append((jnp.stack(cuts).astype(jnp.float32) * gain).astype(jnp.bfloat16))
        return jnp.stack(out)

    columns = []

    def spread(held, origins):
        held_by = [(held, 0)]
        bit = src_count // 2
        while bit:
            swap = [(i, i ^ bit) for i in range(src_count)]
            held_by += [(lax.ppermute(x, "src", swap), mask ^ bit) for x, mask in held_by]
            bit //= 2
        for pieces, mask in held_by:
            for index, first in enumerate(origins):
                columns.append((pieces, index, (owner ^ mask) * span + first * rows, mask))

    def collect(blocks):
        tiles = tiles_of(blocks, mine)
        spread(tiles, [first for _, first in blocks])

    blocks = transposed_blocks(data, devices)
    arrived = [
        lax.all_to_all(b, ("src", "rcv"), split_axis=0, concat_axis=0, tiled=True) for b in blocks
    ]
    own, ahead, behind = [], [], []
    for part in range(2):
        own.append(fill(data, fill_mask, arrived[part], part))
        ahead.append(lax.ppermute(own[part], "rcv", forward))
        behind.append(lax.ppermute(own[part], "rcv", backward))

    rows_of = {0: (own, origin(0)), -1: (ahead, origin(-1)), 1: (behind, origin(1))}
    far = origin(half)
    if not phased:
        collect([rows_of[0]])
        collect([rows_of[-1], rows_of[1]])
        for step in range(2, steps + 1):
            ahead, behind = hop(ahead, forward), hop(behind, backward)
            rows_of[-step], rows_of[step] = (ahead, origin(-step)), (behind, origin(step))
            collect([rows_of[-step], rows_of[step]])
        if rcv_count % 2 == 0:
            last = hop(ahead[:1], forward) + hop(behind[1:], backward)
            rows_of[half] = (last, far)
            collect([rows_of[half]])
        row_buffers, row_starts, pieces, starts = [], [], [], []
        for planes, first in rows_of.values():
            row_buffers += [(planes[0], 0), (planes[1], 1)]
            row_starts += [here(first * rows)] * 2
        for array, index, first, _ in columns:
            if index == 0:
                pieces.append(array)
            starts.append(here(first))
        return product(row_buffers, row_starts, pieces, starts, used, span, total)

    quarter = rcv_count // 4
    near = [quarter - 1, quarter, rcv_count - 1 - quarter, rcv_count - quarter]

    def from_mate(offset):
        pairs = []
        for i in near:
            mate = rcv_count - 1 - i
            if (mate + offset) % rcv_count == (i + half) % rcv_count:
                pairs.append((order[mate], order[i]))
        return pairs

    across = [(order[i], order[(i + half) % rcv_count]) for i in range(rcv_count)]
    far_pieces = cut([(own, origin(0))], far, gains, device)
    far_pieces = lax.ppermute(far_pieces, "rcv", across)
    spread(far_pieces, [far])
    collect([rows_of[0]])
    inside = [0] + [o for step in range(1, steps) for o in (-step, step)]
    outside = [-steps, steps]

    def as_rows(offsets):
        return [(rows_of[o][0], rows_of[o][1] * rows) for o in offsets]

    for step in range(2, steps + 1):
        collect([rows_of[1 - step], rows_of[step - 1]])
        moved = []
        for part in range(2):
            moved.append(lax.ppermute(ahead[part], "rcv", forward))
            moved.append(lax.ppermute(behind[part], "rcv", backward))
        ahead, behind = moved[0::2], moved[1::2]
        rows_of[-step], rows_of[step] = (ahead, origin(-step)), (behind, origin(step))
    taken = [hop(rows_of[offset][0], from_mate(offset)) for offset in (-1, 1)]
    late_from = len(columns)
    collect([rows_of[-steps], rows_of[steps]])
    early, late = columns[:late_from], columns[late_from:]
    out = job(
        device, None, as_rows(inside), early, [c[2] for c in late], used, span, total, True, False
    )
    turns = [
        [(order[(i + d) % rcv_count], order[i]) for i in range(rcv_count) if i not in near]
        for d in (-1, 1)
    ]
    last = []
    for part, plane in enumerate((ahead[0], behind[1])):
        last.append(lax.ppermute(plane, "rcv", turns[part]))
    absent = [c[2] for c in late]
    out = job(device, out, as_rows(outside), early, absent, used, span, total, True, False)
    packed = [(array, index, first, 0) for array, index, first, _ in late]
    nearer = as_rows(inside + outside)
    out = job(device, out, nearer, packed, [], used, span, total, False, True, groups=3)
    chosen = np.zeros(devices)
    for number, offset in enumerate((-1, 1), start=1):
        for _, target in from_mate(offset):
            chosen[mine == target] = number
    candidates = [(*last, *taken[0], *taken[1])]
    rows_far = [(candidates[0], far * rows)]
    return job(device, out, rows_far, columns, [], used, span, total, True, False, [chosen])


def solution(mesh):
    placed = (
        P(None, ("src", "rcv"), None),
        P(("src", "rcv"), None),
        P(),
        P("src", None, None),
        P("src", "rcv"),
    )

    return jax.shard_map(
        local, mesh=mesh, in_specs=placed, out_specs=P(None, "src", "rcv"), check_vma=False
    )
```

```python
import jax
import jax.numpy as jnp
import numpy as np
from jax import lax
from jax.experimental import pallas as pl
from jax.experimental.pallas import tpu as pltpu
from jax.sharding import PartitionSpec as P


TILE_SIZE = 512


def ring_order(count):
    return list(range(0, count, 2)) + list(range(1, count, 2))[::-1]


def split_kernel(data_ref, *out_refs):
    rows = data_ref.shape[1]
    for part, out_ref in enumerate(out_refs):
        for block in range(out_ref.shape[0]):
            out_ref[block] = data_ref[part, :, block * rows : (block + 1) * rows].T


def transposed_blocks(data, devices):
    _, rows, _ = data.shape
    if rows % 128:
        return tuple(jnp.transpose(p.reshape(rows, devices, rows), (1, 0, 2)) for p in data)
    group = 8
    return pl.pallas_call(
        split_kernel,
        out_shape=(jax.ShapeDtypeStruct((devices, rows, rows), data.dtype),) * 2,
        grid=(devices // group,),
        in_specs=[pl.BlockSpec((2, rows, group * rows), lambda i: (0, 0, i))],
        out_specs=(pl.BlockSpec((group, rows, rows), lambda i: (i, 0, 0)),) * 2,
    )(data)


def fill_kernel(data_ref, mask_ref, arrived_ref, out_ref):
    rows = data_ref.shape[0]
    for block in range(arrived_ref.shape[0]):
        span = slice(block * rows, (block + 1) * rows)
        out_ref[:, span] = jnp.where(
            mask_ref[:, span] == 1, data_ref[:, span], arrived_ref[block]
        )


def fill(data, mask, arrived, part):
    _, rows, total = data.shape
    devices = arrived.shape[0]
    if rows % 128:
        transposed = jnp.transpose(arrived, (2, 0, 1)).reshape(rows, total)
        return jnp.where(mask == 1, data[part], transposed)
    group = 8
    return pl.pallas_call(
        fill_kernel,
        out_shape=jax.ShapeDtypeStruct((rows, total), data.dtype),
        grid=(devices // group,),
        in_specs=[
            pl.BlockSpec((None, rows, group * rows), lambda i: (part, 0, i)),
            pl.BlockSpec((rows, group * rows), lambda i: (0, i)),
            pl.BlockSpec((group, rows, rows), lambda i: (i, 0, 0)),
        ],
        out_specs=pl.BlockSpec((rows, group * rows), lambda i: (0, i)),
    )(data, mask, arrived)


def product_kernel(rows, plan_ref, used_ref, *refs):
    (row_refs, piece_refs), out_ref, scratch = refs[0], refs[1], refs[2:]
    left, right, row_sem, piece_sem = scratch
    inner_tiles = right.shape[0]
    out_tiles = out_ref.shape[1] // TILE_SIZE

    def piece_copies():
        copies = []
        at = len(row_refs)
        for ref in piece_refs:
            for index in range(ref.shape[0]):
                first = plan_ref[at]
                tile, offset = first // TILE_SIZE, first % TILE_SIZE
                for part in range(2):
                    row = pl.multiple_of(offset + (1 - part) * TILE_SIZE, rows)
                    copies.append(
                        pltpu.make_async_copy(
                            ref.at[index, part],
                            right.at[tile, pl.ds(row, rows), :],
                            piece_sem,
                        )
                    )
                at += 1
        return copies

    def start_rows(tile):
        for index, (ref, part) in enumerate(row_refs):
            row = pl.multiple_of(plan_ref[index], rows)
            column = pl.multiple_of(tile * 2 * TILE_SIZE + part * TILE_SIZE, TILE_SIZE)
            pltpu.make_async_copy(
                ref.at[:, pl.ds(pl.multiple_of(tile * TILE_SIZE, TILE_SIZE), TILE_SIZE)],
                left.at[pl.ds(row, rows), pl.ds(column, TILE_SIZE)],
                row_sem.at[tile],
            ).start()

    for copy in piece_copies():
        copy.start()

    @pl.loop(0, inner_tiles)
    def _(tile):
        start_rows(tile)

    out_ref[...] = jnp.zeros_like(out_ref)
    pltpu.make_async_copy(
        right.at[:, pl.ds(0, 2 * TILE_SIZE), :], right.at[:, pl.ds(0, 2 * TILE_SIZE), :], piece_sem
    ).wait()

    @pl.loop(0, inner_tiles)
    def _(tile):
        columns = pl.ds(pl.multiple_of(tile * 2 * TILE_SIZE, 2 * TILE_SIZE), 2 * TILE_SIZE)
        pltpu.make_async_copy(left.at[:, columns], left.at[:, columns], row_sem.at[tile]).wait()
        right[tile, 2 * TILE_SIZE :, :] = -right[tile, :TILE_SIZE, :]

        @pl.loop(0, out_tiles)
        def _(out_tile):
            @pl.when(used_ref[out_tile, tile] == 1)
            def _():
                span = pl.ds(pl.multiple_of(out_tile * TILE_SIZE, TILE_SIZE), TILE_SIZE)
                lhs = left[span, columns]
                for part in range(2):
                    rhs = right[tile, pl.ds((1 - part) * TILE_SIZE, 2 * TILE_SIZE), :]
                    out_ref[part, span, :] += jnp.dot(lhs, rhs, preferred_element_type=jnp.float32)


def product(row_buffers, row_starts, pieces, piece_starts, used, span, total):
    rows = row_buffers[0][0].shape[0]
    parts = [part for _, part in row_buffers]
    arrays = [array for array, _ in row_buffers] + list(pieces)
    plan = jnp.stack(row_starts + piece_starts).astype(jnp.int32)

    def kernel(plan_ref, used_ref, *refs):
        ins = refs[: len(arrays)]
        row_refs = list(zip(ins[: len(parts)], parts))
        product_kernel(
            rows, plan_ref, used_ref, (row_refs, ins[len(parts) :]), *refs[len(arrays) :]
        )

    inner_tiles = total // TILE_SIZE
    return pl.pallas_call(
        kernel,
        out_shape=jax.ShapeDtypeStruct((2, span, TILE_SIZE), jnp.float32),
        grid_spec=pltpu.PrefetchScalarGridSpec(
            num_scalar_prefetch=2,
            grid=(1,),
            in_specs=[pl.BlockSpec(memory_space=pl.ANY)] * len(arrays),
            out_specs=pl.BlockSpec((2, span, TILE_SIZE), lambda i, *_: (0, 0, 0), pipeline_mode=pl.Buffered(1)),
            scratch_shapes=[
                pltpu.VMEM((span, 2 * total), jnp.bfloat16),
                pltpu.VMEM((inner_tiles, 3 * TILE_SIZE, TILE_SIZE), jnp.bfloat16),
                pltpu.SemaphoreType.DMA((inner_tiles,)),
                pltpu.SemaphoreType.DMA,
            ],
        ),
        compiler_params=pltpu.CompilerParams(vmem_limit_bytes=67_000_000),
    )(plan, used, *arrays)


def cut_kernel(device_ref, place_ref, *refs):
    planes, out_ref = refs[:-1], refs[-1]
    for block in range(out_ref.shape[0]):
        first, second, gain = planes[3 * block : 3 * block + 3]
        for part, ref in enumerate((first, second)):
            out_ref[block, part] = (ref[...].astype(jnp.float32) * gain[...]).astype(jnp.bfloat16)


def cut(blocks, column, gains, device):
    rows = blocks[0][0][0].shape[0]
    place = np.stack([column] + [first for _, first in blocks], axis=1).astype(np.int32)
    specs, operands = [], []
    for index, (planes, _) in enumerate(blocks):
        specs += [pl.BlockSpec((rows, TILE_SIZE), lambda i, me, place: (0, place[me[0], 0]))] * 2
        specs.append(
            pl.BlockSpec((None, rows, 1), lambda i, me, place, at=index + 1: (place[me[0], at], 0, 0))
        )
        operands += [planes[0], planes[1], gains]
    shape = (len(blocks), 2, rows, TILE_SIZE)
    return pl.pallas_call(
        cut_kernel,
        out_shape=jax.ShapeDtypeStruct(shape, jnp.bfloat16),
        grid_spec=pltpu.PrefetchScalarGridSpec(
            num_scalar_prefetch=2,
            grid=(1,),
            in_specs=specs,
            out_specs=pl.BlockSpec(shape, lambda i, me, place: (0, 0, 0, 0)),
        ),
    )(device, jnp.asarray(place), *operands)


class Job:
    def __init__(self, row_blocks, columns, absent=(), choice=None, pack=(), packed=(), splits=()):
        self.row_blocks, self.columns, self.absent = row_blocks, columns, list(absent)
        self.choice, self.pack, self.packed = choice, list(pack), list(packed)
        self.planes = [] if packed else [p for planes, _ in row_blocks for p in planes]
        self.sources, self.source_at = [], []
        for pieces, *_ in columns:
            if not any(pieces is source for source in self.sources):
                self.sources.append(pieces)
            self.source_at.append([pieces is source for source in self.sources].index(True))
        self.rows = columns[0][0].shape[2]
        self.count = len(row_blocks)
        self.chunks = 1 if packed else 1 + max(column[3] for column in columns)
        bounds = [0, *splits, self.count]
        self.turns = list(zip(bounds[:-1], bounds[1:]))

    def numbers(self):
        listed = [first for _, first in self.row_blocks] + [column[2] for column in self.columns]
        listed += self.absent + [first for first, _ in self.pack]
        return listed + ([] if self.choice is None else [self.choice])

    def operands(self):
        return self.planes + self.sources + [array for array, _ in self.packed]

    def depth(self, total):
        return len(self.columns) * self.rows if self.packed else total

    def scratch(self, total):
        height, depth = self.count * self.rows, self.depth(total)
        shapes = [
            pltpu.VMEM((2, height, depth), jnp.bfloat16),
            pltpu.VMEM((3, depth, TILE_SIZE), jnp.bfloat16),
            pltpu.VMEM((2, height, TILE_SIZE), jnp.float32),
            pltpu.SemaphoreType.DMA((len(self.turns), self.chunks)),
            pltpu.SemaphoreType.DMA((self.chunks,)),
            pltpu.SemaphoreType.DMA((len(self.turns) + 1,)),
        ]
        if self.pack:
            shapes.append(pltpu.VMEM((2, height, len(self.pack) * self.rows), jnp.bfloat16))
            shapes.append(pltpu.SemaphoreType.DMA)
        return shapes

    def bind(self, number, used_ref, refs, out_ref, pack_ref, scratch, total):
        self.number, self.used_ref, self.out_ref, self.pack_ref = number, used_ref, out_ref, pack_ref
        self.plane_refs = refs[: len(self.planes)]
        self.source_refs = refs[len(self.planes) : len(self.planes) + len(self.sources)]
        self.packed_refs = refs[len(self.planes) + len(self.sources) :]
        self.left, self.right, self.held, self.left_sem, self.right_sem, self.held_sem = scratch[:6]
        self.packing = scratch[6:]
        self.chunk_depth = self.depth(total) // self.chunks
        self.members = [
            [at for at, column in enumerate(self.columns) if self.packed or column[3] == chunk]
            for chunk in range(self.chunks)
        ]

    def first_of(self, at):
        return pl.multiple_of(self.number(at), self.rows)

    def start_row(self, chunk):
        return self.number(self.count + self.members[chunk][0]) // self.chunk_depth * self.chunk_depth

    def inner_of(self, chunk):
        if self.packed:
            return slice(None)
        return pl.ds(pl.multiple_of(self.start_row(chunk), self.chunk_depth), self.chunk_depth)

    def held_copy(self, block, part, out, sem):
        here = self.held.at[part, pl.ds(block * self.rows, self.rows), :]
        there = self.out_ref.at[part, pl.ds(self.first_of(block), self.rows), :]
        return pltpu.make_async_copy(*((here, there) if out else (there, here)), sem)

    def start_right(self, chunk):
        for at in self.members[chunk]:
            row = at * self.rows if self.packed else self.first_of(self.count + at)
            for part in range(2):
                pltpu.make_async_copy(
                    self.source_refs[self.source_at[at]].at[self.columns[at][1], part],
                    self.right.at[part, pl.ds(row, self.rows), :],
                    self.right_sem.at[chunk],
                ).start()

    def start_left(self, turn, chunk):
        sem, inner = self.left_sem.at[turn, chunk], self.inner_of(chunk)
        first, end = self.turns[turn]
        rows, base = self.rows, 0
        for ref, (_, blocks) in zip(self.packed_refs, self.packed):
            low, high = max(first, base), min(end, base + blocks)
            if low < high:
                pltpu.make_async_copy(
                    ref.at[:, pl.ds((low - base) * rows, (high - low) * rows), :],
                    self.left.at[:, pl.ds(low * rows, (high - low) * rows), :],
                    sem,
                ).start()
            base += blocks
        if self.packed:
            return
        for block in range(first, end):
            for part in range(2):
                here = self.left.at[part, pl.ds(block * rows, rows), inner]
                candidates = 1 if self.choice is None else len(self.planes) // 2
                for at in range(candidates):
                    ref = self.plane_refs[2 * (block + at) + part]
                    copy = pltpu.make_async_copy(ref.at[:, inner], here, sem)
                    if self.choice is None:
                        copy.start()
                    else:
                        pl.when(self.number(len(self.numbers()) - 1) == at)(copy.start)

    def start(self):
        for chunk in range(self.chunks):
            self.start_right(chunk)
            self.start_left(0, chunk)
        for turn in range(len(self.turns)):
            if turn:
                for chunk in range(self.chunks):
                    self.start_left(turn, chunk)
            if self.packed:
                for block in range(*self.turns[turn]):
                    for part in range(2):
                        self.held_copy(block, part, False, self.held_sem.at[turn]).start()

    def mask(self, chunk, first, end):
        rows = self.rows
        for block in range(first, end):
            own_tile = self.number(block) // TILE_SIZE
            for offset in range(0, self.chunk_depth, TILE_SIZE):
                row = self.start_row(chunk) + offset
                spot = pl.ds(pl.multiple_of(row, TILE_SIZE), TILE_SIZE)

                @pl.when(self.used_ref[own_tile, row // TILE_SIZE] == 0)
                def _():
                    self.left[:, block * rows : (block + 1) * rows, spot] = jnp.zeros(
                        (2, rows, TILE_SIZE), jnp.bfloat16
                    )

    def run(self):
        rows, left, right, held = self.rows, self.left, self.right, self.held
        for at in range(len(self.absent)):
            row = self.first_of(self.count + len(self.columns) + at)
            right[:, pl.ds(row, rows), :] = jnp.zeros((3, rows, TILE_SIZE), jnp.bfloat16)
        pack_at = self.count + len(self.columns) + len(self.absent)
        for turn, (first, end) in enumerate(self.turns):
            band = slice(first * rows, end * rows)
            if self.packed:
                view = held.at[:, pl.ds(first * rows, (end - first) * rows), :]
                pltpu.make_async_copy(view, view, self.held_sem.at[turn]).wait()
            for chunk in range(self.chunks):
                inner = self.inner_of(chunk)
                if turn == 0:
                    view = right.at[pl.ds(0, 2), pl.ds(0, len(self.members[chunk]) * rows), :]
                    pltpu.make_async_copy(view, view, self.right_sem.at[chunk]).wait()
                    right[2, inner, :] = -right[1, inner, :]
                view = left.at[:, pl.ds(0, (end - first) * rows), pl.ds(0, self.chunk_depth)]
                pltpu.make_async_copy(view, view, self.left_sem.at[turn, chunk]).wait()
                if not self.packed:
                    self.mask(chunk, first, end)
                for at, (_, owner) in enumerate(self.pack):
                    if owner == chunk:
                        column = pl.ds(self.first_of(pack_at + at), rows)
                        self.packing[0][:, band, at * rows : (at + 1) * rows] = left[:, band, column]
                lead, trail = left[0, band, inner], left[1, band, inner]
                for part, (upper, lower) in enumerate(((0, 2), (1, 0))):
                    both = jnp.dot(
                        lead, right[upper, inner, :], preferred_element_type=jnp.float32
                    ) + jnp.dot(trail, right[lower, inner, :], preferred_element_type=jnp.float32)
                    if chunk == 0 and not self.packed:
                        held[part, band] = both
                    else:
                        held[part, band] += both
                    if chunk == self.chunks - 1:
                        for block in range(first, end):
                            self.held_copy(block, part, True, self.held_sem.at[len(self.turns)]).start()
        if self.pack:
            pltpu.make_async_copy(self.packing[0], self.pack_ref, self.packing[1]).start()

    def finish(self):
        if self.pack:
            pltpu.make_async_copy(self.packing[0], self.pack_ref, self.packing[1]).wait()
        pltpu.make_async_copy(self.held, self.held, self.held_sem.at[len(self.turns)]).wait()


def launch(device, base, jobs, used, span, total):
    plan = np.stack([n for job in jobs for n in job.numbers()], axis=1).astype(np.int32)
    operands = [array for job in jobs for array in job.operands()]
    operands += [] if base is None else [base]
    packing = [job for job in jobs if job.pack]
    scratch = [job.scratch(total) for job in jobs]
    out_shape = [jax.ShapeDtypeStruct((2, span, TILE_SIZE), jnp.float32)]
    for job in packing:
        shape = (2, job.count * job.rows, len(job.pack) * job.rows)
        out_shape.append(jax.ShapeDtypeStruct(shape, jnp.bfloat16))

    def kernel(device_ref, plan_ref, used_ref, *refs):
        outs = refs[len(operands) : len(operands) + len(out_shape)]
        spare = refs[len(operands) + len(out_shape) :]
        at, spare_at, plan_at = 0, 0, 0
        for job, shapes in zip(jobs, scratch):
            size = len(job.operands())
            job.bind(
                lambda n, plan_at=plan_at: plan_ref[device_ref[0], plan_at + n],
                used_ref,
                refs[at : at + size],
                outs[0],
                outs[1 + packing.index(job)] if job.pack else None,
                spare[spare_at : spare_at + len(shapes)],
                total,
            )
            at, spare_at, plan_at = at + size, spare_at + len(shapes), plan_at + len(job.numbers())
        for job in jobs:
            job.start()
        for job in jobs:
            job.run()
        for job in jobs:
            job.finish()

    flops = sum(8 * job.count * job.rows * job.depth(total) * TILE_SIZE for job in jobs)
    return pl.pallas_call(
        kernel,
        out_shape=out_shape,
        grid_spec=pltpu.PrefetchScalarGridSpec(
            num_scalar_prefetch=3,
            grid=(1,),
            in_specs=[pl.BlockSpec(memory_space=pl.ANY)] * len(operands),
            out_specs=[pl.BlockSpec(memory_space=pl.ANY)] * len(out_shape),
            scratch_shapes=[shape for shapes in scratch for shape in shapes],
        ),
        input_output_aliases={} if base is None else {3 + len(operands) - 1: 0},
        cost_estimate=pl.CostEstimate(flops=flops, bytes_accessed=20 * span * total, transcendentals=0),
        compiler_params=pltpu.CompilerParams(vmem_limit_bytes=60 * 1024 * 1024),
    )(device, jnp.asarray(plan), used, *operands)


def used_tiles(aperture, lengths, rcv_index, total):
    lists = lax.dynamic_index_in_dim(aperture, rcv_index, 1, keepdims=False)
    slot = jnp.arange(lists.shape[1], dtype=jnp.int32)
    wanted = (slot[None, :] < lengths)[:, :, None]
    tiles = jnp.arange(total // TILE_SIZE, dtype=jnp.int32)
    return jnp.any(wanted & (lists[:, :, None] == tiles), axis=1).astype(jnp.int32)


def local(data, fill_mask, obliquity, aperture, lengths):
    _, rows, total = data.shape
    src_count = lax.axis_size("src")
    rcv_count = lax.axis_size("rcv")
    src_index = lax.axis_index("src")
    rcv_index = lax.axis_index("rcv")
    devices = src_count * rcv_count
    span = rows * rcv_count
    device = (src_index * rcv_count + rcv_index).reshape(1)
    phased = rows % 128 == 0 and rcv_count % 4 == 0 and rcv_count > 4

    order = ring_order(rcv_count)
    owner, mine = np.divmod(np.arange(devices), rcv_count)
    place = np.asarray([order.index(i) for i in range(rcv_count)])[mine]
    half = rcv_count // 2
    steps = (rcv_count - 1) // 2

    def origin(offset):
        return np.asarray(order)[(place + offset) % rcv_count]

    def here(numbers):
        return jnp.asarray(numbers, jnp.int32)[device[0]]

    forward = [(order[i], order[(i + 1) % rcv_count]) for i in range(rcv_count)]
    backward = [(b, a) for a, b in forward]

    def hop(planes, pairs):
        return tuple(lax.ppermute(p, "rcv", pairs) for p in planes)

    used = used_tiles(aperture, lengths, rcv_index, total)
    my_gains = -lax.dynamic_slice_in_dim(obliquity, src_index * span, span)
    gains = my_gains.reshape(rcv_count, rows, 1)

    def tiles_of(blocks, column):
        if phased:
            return cut(blocks, column, gains, device)
        out = []
        for planes, first in blocks:
            start = here(column) * TILE_SIZE
            cuts = [lax.dynamic_slice_in_dim(p, start, TILE_SIZE, 1) for p in planes]
            gain = lax.dynamic_index_in_dim(gains, here(first), 0, keepdims=True)
            out.append((jnp.stack(cuts).astype(jnp.float32) * gain).astype(jnp.bfloat16))
        return jnp.stack(out)

    columns = []

    def spread(held, origins):
        held_by = [(held, 0)]
        bit = src_count // 2
        while bit:
            swap = [(i, i ^ bit) for i in range(src_count)]
            held_by += [(lax.ppermute(x, "src", swap), mask ^ bit) for x, mask in held_by]
            bit //= 2
        for pieces, mask in held_by:
            for index, first in enumerate(origins):
                columns.append((pieces, index, (owner ^ mask) * span + first * rows, mask))

    def collect(blocks):
        tiles = tiles_of(blocks, mine)
        spread(tiles, [first for _, first in blocks])

    blocks = transposed_blocks(data, devices)
    arrived = [
        lax.all_to_all(b, ("src", "rcv"), split_axis=0, concat_axis=0, tiled=True) for b in blocks
    ]
    own, ahead, behind = [], [], []
    for part in range(2):
        own.append(fill(data, fill_mask, arrived[part], part))
        ahead.append(lax.ppermute(own[part], "rcv", forward))
        behind.append(lax.ppermute(own[part], "rcv", backward))

    rows_of = {0: (own, origin(0)), -1: (ahead, origin(-1)), 1: (behind, origin(1))}
    far = origin(half)
    if not phased:
        collect([rows_of[0]])
        collect([rows_of[-1], rows_of[1]])
        for step in range(2, steps + 1):
            ahead, behind = hop(ahead, forward), hop(behind, backward)
            rows_of[-step], rows_of[step] = (ahead, origin(-step)), (behind, origin(step))
            collect([rows_of[-step], rows_of[step]])
        if rcv_count % 2 == 0:
            last = hop(ahead[:1], forward) + hop(behind[1:], backward)
            rows_of[half] = (last, far)
            collect([rows_of[half]])
        row_buffers, row_starts, pieces, starts = [], [], [], []
        for planes, first in rows_of.values():
            row_buffers += [(planes[0], 0), (planes[1], 1)]
            row_starts += [here(first * rows)] * 2
        for array, index, first, _ in columns:
            if index == 0:
                pieces.append(array)
            starts.append(here(first))
        return product(row_buffers, row_starts, pieces, starts, used, span, total)

    quarter = rcv_count // 4
    near = [quarter - 1, quarter, rcv_count - 1 - quarter, rcv_count - quarter]

    def from_mate(offset):
        pairs = []
        for i in near:
            mate = rcv_count - 1 - i
            if (mate + offset) % rcv_count == (i + half) % rcv_count:
                pairs.append((order[mate], order[i]))
        return pairs

    collect([rows_of[0]])
    inside = [0] + [o for step in range(1, steps) for o in (-step, step)]
    outside = [-steps, steps]

    def as_rows(offsets):
        return [(rows_of[o][0], rows_of[o][1] * rows) for o in offsets]

    for step in range(2, steps + 1):
        collect([rows_of[1 - step], rows_of[step - 1]])
        moved = []
        for part in range(2):
            moved.append(lax.ppermute(ahead[part], "rcv", forward))
            moved.append(lax.ppermute(behind[part], "rcv", backward))
        ahead, behind = moved[0::2], moved[1::2]
        rows_of[-step], rows_of[step] = (ahead, origin(-step)), (behind, origin(step))
    taken = [hop(rows_of[offset][0], from_mate(offset)) for offset in (-1, 1)]
    late_from = len(columns)
    collect([rows_of[-steps], rows_of[steps]])
    across = [(order[i], order[(i + half) % rcv_count]) for i in range(rcv_count)]
    far_pieces = cut([(own, origin(0))], far, gains, device)
    far_pieces = lax.ppermute(far_pieces, "rcv", across)
    spread(far_pieces, [far])
    early, late = columns[:late_from], columns[late_from:]
    absent, pack = [c[2] for c in late], [(c[2], c[3]) for c in late]
    jobs = [Job(as_rows(inside), early, absent, pack=pack)]
    out, packed_inside = launch(device, None, jobs, used, span, total)
    turns = [
        [(order[(i + d) % rcv_count], order[i]) for i in range(rcv_count) if i not in near]
        for d in (-1, 1)
    ]
    last = []
    for part, plane in enumerate((ahead[0], behind[1])):
        last.append(lax.ppermute(plane, "rcv", turns[part]))
    jobs = [Job(as_rows(outside), early, absent, pack=pack)]
    out, packed_outside = launch(device, out, jobs, used, span, total)
    chosen = np.zeros(devices)
    for number, offset in enumerate((-1, 1), start=1):
        for _, target in from_mate(offset):
            chosen[mine == target] = number
    candidates = (*last, *taken[0], *taken[1])
    packed = [(packed_inside, len(inside)), (packed_outside, len(outside))]
    splits = [len(inside) // 2, len(inside)]
    near_rows = Job(as_rows(inside + outside), late, packed=packed, splits=splits)
    far_rows = Job([(candidates, far * rows)], columns, choice=chosen)
    return launch(device, out, [near_rows, far_rows], used, span, total)[0]


def solution(mesh):
    placed = (
        P(None, ("src", "rcv"), None),
        P(("src", "rcv"), None),
        P(),
        P("src", None, None),
        P("src", "rcv"),
    )

    return jax.shard_map(
        local, mesh=mesh, in_specs=placed, out_specs=P(None, "src", "rcv"), check_vma=False
    )
```

```python
import jax
import jax.numpy as jnp
import numpy as np
from jax import lax
from jax.experimental import pallas as pl
from jax.experimental.pallas import tpu as pltpu
from jax.sharding import PartitionSpec as P


TILE_SIZE = 512
AHEAD = 2


def ring_order(count):
    return list(range(0, count, 2)) + list(range(1, count, 2))[::-1]


def split_kernel(data_ref, *out_refs):
    rows = data_ref.shape[1]
    for part, out_ref in enumerate(out_refs):
        for block in range(out_ref.shape[0]):
            out_ref[block] = data_ref[part, :, block * rows : (block + 1) * rows].T


def transposed_blocks(data, devices):
    _, rows, _ = data.shape
    if rows % 128:
        return tuple(jnp.transpose(p.reshape(rows, devices, rows), (1, 0, 2)) for p in data)
    group = 8
    return pl.pallas_call(
        split_kernel,
        out_shape=(jax.ShapeDtypeStruct((devices, rows, rows), data.dtype),) * 2,
        grid=(devices // group,),
        in_specs=[pl.BlockSpec((2, rows, group * rows), lambda i: (0, 0, i))],
        out_specs=(pl.BlockSpec((group, rows, rows), lambda i: (i, 0, 0)),) * 2,
    )(data)


def fill_kernel(data_ref, mask_ref, arrived_ref, out_ref):
    rows = data_ref.shape[0]
    for block in range(arrived_ref.shape[0]):
        span = slice(block * rows, (block + 1) * rows)
        out_ref[:, span] = jnp.where(
            mask_ref[:, span] == 1, data_ref[:, span], arrived_ref[block]
        )


def fill(data, mask, arrived, part):
    _, rows, total = data.shape
    devices = arrived.shape[0]
    if rows % 128:
        transposed = jnp.transpose(arrived, (2, 0, 1)).reshape(rows, total)
        return jnp.where(mask == 1, data[part], transposed)
    group = 8
    return pl.pallas_call(
        fill_kernel,
        out_shape=jax.ShapeDtypeStruct((rows, total), data.dtype),
        grid=(devices // group,),
        in_specs=[
            pl.BlockSpec((None, rows, group * rows), lambda i: (part, 0, i)),
            pl.BlockSpec((rows, group * rows), lambda i: (0, i)),
            pl.BlockSpec((group, rows, rows), lambda i: (i, 0, 0)),
        ],
        out_specs=pl.BlockSpec((rows, group * rows), lambda i: (0, i)),
    )(data, mask, arrived)


def product_kernel(rows, plan_ref, used_ref, *refs):
    (row_refs, piece_refs), out_ref, scratch = refs[0], refs[1], refs[2:]
    left, right, row_sem, piece_sem = scratch
    inner_tiles = right.shape[0]
    out_tiles = out_ref.shape[1] // TILE_SIZE

    def piece_copies():
        copies = []
        at = len(row_refs)
        for ref in piece_refs:
            for index in range(ref.shape[0]):
                first = plan_ref[at]
                tile, offset = first // TILE_SIZE, first % TILE_SIZE
                for part in range(2):
                    row = pl.multiple_of(offset + (1 - part) * TILE_SIZE, rows)
                    copies.append(
                        pltpu.make_async_copy(
                            ref.at[index, part],
                            right.at[tile, pl.ds(row, rows), :],
                            piece_sem,
                        )
                    )
                at += 1
        return copies

    def start_rows(tile):
        for index, (ref, part) in enumerate(row_refs):
            row = pl.multiple_of(plan_ref[index], rows)
            column = pl.multiple_of(tile * 2 * TILE_SIZE + part * TILE_SIZE, TILE_SIZE)
            pltpu.make_async_copy(
                ref.at[:, pl.ds(pl.multiple_of(tile * TILE_SIZE, TILE_SIZE), TILE_SIZE)],
                left.at[pl.ds(row, rows), pl.ds(column, TILE_SIZE)],
                row_sem.at[tile],
            ).start()

    for copy in piece_copies():
        copy.start()

    @pl.loop(0, inner_tiles)
    def _(tile):
        start_rows(tile)

    out_ref[...] = jnp.zeros_like(out_ref)
    pltpu.make_async_copy(
        right.at[:, pl.ds(0, 2 * TILE_SIZE), :], right.at[:, pl.ds(0, 2 * TILE_SIZE), :], piece_sem
    ).wait()

    @pl.loop(0, inner_tiles)
    def _(tile):
        columns = pl.ds(pl.multiple_of(tile * 2 * TILE_SIZE, 2 * TILE_SIZE), 2 * TILE_SIZE)
        pltpu.make_async_copy(left.at[:, columns], left.at[:, columns], row_sem.at[tile]).wait()
        right[tile, 2 * TILE_SIZE :, :] = -right[tile, :TILE_SIZE, :]

        @pl.loop(0, out_tiles)
        def _(out_tile):
            @pl.when(used_ref[out_tile, tile] == 1)
            def _():
                span = pl.ds(pl.multiple_of(out_tile * TILE_SIZE, TILE_SIZE), TILE_SIZE)
                lhs = left[span, columns]
                for part in range(2):
                    rhs = right[tile, pl.ds((1 - part) * TILE_SIZE, 2 * TILE_SIZE), :]
                    out_ref[part, span, :] += jnp.dot(lhs, rhs, preferred_element_type=jnp.float32)


def product(row_buffers, row_starts, pieces, piece_starts, used, span, total):
    rows = row_buffers[0][0].shape[0]
    parts = [part for _, part in row_buffers]
    arrays = [array for array, _ in row_buffers] + list(pieces)
    plan = jnp.stack(row_starts + piece_starts).astype(jnp.int32)

    def kernel(plan_ref, used_ref, *refs):
        ins = refs[: len(arrays)]
        row_refs = list(zip(ins[: len(parts)], parts))
        product_kernel(
            rows, plan_ref, used_ref, (row_refs, ins[len(parts) :]), *refs[len(arrays) :]
        )

    inner_tiles = total // TILE_SIZE
    return pl.pallas_call(
        kernel,
        out_shape=jax.ShapeDtypeStruct((2, span, TILE_SIZE), jnp.float32),
        grid_spec=pltpu.PrefetchScalarGridSpec(
            num_scalar_prefetch=2,
            grid=(1,),
            in_specs=[pl.BlockSpec(memory_space=pl.ANY)] * len(arrays),
            out_specs=pl.BlockSpec((2, span, TILE_SIZE), lambda i, *_: (0, 0, 0), pipeline_mode=pl.Buffered(1)),
            scratch_shapes=[
                pltpu.VMEM((span, 2 * total), jnp.bfloat16),
                pltpu.VMEM((inner_tiles, 3 * TILE_SIZE, TILE_SIZE), jnp.bfloat16),
                pltpu.SemaphoreType.DMA((inner_tiles,)),
                pltpu.SemaphoreType.DMA,
            ],
        ),
        compiler_params=pltpu.CompilerParams(vmem_limit_bytes=67_000_000),
    )(plan, used, *arrays)


def cut_kernel(device_ref, place_ref, *refs):
    ins, out_ref = refs[:-1], refs[-1]
    blocks, parts = out_ref.shape[:2]
    for block in range(blocks):
        *planes, gain = ins[(parts + 1) * block : (parts + 1) * (block + 1)]
        for part, ref in enumerate(planes):
            out_ref[block, part] = (ref[...].astype(jnp.float32) * gain[...]).astype(jnp.bfloat16)


def cut(blocks, column, gains, device, parts=(0, 1)):
    rows = blocks[0][0][0].shape[0]
    place = np.stack([column] + [first for _, first in blocks], axis=1).astype(np.int32)
    specs, operands = [], []
    for index, (planes, _) in enumerate(blocks):
        spec = pl.BlockSpec((rows, TILE_SIZE), lambda i, me, place: (0, place[me[0], 0]))
        specs += [spec] * len(parts)
        specs.append(
            pl.BlockSpec((None, rows, 1), lambda i, me, place, at=index + 1: (place[me[0], at], 0, 0))
        )
        operands += [*(planes[part] for part in parts), gains]
    shape = (len(blocks), len(parts), rows, TILE_SIZE)
    return pl.pallas_call(
        cut_kernel,
        out_shape=jax.ShapeDtypeStruct(shape, jnp.bfloat16),
        grid_spec=pltpu.PrefetchScalarGridSpec(
            num_scalar_prefetch=2,
            grid=(1,),
            in_specs=specs,
            out_specs=pl.BlockSpec(shape, lambda i, me, place: (0, 0, 0, 0)),
        ),
    )(device, jnp.asarray(place), *operands)


class Job:
    def __init__(self, row_blocks, columns, absent=(), choice=None, pack=(), packed=(), splits=()):
        self.row_blocks, self.columns, self.absent = row_blocks, columns, list(absent)
        self.choice, self.pack, self.packed = choice, list(pack), list(packed)
        self.planes, self.plane_bands = [], []
        for plane in [] if packed else [p for planes, _ in row_blocks for p in planes]:
            self.plane_bands.append([])
            row = 0
            for array in plane if isinstance(plane, tuple) else (plane,):
                self.plane_bands[-1].append((len(self.planes), row, array.shape[0]))
                self.planes.append(array)
                row += array.shape[0]
        self.sources, self.source_at = [], []
        for pieces, *_ in columns:
            apart = isinstance(pieces, tuple)
            spots = []
            for part, array in enumerate(pieces if apart else (pieces, pieces)):
                if not any(array is source for source in self.sources):
                    self.sources.append(array)
                spots.append(([array is source for source in self.sources].index(True), 0 if apart else part))
            self.source_at.append(spots)
        self.rows = self.sources[0].shape[2]
        self.count = len(row_blocks)
        self.chunks = 1 if packed else 1 + max(column[3] for column in columns)
        bounds = [0, *splits, self.count]
        self.turns = list(zip(bounds[:-1], bounds[1:]))

    def numbers(self):
        listed = [first for _, first in self.row_blocks] + [column[2] for column in self.columns]
        listed += [first for first, _ in self.absent + self.pack]
        return listed + ([] if self.choice is None else [self.choice])

    def operands(self):
        return self.planes + self.sources + [array for array, _ in self.packed]

    def depth(self, total):
        return len(self.columns) * self.rows if self.packed else total

    def scratch(self, total):
        height, depth = self.count * self.rows, self.depth(total)
        shapes = [
            pltpu.VMEM((self.chunks, 2, height, depth // self.chunks), jnp.bfloat16),
            pltpu.VMEM((self.chunks, 2, depth // self.chunks, TILE_SIZE), jnp.bfloat16),
            pltpu.VMEM((2, height, TILE_SIZE), jnp.float32),
            pltpu.SemaphoreType.DMA((len(self.turns), self.chunks)),
            pltpu.SemaphoreType.DMA((self.chunks,)),
            pltpu.SemaphoreType.DMA((len(self.turns) + 1,)),
        ]
        if self.pack:
            shapes.append(pltpu.VMEM((2, height, len(self.pack) * self.rows), jnp.bfloat16))
            shapes.append(pltpu.SemaphoreType.DMA)
        return shapes

    def bind(self, number, used_ref, refs, out_ref, pack_ref, scratch, total):
        self.number, self.used_ref, self.out_ref, self.pack_ref = number, used_ref, out_ref, pack_ref
        self.plane_refs = refs[: len(self.planes)]
        self.source_refs = refs[len(self.planes) : len(self.planes) + len(self.sources)]
        self.packed_refs = refs[len(self.planes) + len(self.sources) :]
        self.left, self.right, self.held, self.left_sem, self.right_sem, self.held_sem = scratch[:6]
        self.packing = scratch[6:]
        self.chunk_depth = self.depth(total) // self.chunks
        self.members = [
            [at for at, column in enumerate(self.columns) if self.packed or column[3] == chunk]
            for chunk in range(self.chunks)
        ]

    def first_of(self, at):
        return pl.multiple_of(self.number(at), self.rows)

    def start_row(self, chunk):
        return self.number(self.count + self.members[chunk][0]) // self.chunk_depth * self.chunk_depth

    def within(self, at):
        return pl.multiple_of(self.number(at) % self.chunk_depth, self.rows)

    def held_copy(self, block, part, out, sem):
        here = self.held.at[part, pl.ds(block * self.rows, self.rows), :]
        there = self.out_ref.at[part, pl.ds(self.first_of(block), self.rows), :]
        return pltpu.make_async_copy(*((here, there) if out else (there, here)), sem)

    def start_right(self, chunk):
        for at in self.members[chunk]:
            row = at * self.rows if self.packed else self.within(self.count + at)
            for part in range(2):
                source, part_at = self.source_at[at][part]
                pltpu.make_async_copy(
                    self.source_refs[source].at[self.columns[at][1], part_at],
                    self.right.at[chunk, part, pl.ds(row, self.rows), :],
                    self.right_sem.at[chunk],
                ).start()

    def start_left(self, turn, chunk):
        sem = self.left_sem.at[turn, chunk]
        first, end = self.turns[turn]
        rows, base = self.rows, 0
        for ref, (_, blocks) in zip(self.packed_refs, self.packed):
            low, high = max(first, base), min(end, base + blocks)
            if low < high:
                pltpu.make_async_copy(
                    ref.at[:, pl.ds((low - base) * rows, (high - low) * rows), :],
                    self.left.at[chunk, :, pl.ds(low * rows, (high - low) * rows), :],
                    sem,
                ).start()
            base += blocks
        if self.packed:
            return
        inner = pl.ds(pl.multiple_of(self.start_row(chunk), self.chunk_depth), self.chunk_depth)
        for block in range(first, end):
            for part in range(2):
                candidates = 1 if self.choice is None else len(self.plane_bands) // 2
                for at in range(candidates):
                    for index, row, size in self.plane_bands[2 * (block + at) + part]:
                        copy = pltpu.make_async_copy(
                            self.plane_refs[index].at[:, inner],
                            self.left.at[chunk, part, pl.ds(block * rows + row, size), :],
                            sem,
                        )
                        if self.choice is None:
                            copy.start()
                        else:
                            pl.when(self.number(len(self.numbers()) - 1) == at)(copy.start)

    def steps(self):
        return [(self, turn, chunk) for turn in range(len(self.turns)) for chunk in range(self.chunks)]

    def start(self, turn, chunk):
        if turn == 0:
            self.start_right(chunk)
        self.start_left(turn, chunk)
        if self.packed:
            for block in range(*self.turns[turn]):
                for part in range(2):
                    self.held_copy(block, part, False, self.held_sem.at[turn]).start()

    def clear_absent(self, chunk):
        for at, (_, owner) in enumerate(self.absent):
            if owner == chunk:
                row = self.within(self.count + len(self.columns) + at)
                self.right[chunk, :, pl.ds(row, self.rows), :] = jnp.zeros(
                    (2, self.rows, TILE_SIZE), jnp.bfloat16
                )

    def wait(self, turn, chunk):
        first, end = self.turns[turn]
        height = (end - first) * self.rows
        views = [(self.left.at[chunk, :, pl.ds(0, height), :], self.left_sem.at[turn, chunk])]
        if turn == 0:
            rows = len(self.members[chunk]) * self.rows
            views.append((self.right.at[chunk, :, pl.ds(0, rows), :], self.right_sem.at[chunk]))
        if self.packed:
            views.append((self.held.at[:, pl.ds(0, height), :], self.held_sem.at[turn]))
        for view, sem in views:
            pltpu.make_async_copy(view, view, sem).wait()

    def mask(self, chunk, first, end):
        rows = self.rows
        for block in range(first, end):
            own_tile = self.number(block) // TILE_SIZE
            for offset in range(0, self.chunk_depth, TILE_SIZE):
                tile = (self.start_row(chunk) + offset) // TILE_SIZE

                @pl.when(self.used_ref[own_tile, tile] == 0)
                def _():
                    self.left[
                        chunk, :, block * rows : (block + 1) * rows, offset : offset + TILE_SIZE
                    ] = jnp.zeros((2, rows, TILE_SIZE), jnp.bfloat16)

    def write_packed(self, chunk, first, end):
        rows, (packing, sem) = self.rows, self.packing
        pack_at = self.count + len(self.columns) + len(self.absent)
        band = slice(first * rows, end * rows)
        for at, (_, owner) in enumerate(self.pack):
            if owner == chunk:
                to = slice(at * rows, (at + 1) * rows)
                packing[:, band, to] = self.left[chunk, :, band, pl.ds(self.within(pack_at + at), rows)]
                area = (slice(None), pl.ds(first * rows, (end - first) * rows), pl.ds(at * rows, rows))
                pltpu.make_async_copy(packing.at[area], self.pack_ref.at[area], sem).start()

    def products(self, chunk, band):
        by_part = ((0, 0, 1, 1), (0, 1, 1, 0))
        out = []
        for part, (a, b, c, d) in enumerate(by_part):
            first = jnp.dot(
                self.left[chunk, a, band], self.right[chunk, b], preferred_element_type=jnp.float32
            )
            second = jnp.dot(
                self.left[chunk, c, band], self.right[chunk, d], preferred_element_type=jnp.float32
            )
            out.append(first + second if part else first - second)
        return out

    def run(self, turn, chunk):
        rows, held = self.rows, self.held
        first, end = self.turns[turn]
        band = slice(first * rows, end * rows)
        if not self.packed:
            self.mask(chunk, first, end)
            if turn == 0:
                self.clear_absent(chunk)
        if self.pack:
            self.write_packed(chunk, first, end)
        sums = self.products(chunk, band)
        for part in range(2):
            if chunk == 0 and not self.packed:
                held[part, band] = sums[part]
            else:
                held[part, band] += sums[part]
            if chunk == self.chunks - 1:
                for block in range(first, end):
                    self.held_copy(block, part, True, self.held_sem.at[len(self.turns)]).start()

    def finish(self):
        if self.pack:
            pltpu.make_async_copy(self.packing[0], self.pack_ref, self.packing[1]).wait()
        pltpu.make_async_copy(self.held, self.held, self.held_sem.at[len(self.turns)]).wait()


def launch(device, base, jobs, used, span, total):
    plan = np.stack([n for job in jobs for n in job.numbers()], axis=1).astype(np.int32)
    operands = [array for job in jobs for array in job.operands()]
    operands += [] if base is None else [base]
    packing = [job for job in jobs if job.pack]
    scratch = [job.scratch(total) for job in jobs]
    out_shape = [jax.ShapeDtypeStruct((2, span, TILE_SIZE), jnp.float32)]
    for job in packing:
        shape = (2, job.count * job.rows, len(job.pack) * job.rows)
        out_shape.append(jax.ShapeDtypeStruct(shape, jnp.bfloat16))

    def kernel(device_ref, plan_ref, used_ref, *refs):
        outs = refs[len(operands) : len(operands) + len(out_shape)]
        spare = refs[len(operands) + len(out_shape) :]
        at, spare_at, plan_at = 0, 0, 0
        for job, shapes in zip(jobs, scratch):
            size = len(job.operands())
            job.bind(
                lambda n, plan_at=plan_at: plan_ref[device_ref[0], plan_at + n],
                used_ref,
                refs[at : at + size],
                outs[0],
                outs[1 + packing.index(job)] if job.pack else None,
                spare[spare_at : spare_at + len(shapes)],
                total,
            )
            at, spare_at, plan_at = at + size, spare_at + len(shapes), plan_at + len(job.numbers())
        steps = [step for job in jobs for step in job.steps()]
        for job, *step in steps[:AHEAD]:
            job.start(*step)
        for at, (job, *step) in enumerate(steps):
            job.wait(*step)
            for later, *later_step in steps[at + AHEAD : at + AHEAD + 1]:
                later.start(*later_step)
            job.run(*step)
        for job in jobs:
            job.finish()

    flops = sum(8 * job.count * job.rows * job.depth(total) * TILE_SIZE for job in jobs)
    return pl.pallas_call(
        kernel,
        out_shape=out_shape,
        grid_spec=pltpu.PrefetchScalarGridSpec(
            num_scalar_prefetch=3,
            grid=(1,),
            in_specs=[pl.BlockSpec(memory_space=pl.ANY)] * len(operands),
            out_specs=[pl.BlockSpec(memory_space=pl.ANY)] * len(out_shape),
            scratch_shapes=[shape for shapes in scratch for shape in shapes],
        ),
        input_output_aliases={} if base is None else {3 + len(operands) - 1: 0},
        cost_estimate=pl.CostEstimate(flops=flops, bytes_accessed=20 * span * total, transcendentals=0),
        compiler_params=pltpu.CompilerParams(vmem_limit_bytes=60 * 1024 * 1024),
    )(device, jnp.asarray(plan), used, *operands)


def used_tiles(aperture, lengths, rcv_index, total):
    lists = lax.dynamic_index_in_dim(aperture, rcv_index, 1, keepdims=False)
    slot = jnp.arange(lists.shape[1], dtype=jnp.int32)
    wanted = (slot[None, :] < lengths)[:, :, None]
    tiles = jnp.arange(total // TILE_SIZE, dtype=jnp.int32)
    return jnp.any(wanted & (lists[:, :, None] == tiles), axis=1).astype(jnp.int32)


def local(data, fill_mask, obliquity, aperture, lengths):
    _, rows, total = data.shape
    src_count = lax.axis_size("src")
    rcv_count = lax.axis_size("rcv")
    src_index = lax.axis_index("src")
    rcv_index = lax.axis_index("rcv")
    devices = src_count * rcv_count
    span = rows * rcv_count
    device = (src_index * rcv_count + rcv_index).reshape(1)
    phased = rows % 128 == 0 and rcv_count % 4 == 0 and rcv_count > 4

    order = ring_order(rcv_count)
    owner, mine = np.divmod(np.arange(devices), rcv_count)
    place = np.asarray([order.index(i) for i in range(rcv_count)])[mine]
    half = rcv_count // 2
    steps = (rcv_count - 1) // 2

    def origin(offset):
        return np.asarray(order)[(place + offset) % rcv_count]

    def here(numbers):
        return jnp.asarray(numbers, jnp.int32)[device[0]]

    forward = [(order[i], order[(i + 1) % rcv_count]) for i in range(rcv_count)]
    backward = [(b, a) for a, b in forward]

    def hop(planes, pairs):
        return tuple(lax.ppermute(p, "rcv", pairs) for p in planes)

    used = used_tiles(aperture, lengths, rcv_index, total)
    my_gains = -lax.dynamic_slice_in_dim(obliquity, src_index * span, span)
    gains = my_gains.reshape(rcv_count, rows, 1)

    def tiles_of(blocks, column):
        if phased:
            return cut(blocks, column, gains, device)
        out = []
        for planes, first in blocks:
            start = here(column) * TILE_SIZE
            cuts = [lax.dynamic_slice_in_dim(p, start, TILE_SIZE, 1) for p in planes]
            gain = lax.dynamic_index_in_dim(gains, here(first), 0, keepdims=True)
            out.append((jnp.stack(cuts).astype(jnp.float32) * gain).astype(jnp.bfloat16))
        return jnp.stack(out)

    columns = []

    def exchange(held):
        held_by = [(held, 0)]
        bit = src_count // 2
        while bit:
            swap = [(i, i ^ bit) for i in range(src_count)]
            held_by += [(lax.ppermute(x, "src", swap), mask ^ bit) for x, mask in held_by]
            bit //= 2
        return held_by

    def note(held_by, origins):
        for pieces, mask in held_by:
            for index, first in enumerate(origins):
                columns.append((pieces, index, (owner ^ mask) * span + first * rows, mask))

    def collect(blocks):
        tiles = tiles_of(blocks, mine)
        note(exchange(tiles), [first for _, first in blocks])

    def collect_apart(blocks):
        by_part = []
        for part in range(2):
            tiles = cut(blocks, mine, gains, device, (part,))
            by_part.append(exchange(tiles))
        pairs = [((first, second), mask) for (first, mask), (second, _) in zip(*by_part)]
        note(pairs, [first for _, first in blocks])

    blocks = transposed_blocks(data, devices)
    arrived = [
        lax.all_to_all(b, ("src", "rcv"), split_axis=0, concat_axis=0, tiled=True) for b in blocks
    ]
    own, ahead, behind = [], [], []
    for part in range(2):
        own.append(fill(data, fill_mask, arrived[part], part))
        ahead.append(lax.ppermute(own[part], "rcv", forward))
        behind.append(lax.ppermute(own[part], "rcv", backward))

    rows_of = {0: (own, origin(0)), -1: (ahead, origin(-1)), 1: (behind, origin(1))}
    far = origin(half)
    if not phased:
        collect([rows_of[0]])
        collect([rows_of[-1], rows_of[1]])
        for step in range(2, steps + 1):
            ahead, behind = hop(ahead, forward), hop(behind, backward)
            rows_of[-step], rows_of[step] = (ahead, origin(-step)), (behind, origin(step))
            collect([rows_of[-step], rows_of[step]])
        if rcv_count % 2 == 0:
            last = hop(ahead[:1], forward) + hop(behind[1:], backward)
            rows_of[half] = (last, far)
            collect([rows_of[half]])
        row_buffers, row_starts, pieces, starts = [], [], [], []
        for planes, first in rows_of.values():
            row_buffers += [(planes[0], 0), (planes[1], 1)]
            row_starts += [here(first * rows)] * 2
        for array, index, first, _ in columns:
            if index == 0:
                pieces.append(array)
            starts.append(here(first))
        return product(row_buffers, row_starts, pieces, starts, used, span, total)

    quarter = rcv_count // 4
    near = [quarter - 1, quarter, rcv_count - 1 - quarter, rcv_count - quarter]

    def from_mate(offset):
        pairs = []
        for i in near:
            mate = rcv_count - 1 - i
            if (mate + offset) % rcv_count == (i + half) % rcv_count:
                pairs.append((order[mate], order[i]))
        return pairs

    collect([rows_of[0]])
    inside = [0] + [o for step in range(1, steps) for o in (-step, step)]
    outside = [-steps, steps]

    def as_rows(offsets):
        return [(rows_of[o][0], rows_of[o][1] * rows) for o in offsets]

    for step in range(2, steps + 1):
        collect([rows_of[1 - step], rows_of[step - 1]])
        moved = []
        for part in range(2):
            moved.append(lax.ppermute(ahead[part], "rcv", forward))
            moved.append(lax.ppermute(behind[part], "rcv", backward))
        ahead, behind = moved[0::2], moved[1::2]
        rows_of[-step], rows_of[step] = (ahead, origin(-step)), (behind, origin(step))
    taken = [hop(rows_of[offset][0], from_mate(offset)) for offset in (-1, 1)]
    late_from = len(columns)
    collect_apart([rows_of[-steps], rows_of[steps]])
    across = [(order[i], order[(i + half) % rcv_count]) for i in range(rcv_count)]
    far_pieces = cut([(own, origin(0))], far, gains, device)
    far_pieces = lax.ppermute(far_pieces, "rcv", across)
    note(exchange(far_pieces), [far])
    early, late = columns[:late_from], columns[late_from:]
    absent = pack = [(c[2], c[3]) for c in late]
    jobs = [Job(as_rows(inside), early, absent, pack=pack)]
    out, packed_inside = launch(device, None, jobs, used, span, total)
    turns = [
        [(order[(i + d) % rcv_count], order[i]) for i in range(rcv_count) if i not in near]
        for d in (-1, 1)
    ]
    last = []
    for part in range(2):
        upper = lax.ppermute(ahead[part][: rows // 2], "rcv", turns[0])
        lower = lax.ppermute(behind[part][rows // 2 :], "rcv", turns[1])
        last.append((upper, lower))
    jobs = [Job(as_rows(outside), early, absent, pack=pack)]
    out, packed_outside = launch(device, out, jobs, used, span, total)
    chosen = np.zeros(devices)
    for number, offset in enumerate((-1, 1), start=1):
        for _, target in from_mate(offset):
            chosen[mine == target] = number
    candidates = (*last, *taken[0], *taken[1])
    packed = [(packed_inside, len(inside)), (packed_outside, len(outside))]
    splits = [len(inside) // 2, len(inside)]
    jobs = [Job(as_rows(inside + outside), late, packed=packed, splits=splits)]
    out = launch(device, out, jobs, used, span, total)[0]
    jobs = [Job([(candidates, far * rows)], columns, choice=chosen)]
    return launch(device, out, jobs, used, span, total)[0]


def solution(mesh):
    placed = (
        P(None, ("src", "rcv"), None),
        P(("src", "rcv"), None),
        P(),
        P("src", None, None),
        P("src", "rcv"),
    )

    return jax.shard_map(
        local, mesh=mesh, in_specs=placed, out_specs=P(None, "src", "rcv"), check_vma=False
    )
```

```python
import jax
import jax.numpy as jnp
import numpy as np
from jax import lax
from jax.experimental import pallas as pl
from jax.experimental.pallas import tpu as pltpu
from jax.sharding import PartitionSpec as P


TILE_SIZE = 512
AHEAD = 2


def ring_order(count):
    return list(range(0, count, 2)) + list(range(1, count, 2))[::-1]


def split_kernel(data_ref, *out_refs):
    rows = data_ref.shape[1]
    for part, out_ref in enumerate(out_refs):
        for block in range(out_ref.shape[0]):
            out_ref[block] = data_ref[part, :, block * rows : (block + 1) * rows].T


def transposed_blocks(data, devices):
    _, rows, _ = data.shape
    if rows % 128:
        return tuple(jnp.transpose(p.reshape(rows, devices, rows), (1, 0, 2)) for p in data)
    group = 8
    return pl.pallas_call(
        split_kernel,
        out_shape=(jax.ShapeDtypeStruct((devices, rows, rows), data.dtype),) * 2,
        grid=(devices // group,),
        in_specs=[pl.BlockSpec((2, rows, group * rows), lambda i: (0, 0, i))],
        out_specs=(pl.BlockSpec((group, rows, rows), lambda i: (i, 0, 0)),) * 2,
    )(data)


def fill_kernel(data_ref, mask_ref, arrived_ref, out_ref):
    rows = data_ref.shape[0]
    for block in range(arrived_ref.shape[0]):
        span = slice(block * rows, (block + 1) * rows)
        out_ref[:, span] = jnp.where(
            mask_ref[:, span] == 1, data_ref[:, span], arrived_ref[block]
        )


def fill(data, mask, arrived, part):
    _, rows, total = data.shape
    devices = arrived.shape[0]
    if rows % 128:
        transposed = jnp.transpose(arrived, (2, 0, 1)).reshape(rows, total)
        return jnp.where(mask == 1, data[part], transposed)
    group = 8
    return pl.pallas_call(
        fill_kernel,
        out_shape=jax.ShapeDtypeStruct((rows, total), data.dtype),
        grid=(devices // group,),
        in_specs=[
            pl.BlockSpec((None, rows, group * rows), lambda i: (part, 0, i)),
            pl.BlockSpec((rows, group * rows), lambda i: (0, i)),
            pl.BlockSpec((group, rows, rows), lambda i: (i, 0, 0)),
        ],
        out_specs=pl.BlockSpec((rows, group * rows), lambda i: (0, i)),
    )(data, mask, arrived)


def product_kernel(rows, plan_ref, used_ref, *refs):
    (row_refs, piece_refs), out_ref, scratch = refs[0], refs[1], refs[2:]
    left, right, row_sem, piece_sem = scratch
    inner_tiles = right.shape[0]
    out_tiles = out_ref.shape[1] // TILE_SIZE

    def piece_copies():
        copies = []
        at = len(row_refs)
        for ref in piece_refs:
            for index in range(ref.shape[0]):
                first = plan_ref[at]
                tile, offset = first // TILE_SIZE, first % TILE_SIZE
                for part in range(2):
                    row = pl.multiple_of(offset + (1 - part) * TILE_SIZE, rows)
                    copies.append(
                        pltpu.make_async_copy(
                            ref.at[index, part],
                            right.at[tile, pl.ds(row, rows), :],
                            piece_sem,
                        )
                    )
                at += 1
        return copies

    def start_rows(tile):
        for index, (ref, part) in enumerate(row_refs):
            row = pl.multiple_of(plan_ref[index], rows)
            column = pl.multiple_of(tile * 2 * TILE_SIZE + part * TILE_SIZE, TILE_SIZE)
            pltpu.make_async_copy(
                ref.at[:, pl.ds(pl.multiple_of(tile * TILE_SIZE, TILE_SIZE), TILE_SIZE)],
                left.at[pl.ds(row, rows), pl.ds(column, TILE_SIZE)],
                row_sem.at[tile],
            ).start()

    for copy in piece_copies():
        copy.start()

    @pl.loop(0, inner_tiles)
    def _(tile):
        start_rows(tile)

    out_ref[...] = jnp.zeros_like(out_ref)
    pltpu.make_async_copy(
        right.at[:, pl.ds(0, 2 * TILE_SIZE), :], right.at[:, pl.ds(0, 2 * TILE_SIZE), :], piece_sem
    ).wait()

    @pl.loop(0, inner_tiles)
    def _(tile):
        columns = pl.ds(pl.multiple_of(tile * 2 * TILE_SIZE, 2 * TILE_SIZE), 2 * TILE_SIZE)
        pltpu.make_async_copy(left.at[:, columns], left.at[:, columns], row_sem.at[tile]).wait()
        right[tile, 2 * TILE_SIZE :, :] = -right[tile, :TILE_SIZE, :]

        @pl.loop(0, out_tiles)
        def _(out_tile):
            @pl.when(used_ref[out_tile, tile] == 1)
            def _():
                span = pl.ds(pl.multiple_of(out_tile * TILE_SIZE, TILE_SIZE), TILE_SIZE)
                lhs = left[span, columns]
                for part in range(2):
                    rhs = right[tile, pl.ds((1 - part) * TILE_SIZE, 2 * TILE_SIZE), :]
                    out_ref[part, span, :] += jnp.dot(lhs, rhs, preferred_element_type=jnp.float32)


def product(row_buffers, row_starts, pieces, piece_starts, used, span, total):
    rows = row_buffers[0][0].shape[0]
    parts = [part for _, part in row_buffers]
    arrays = [array for array, _ in row_buffers] + list(pieces)
    plan = jnp.stack(row_starts + piece_starts).astype(jnp.int32)

    def kernel(plan_ref, used_ref, *refs):
        ins = refs[: len(arrays)]
        row_refs = list(zip(ins[: len(parts)], parts))
        product_kernel(
            rows, plan_ref, used_ref, (row_refs, ins[len(parts) :]), *refs[len(arrays) :]
        )

    inner_tiles = total // TILE_SIZE
    return pl.pallas_call(
        kernel,
        out_shape=jax.ShapeDtypeStruct((2, span, TILE_SIZE), jnp.float32),
        grid_spec=pltpu.PrefetchScalarGridSpec(
            num_scalar_prefetch=2,
            grid=(1,),
            in_specs=[pl.BlockSpec(memory_space=pl.ANY)] * len(arrays),
            out_specs=pl.BlockSpec((2, span, TILE_SIZE), lambda i, *_: (0, 0, 0), pipeline_mode=pl.Buffered(1)),
            scratch_shapes=[
                pltpu.VMEM((span, 2 * total), jnp.bfloat16),
                pltpu.VMEM((inner_tiles, 3 * TILE_SIZE, TILE_SIZE), jnp.bfloat16),
                pltpu.SemaphoreType.DMA((inner_tiles,)),
                pltpu.SemaphoreType.DMA,
            ],
        ),
        compiler_params=pltpu.CompilerParams(vmem_limit_bytes=67_000_000),
    )(plan, used, *arrays)


def cut_kernel(device_ref, place_ref, *refs):
    ins, out_ref = refs[:-1], refs[-1]
    blocks, parts = out_ref.shape[:2]
    for block in range(blocks):
        *planes, gain = ins[(parts + 1) * block : (parts + 1) * (block + 1)]
        for part, ref in enumerate(planes):
            out_ref[block, part] = (ref[...].astype(jnp.float32) * gain[...]).astype(jnp.bfloat16)


def cut(blocks, column, gains, device, parts=(0, 1)):
    rows = blocks[0][0][0].shape[0]
    place = np.stack([column] + [first for _, first in blocks], axis=1).astype(np.int32)
    specs, operands = [], []
    for index, (planes, _) in enumerate(blocks):
        spec = pl.BlockSpec((rows, TILE_SIZE), lambda i, me, place: (0, place[me[0], 0]))
        specs += [spec] * len(parts)
        specs.append(
            pl.BlockSpec((None, rows, 1), lambda i, me, place, at=index + 1: (place[me[0], at], 0, 0))
        )
        operands += [*(planes[part] for part in parts), gains]
    shape = (len(blocks), len(parts), rows, TILE_SIZE)
    return pl.pallas_call(
        cut_kernel,
        out_shape=jax.ShapeDtypeStruct(shape, jnp.bfloat16),
        grid_spec=pltpu.PrefetchScalarGridSpec(
            num_scalar_prefetch=2,
            grid=(1,),
            in_specs=specs,
            out_specs=pl.BlockSpec(shape, lambda i, me, place: (0, 0, 0, 0)),
        ),
    )(device, jnp.asarray(place), *operands)


class Job:
    def __init__(self, row_blocks, columns, absent=(), choice=None, pack=(), packed=(), splits=()):
        self.row_blocks, self.columns, self.absent = row_blocks, columns, list(absent)
        self.choice, self.pack, self.packed = choice, list(pack), list(packed)
        self.planes, self.plane_bands = [], []
        for plane in [] if packed else [p for planes, _ in row_blocks for p in planes]:
            self.plane_bands.append([])
            row = 0
            for array in plane if isinstance(plane, tuple) else (plane,):
                self.plane_bands[-1].append((len(self.planes), row, array.shape[0]))
                self.planes.append(array)
                row += array.shape[0]
        self.sources, self.source_at = [], []
        for pieces, *_ in columns:
            apart = isinstance(pieces, tuple)
            spots = []
            for part, array in enumerate(pieces if apart else (pieces, pieces)):
                if not any(array is source for source in self.sources):
                    self.sources.append(array)
                spots.append(([array is source for source in self.sources].index(True), 0 if apart else part))
            self.source_at.append(spots)
        self.rows = self.sources[0].shape[2]
        self.count = len(row_blocks)
        self.chunks = 1 if packed else 1 + max(column[3] for column in columns)
        bounds = [0, *splits, self.count]
        self.turns = list(zip(bounds[:-1], bounds[1:]))

    def numbers(self):
        listed = [first for _, first in self.row_blocks] + [column[2] for column in self.columns]
        listed += [first for first, _ in self.absent + self.pack]
        return listed + ([] if self.choice is None else [self.choice])

    def operands(self):
        return self.planes + self.sources + [array for array, _ in self.packed]

    def depth(self, total):
        return len(self.columns) * self.rows if self.packed else total

    def scratch(self, total):
        height, depth = self.count * self.rows, self.depth(total)
        shapes = [
            pltpu.VMEM((self.chunks, 2, height, depth // self.chunks), jnp.bfloat16),
            pltpu.VMEM((self.chunks, 2, depth // self.chunks, TILE_SIZE), jnp.bfloat16),
            pltpu.VMEM((2, height, TILE_SIZE), jnp.float32),
            pltpu.SemaphoreType.DMA((len(self.turns), self.chunks)),
            pltpu.SemaphoreType.DMA((self.chunks,)),
            pltpu.SemaphoreType.DMA((len(self.turns) + 1,)),
        ]
        if self.pack:
            shapes.append(pltpu.VMEM((2, height, len(self.pack) * self.rows), jnp.bfloat16))
            shapes.append(pltpu.SemaphoreType.DMA)
        return shapes

    def bind(self, number, used_ref, refs, out_ref, pack_ref, scratch, total):
        self.number, self.used_ref, self.out_ref, self.pack_ref = number, used_ref, out_ref, pack_ref
        self.plane_refs = refs[: len(self.planes)]
        self.source_refs = refs[len(self.planes) : len(self.planes) + len(self.sources)]
        self.packed_refs = refs[len(self.planes) + len(self.sources) :]
        self.left, self.right, self.held, self.left_sem, self.right_sem, self.held_sem = scratch[:6]
        self.packing = scratch[6:]
        self.chunk_depth = self.depth(total) // self.chunks
        self.members = [
            [at for at, column in enumerate(self.columns) if self.packed or column[3] == chunk]
            for chunk in range(self.chunks)
        ]

    def first_of(self, at):
        return pl.multiple_of(self.number(at), self.rows)

    def start_row(self, chunk):
        return self.number(self.count + self.members[chunk][0]) // self.chunk_depth * self.chunk_depth

    def within(self, at):
        return pl.multiple_of(self.number(at) % self.chunk_depth, self.rows)

    def held_copy(self, block, part, out, sem):
        here = self.held.at[part, pl.ds(block * self.rows, self.rows), :]
        there = self.out_ref.at[part, pl.ds(self.first_of(block), self.rows), :]
        return pltpu.make_async_copy(*((here, there) if out else (there, here)), sem)

    def start_right(self, chunk):
        for at in self.members[chunk]:
            row = at * self.rows if self.packed else self.within(self.count + at)
            for part in range(2):
                source, part_at = self.source_at[at][part]
                pltpu.make_async_copy(
                    self.source_refs[source].at[self.columns[at][1], part_at],
                    self.right.at[chunk, part, pl.ds(row, self.rows), :],
                    self.right_sem.at[chunk],
                ).start()

    def start_left(self, turn, chunk):
        sem = self.left_sem.at[turn, chunk]
        first, end = self.turns[turn]
        rows, base = self.rows, 0
        for ref, (_, blocks) in zip(self.packed_refs, self.packed):
            low, high = max(first, base), min(end, base + blocks)
            if low < high:
                pltpu.make_async_copy(
                    ref.at[:, pl.ds((low - base) * rows, (high - low) * rows), :],
                    self.left.at[chunk, :, pl.ds(low * rows, (high - low) * rows), :],
                    sem,
                ).start()
            base += blocks
        if self.packed:
            return
        inner = pl.ds(pl.multiple_of(self.start_row(chunk), self.chunk_depth), self.chunk_depth)
        for block in range(first, end):
            for part in range(2):
                candidates = 1 if self.choice is None else len(self.plane_bands) // 2
                for at in range(candidates):
                    for index, row, size in self.plane_bands[2 * (block + at) + part]:
                        copy = pltpu.make_async_copy(
                            self.plane_refs[index].at[:, inner],
                            self.left.at[chunk, part, pl.ds(block * rows + row, size), :],
                            sem,
                        )
                        if self.choice is None:
                            copy.start()
                        else:
                            pl.when(self.number(len(self.numbers()) - 1) == at)(copy.start)

    def steps(self):
        return [(self, turn, chunk) for turn in range(len(self.turns)) for chunk in range(self.chunks)]

    def start(self, turn, chunk):
        if turn == 0:
            self.start_right(chunk)
        self.start_left(turn, chunk)
        if self.packed:
            for block in range(*self.turns[turn]):
                for part in range(2):
                    self.held_copy(block, part, False, self.held_sem.at[turn]).start()

    def clear_absent(self, chunk):
        for at, (_, owner) in enumerate(self.absent):
            if owner == chunk:
                row = self.within(self.count + len(self.columns) + at)
                self.right[chunk, :, pl.ds(row, self.rows), :] = jnp.zeros(
                    (2, self.rows, TILE_SIZE), jnp.bfloat16
                )

    def wait(self, turn, chunk):
        first, end = self.turns[turn]
        height = (end - first) * self.rows
        views = [(self.left.at[chunk, :, pl.ds(0, height), :], self.left_sem.at[turn, chunk])]
        if turn == 0:
            rows = len(self.members[chunk]) * self.rows
            views.append((self.right.at[chunk, :, pl.ds(0, rows), :], self.right_sem.at[chunk]))
        if self.packed:
            views.append((self.held.at[:, pl.ds(0, height), :], self.held_sem.at[turn]))
        for view, sem in views:
            pltpu.make_async_copy(view, view, sem).wait()

    def mask(self, chunk, first, end):
        rows = self.rows
        for block in range(first, end):
            own_tile = self.number(block) // TILE_SIZE
            for offset in range(0, self.chunk_depth, TILE_SIZE):
                tile = (self.start_row(chunk) + offset) // TILE_SIZE

                @pl.when(self.used_ref[own_tile, tile] == 0)
                def _():
                    self.left[
                        chunk, :, block * rows : (block + 1) * rows, offset : offset + TILE_SIZE
                    ] = jnp.zeros((2, rows, TILE_SIZE), jnp.bfloat16)

    def write_packed(self, chunk, first, end):
        rows, (packing, sem) = self.rows, self.packing
        pack_at = self.count + len(self.columns) + len(self.absent)
        band = slice(first * rows, end * rows)
        for at, (_, owner) in enumerate(self.pack):
            if owner == chunk:
                to = slice(at * rows, (at + 1) * rows)
                packing[:, band, to] = self.left[chunk, :, band, pl.ds(self.within(pack_at + at), rows)]
                area = (slice(None), pl.ds(first * rows, (end - first) * rows), pl.ds(at * rows, rows))
                pltpu.make_async_copy(packing.at[area], self.pack_ref.at[area], sem).start()

    def products(self, chunk, band):
        by_part = ((0, 0, 1, 1), (0, 1, 1, 0))
        out = []
        for part, (a, b, c, d) in enumerate(by_part):
            first = jnp.dot(
                self.left[chunk, a, band], self.right[chunk, b], preferred_element_type=jnp.float32
            )
            second = jnp.dot(
                self.left[chunk, c, band], self.right[chunk, d], preferred_element_type=jnp.float32
            )
            out.append(first + second if part else first - second)
        return out

    def run(self, turn, chunk):
        rows, held = self.rows, self.held
        first, end = self.turns[turn]
        band = slice(first * rows, end * rows)
        if not self.packed:
            self.mask(chunk, first, end)
            if turn == 0:
                self.clear_absent(chunk)
        if self.pack:
            self.write_packed(chunk, first, end)
        sums = self.products(chunk, band)
        for part in range(2):
            if chunk == 0 and not self.packed:
                held[part, band] = sums[part]
            else:
                held[part, band] += sums[part]
            if chunk == self.chunks - 1:
                for block in range(first, end):
                    self.held_copy(block, part, True, self.held_sem.at[len(self.turns)]).start()

    def finish(self):
        if self.pack:
            pltpu.make_async_copy(self.packing[0], self.pack_ref, self.packing[1]).wait()
        pltpu.make_async_copy(self.held, self.held, self.held_sem.at[len(self.turns)]).wait()


def launch(device, base, jobs, used, span, total):
    plan = np.stack([n for job in jobs for n in job.numbers()], axis=1).astype(np.int32)
    operands = [array for job in jobs for array in job.operands()]
    operands += [] if base is None else [base]
    packing = [job for job in jobs if job.pack]
    scratch = [job.scratch(total) for job in jobs]
    out_shape = [jax.ShapeDtypeStruct((2, span, TILE_SIZE), jnp.float32)]
    for job in packing:
        shape = (2, job.count * job.rows, len(job.pack) * job.rows)
        out_shape.append(jax.ShapeDtypeStruct(shape, jnp.bfloat16))

    def kernel(device_ref, plan_ref, used_ref, *refs):
        outs = refs[len(operands) : len(operands) + len(out_shape)]
        spare = refs[len(operands) + len(out_shape) :]
        at, spare_at, plan_at = 0, 0, 0
        for job, shapes in zip(jobs, scratch):
            size = len(job.operands())
            job.bind(
                lambda n, plan_at=plan_at: plan_ref[device_ref[0], plan_at + n],
                used_ref,
                refs[at : at + size],
                outs[0],
                outs[1 + packing.index(job)] if job.pack else None,
                spare[spare_at : spare_at + len(shapes)],
                total,
            )
            at, spare_at, plan_at = at + size, spare_at + len(shapes), plan_at + len(job.numbers())
        steps = [step for job in jobs for step in job.steps()]
        for job, *step in steps[:AHEAD]:
            job.start(*step)
        for at, (job, *step) in enumerate(steps):
            job.wait(*step)
            for later, *later_step in steps[at + AHEAD : at + AHEAD + 1]:
                later.start(*later_step)
            job.run(*step)
        for job in jobs:
            job.finish()

    flops = sum(8 * job.count * job.rows * job.depth(total) * TILE_SIZE for job in jobs)
    return pl.pallas_call(
        kernel,
        out_shape=out_shape,
        grid_spec=pltpu.PrefetchScalarGridSpec(
            num_scalar_prefetch=3,
            grid=(1,),
            in_specs=[pl.BlockSpec(memory_space=pl.ANY)] * len(operands),
            out_specs=[pl.BlockSpec(memory_space=pl.ANY)] * len(out_shape),
            scratch_shapes=[shape for shapes in scratch for shape in shapes],
        ),
        input_output_aliases={} if base is None else {3 + len(operands) - 1: 0},
        cost_estimate=pl.CostEstimate(flops=flops, bytes_accessed=20 * span * total, transcendentals=0),
        compiler_params=pltpu.CompilerParams(vmem_limit_bytes=60 * 1024 * 1024),
    )(device, jnp.asarray(plan), used, *operands)


def used_tiles(aperture, lengths, rcv_index, total):
    lists = lax.dynamic_index_in_dim(aperture, rcv_index, 1, keepdims=False)
    slot = jnp.arange(lists.shape[1], dtype=jnp.int32)
    wanted = (slot[None, :] < lengths)[:, :, None]
    tiles = jnp.arange(total // TILE_SIZE, dtype=jnp.int32)
    return jnp.any(wanted & (lists[:, :, None] == tiles), axis=1).astype(jnp.int32)


def local(data, fill_mask, obliquity, aperture, lengths):
    _, rows, total = data.shape
    src_count = lax.axis_size("src")
    rcv_count = lax.axis_size("rcv")
    src_index = lax.axis_index("src")
    rcv_index = lax.axis_index("rcv")
    devices = src_count * rcv_count
    span = rows * rcv_count
    device = (src_index * rcv_count + rcv_index).reshape(1)
    phased = rows % 128 == 0 and rcv_count % 4 == 0 and rcv_count > 4

    order = ring_order(rcv_count)
    owner, mine = np.divmod(np.arange(devices), rcv_count)
    place = np.asarray([order.index(i) for i in range(rcv_count)])[mine]
    half = rcv_count // 2
    steps = (rcv_count - 1) // 2

    def origin(offset):
        return np.asarray(order)[(place + offset) % rcv_count]

    def here(numbers):
        return jnp.asarray(numbers, jnp.int32)[device[0]]

    forward = [(order[i], order[(i + 1) % rcv_count]) for i in range(rcv_count)]
    backward = [(b, a) for a, b in forward]

    def hop(planes, pairs):
        return tuple(lax.ppermute(p, "rcv", pairs) for p in planes)

    used = used_tiles(aperture, lengths, rcv_index, total)
    my_gains = -lax.dynamic_slice_in_dim(obliquity, src_index * span, span)
    gains = my_gains.reshape(rcv_count, rows, 1)

    def tiles_of(blocks, column):
        if phased:
            return cut(blocks, column, gains, device)
        out = []
        for planes, first in blocks:
            start = here(column) * TILE_SIZE
            cuts = [lax.dynamic_slice_in_dim(p, start, TILE_SIZE, 1) for p in planes]
            gain = lax.dynamic_index_in_dim(gains, here(first), 0, keepdims=True)
            out.append((jnp.stack(cuts).astype(jnp.float32) * gain).astype(jnp.bfloat16))
        return jnp.stack(out)

    columns = []

    def exchange(held):
        held_by = [(held, 0)]
        bit = src_count // 2
        while bit:
            swap = [(i, i ^ bit) for i in range(src_count)]
            held_by += [(lax.ppermute(x, "src", swap), mask ^ bit) for x, mask in held_by]
            bit //= 2
        return held_by

    def note(held_by, origins):
        for pieces, mask in held_by:
            for index, first in enumerate(origins):
                columns.append((pieces, index, (owner ^ mask) * span + first * rows, mask))

    def collect(blocks):
        tiles = tiles_of(blocks, mine)
        note(exchange(tiles), [first for _, first in blocks])

    blocks = transposed_blocks(data, devices)
    arrived = [
        lax.all_to_all(b, ("src", "rcv"), split_axis=0, concat_axis=0, tiled=True) for b in blocks
    ]
    own, ahead, behind = [], [], []
    for part in range(2):
        own.append(fill(data, fill_mask, arrived[part], part))
        ahead.append(lax.ppermute(own[part], "rcv", forward))
        behind.append(lax.ppermute(own[part], "rcv", backward))

    rows_of = {0: (own, origin(0)), -1: (ahead, origin(-1)), 1: (behind, origin(1))}
    far = origin(half)
    if not phased:
        collect([rows_of[0]])
        collect([rows_of[-1], rows_of[1]])
        for step in range(2, steps + 1):
            ahead, behind = hop(ahead, forward), hop(behind, backward)
            rows_of[-step], rows_of[step] = (ahead, origin(-step)), (behind, origin(step))
            collect([rows_of[-step], rows_of[step]])
        if rcv_count % 2 == 0:
            last = hop(ahead[:1], forward) + hop(behind[1:], backward)
            rows_of[half] = (last, far)
            collect([rows_of[half]])
        row_buffers, row_starts, pieces, starts = [], [], [], []
        for planes, first in rows_of.values():
            row_buffers += [(planes[0], 0), (planes[1], 1)]
            row_starts += [here(first * rows)] * 2
        for array, index, first, _ in columns:
            if index == 0:
                pieces.append(array)
            starts.append(here(first))
        return product(row_buffers, row_starts, pieces, starts, used, span, total)

    quarter = rcv_count // 4
    near = [quarter - 1, quarter, rcv_count - 1 - quarter, rcv_count - quarter]

    def from_mate(offset):
        pairs = []
        for i in near:
            mate = rcv_count - 1 - i
            if (mate + offset) % rcv_count == (i + half) % rcv_count:
                pairs.append((order[mate], order[i]))
        return pairs

    collect([rows_of[0]])
    inside = [0] + [o for step in range(1, steps) for o in (-step, step)]
    outside = [-steps, steps]

    def as_rows(offsets):
        return [(rows_of[o][0], rows_of[o][1] * rows) for o in offsets]

    for step in range(2, steps + 1):
        collect([rows_of[1 - step], rows_of[step - 1]])
        moved = []
        for part in range(2):
            moved.append(lax.ppermute(ahead[part], "rcv", forward))
            moved.append(lax.ppermute(behind[part], "rcv", backward))
        ahead, behind = moved[0::2], moved[1::2]
        rows_of[-step], rows_of[step] = (ahead, origin(-step)), (behind, origin(step))
    taken = [hop(rows_of[offset][0], from_mate(offset)) for offset in (-1, 1)]
    late_from = len(columns)
    collect([rows_of[-steps], rows_of[steps]])
    across = [(order[i], order[(i + half) % rcv_count]) for i in range(rcv_count)]
    far_pieces = cut([(own, origin(0))], far, gains, device)
    far_pieces = lax.ppermute(far_pieces, "rcv", across)
    note(exchange(far_pieces), [far])
    early, late = columns[:late_from], columns[late_from:]
    absent = pack = [(c[2], c[3]) for c in late]
    jobs = [Job(as_rows(inside), early, absent, pack=pack)]
    out, packed_inside = launch(device, None, jobs, used, span, total)
    turns = [
        [(order[(i + d) % rcv_count], order[i]) for i in range(rcv_count) if i not in near]
        for d in (-1, 1)
    ]
    last = []
    for part in range(2):
        upper = lax.ppermute(ahead[part][: rows // 2], "rcv", turns[0])
        lower = lax.ppermute(behind[part][rows // 2 :], "rcv", turns[1])
        last.append((upper, lower))
    jobs = [Job(as_rows(outside), early, absent, pack=pack)]
    out, packed_outside = launch(device, out, jobs, used, span, total)
    chosen = np.zeros(devices)
    for number, offset in enumerate((-1, 1), start=1):
        for _, target in from_mate(offset):
            chosen[mine == target] = number
    candidates = (*last, *taken[0], *taken[1])
    packed = [(packed_inside, len(inside)), (packed_outside, len(outside))]
    splits = [len(inside) // 2, len(inside)]
    near_rows = Job(as_rows(inside + outside), late, packed=packed, splits=splits)
    far_rows = Job([(candidates, far * rows)], columns, choice=chosen)
    return launch(device, out, [near_rows, far_rows], used, span, total)[0]


def solution(mesh):
    placed = (
        P(None, ("src", "rcv"), None),
        P(("src", "rcv"), None),
        P(),
        P("src", None, None),
        P("src", "rcv"),
    )

    return jax.shard_map(
        local, mesh=mesh, in_specs=placed, out_specs=P(None, "src", "rcv"), check_vma=False
    )
```

```python
import jax
import jax.numpy as jnp
import numpy as np
from jax import lax
from jax.experimental import pallas as pl
from jax.experimental.pallas import tpu as pltpu
from jax.sharding import PartitionSpec as P


TILE_SIZE = 512
AHEAD = 2


def ring_order(count):
    return list(range(0, count, 2)) + list(range(1, count, 2))[::-1]


def split_kernel(data_ref, *out_refs):
    rows = data_ref.shape[1]
    for part, out_ref in enumerate(out_refs):
        for block in range(out_ref.shape[0]):
            out_ref[block] = data_ref[part, :, block * rows : (block + 1) * rows].T


def transposed_blocks(data, devices):
    _, rows, _ = data.shape
    if rows % 128:
        return tuple(jnp.transpose(p.reshape(rows, devices, rows), (1, 0, 2)) for p in data)
    group = 8
    return pl.pallas_call(
        split_kernel,
        out_shape=(jax.ShapeDtypeStruct((devices, rows, rows), data.dtype),) * 2,
        grid=(devices // group,),
        in_specs=[pl.BlockSpec((2, rows, group * rows), lambda i: (0, 0, i))],
        out_specs=(pl.BlockSpec((group, rows, rows), lambda i: (i, 0, 0)),) * 2,
    )(data)


def fill_kernel(data_ref, mask_ref, arrived_ref, out_ref):
    rows = data_ref.shape[0]
    for block in range(arrived_ref.shape[0]):
        span = slice(block * rows, (block + 1) * rows)
        out_ref[:, span] = jnp.where(
            mask_ref[:, span] == 1, data_ref[:, span], arrived_ref[block]
        )


def fill(data, mask, arrived, part):
    _, rows, total = data.shape
    devices = arrived.shape[0]
    if rows % 128:
        transposed = jnp.transpose(arrived, (2, 0, 1)).reshape(rows, total)
        return jnp.where(mask == 1, data[part], transposed)
    group = 8
    return pl.pallas_call(
        fill_kernel,
        out_shape=jax.ShapeDtypeStruct((rows, total), data.dtype),
        grid=(devices // group,),
        in_specs=[
            pl.BlockSpec((None, rows, group * rows), lambda i: (part, 0, i)),
            pl.BlockSpec((rows, group * rows), lambda i: (0, i)),
            pl.BlockSpec((group, rows, rows), lambda i: (i, 0, 0)),
        ],
        out_specs=pl.BlockSpec((rows, group * rows), lambda i: (0, i)),
    )(data, mask, arrived)


def product_kernel(rows, plan_ref, used_ref, *refs):
    (row_refs, piece_refs), out_ref, scratch = refs[0], refs[1], refs[2:]
    left, right, row_sem, piece_sem = scratch
    inner_tiles = right.shape[0]
    out_tiles = out_ref.shape[1] // TILE_SIZE

    def piece_copies():
        copies = []
        at = len(row_refs)
        for ref in piece_refs:
            for index in range(ref.shape[0]):
                first = plan_ref[at]
                tile, offset = first // TILE_SIZE, first % TILE_SIZE
                for part in range(2):
                    row = pl.multiple_of(offset + (1 - part) * TILE_SIZE, rows)
                    copies.append(
                        pltpu.make_async_copy(
                            ref.at[index, part],
                            right.at[tile, pl.ds(row, rows), :],
                            piece_sem,
                        )
                    )
                at += 1
        return copies

    def start_rows(tile):
        for index, (ref, part) in enumerate(row_refs):
            row = pl.multiple_of(plan_ref[index], rows)
            column = pl.multiple_of(tile * 2 * TILE_SIZE + part * TILE_SIZE, TILE_SIZE)
            pltpu.make_async_copy(
                ref.at[:, pl.ds(pl.multiple_of(tile * TILE_SIZE, TILE_SIZE), TILE_SIZE)],
                left.at[pl.ds(row, rows), pl.ds(column, TILE_SIZE)],
                row_sem.at[tile],
            ).start()

    for copy in piece_copies():
        copy.start()

    @pl.loop(0, inner_tiles)
    def _(tile):
        start_rows(tile)

    out_ref[...] = jnp.zeros_like(out_ref)
    pltpu.make_async_copy(
        right.at[:, pl.ds(0, 2 * TILE_SIZE), :], right.at[:, pl.ds(0, 2 * TILE_SIZE), :], piece_sem
    ).wait()

    @pl.loop(0, inner_tiles)
    def _(tile):
        columns = pl.ds(pl.multiple_of(tile * 2 * TILE_SIZE, 2 * TILE_SIZE), 2 * TILE_SIZE)
        pltpu.make_async_copy(left.at[:, columns], left.at[:, columns], row_sem.at[tile]).wait()
        right[tile, 2 * TILE_SIZE :, :] = -right[tile, :TILE_SIZE, :]

        @pl.loop(0, out_tiles)
        def _(out_tile):
            @pl.when(used_ref[out_tile, tile] == 1)
            def _():
                span = pl.ds(pl.multiple_of(out_tile * TILE_SIZE, TILE_SIZE), TILE_SIZE)
                lhs = left[span, columns]
                for part in range(2):
                    rhs = right[tile, pl.ds((1 - part) * TILE_SIZE, 2 * TILE_SIZE), :]
                    out_ref[part, span, :] += jnp.dot(lhs, rhs, preferred_element_type=jnp.float32)


def product(row_buffers, row_starts, pieces, piece_starts, used, span, total):
    rows = row_buffers[0][0].shape[0]
    parts = [part for _, part in row_buffers]
    arrays = [array for array, _ in row_buffers] + list(pieces)
    plan = jnp.stack(row_starts + piece_starts).astype(jnp.int32)

    def kernel(plan_ref, used_ref, *refs):
        ins = refs[: len(arrays)]
        row_refs = list(zip(ins[: len(parts)], parts))
        product_kernel(
            rows, plan_ref, used_ref, (row_refs, ins[len(parts) :]), *refs[len(arrays) :]
        )

    inner_tiles = total // TILE_SIZE
    return pl.pallas_call(
        kernel,
        out_shape=jax.ShapeDtypeStruct((2, span, TILE_SIZE), jnp.float32),
        grid_spec=pltpu.PrefetchScalarGridSpec(
            num_scalar_prefetch=2,
            grid=(1,),
            in_specs=[pl.BlockSpec(memory_space=pl.ANY)] * len(arrays),
            out_specs=pl.BlockSpec((2, span, TILE_SIZE), lambda i, *_: (0, 0, 0), pipeline_mode=pl.Buffered(1)),
            scratch_shapes=[
                pltpu.VMEM((span, 2 * total), jnp.bfloat16),
                pltpu.VMEM((inner_tiles, 3 * TILE_SIZE, TILE_SIZE), jnp.bfloat16),
                pltpu.SemaphoreType.DMA((inner_tiles,)),
                pltpu.SemaphoreType.DMA,
            ],
        ),
        compiler_params=pltpu.CompilerParams(vmem_limit_bytes=67_000_000),
    )(plan, used, *arrays)


def cut_kernel(device_ref, place_ref, *refs):
    planes, out_ref = refs[:-1], refs[-1]
    for block in range(out_ref.shape[0]):
        first, second, gain = planes[3 * block : 3 * block + 3]
        for part, ref in enumerate((first, second)):
            out_ref[block, part] = (ref[...].astype(jnp.float32) * gain[...]).astype(jnp.bfloat16)


def cut(blocks, column, gains, device):
    rows = blocks[0][0][0].shape[0]
    place = np.stack([column] + [first for _, first in blocks], axis=1).astype(np.int32)
    specs, operands = [], []
    for index, (planes, _) in enumerate(blocks):
        specs += [pl.BlockSpec((rows, TILE_SIZE), lambda i, me, place: (0, place[me[0], 0]))] * 2
        specs.append(
            pl.BlockSpec((None, rows, 1), lambda i, me, place, at=index + 1: (place[me[0], at], 0, 0))
        )
        operands += [planes[0], planes[1], gains]
    shape = (len(blocks), 2, rows, TILE_SIZE)
    return pl.pallas_call(
        cut_kernel,
        out_shape=jax.ShapeDtypeStruct(shape, jnp.bfloat16),
        grid_spec=pltpu.PrefetchScalarGridSpec(
            num_scalar_prefetch=2,
            grid=(1,),
            in_specs=specs,
            out_specs=pl.BlockSpec(shape, lambda i, me, place: (0, 0, 0, 0)),
        ),
    )(device, jnp.asarray(place), *operands)


class Job:
    def __init__(self, row_blocks, columns, absent=(), choice=None, pack=(), packed=(), splits=()):
        self.row_blocks, self.columns, self.absent = row_blocks, columns, list(absent)
        self.choice, self.pack, self.packed = choice, list(pack), list(packed)
        self.planes = [] if packed else [p for planes, _ in row_blocks for p in planes]
        self.sources, self.source_at = [], []
        for pieces, *_ in columns:
            if not any(pieces is source for source in self.sources):
                self.sources.append(pieces)
            self.source_at.append([pieces is source for source in self.sources].index(True))
        self.rows = columns[0][0].shape[2]
        self.count = len(row_blocks)
        self.chunks = 1 if packed else 1 + max(column[3] for column in columns)
        bounds = [0, *splits, self.count]
        self.turns = list(zip(bounds[:-1], bounds[1:]))

    def numbers(self):
        listed = [first for _, first in self.row_blocks] + [column[2] for column in self.columns]
        listed += [first for first, _ in self.absent + self.pack]
        return listed + ([] if self.choice is None else [self.choice])

    def operands(self):
        return self.planes + self.sources + [array for array, _ in self.packed]

    def depth(self, total):
        return len(self.columns) * self.rows if self.packed else total

    def scratch(self, total):
        height, depth = self.count * self.rows, self.depth(total)
        shapes = [
            pltpu.VMEM((self.chunks, 2, height, depth // self.chunks), jnp.bfloat16),
            pltpu.VMEM((self.chunks, 2, depth // self.chunks, TILE_SIZE), jnp.bfloat16),
            pltpu.VMEM((2, height, TILE_SIZE), jnp.float32),
            pltpu.SemaphoreType.DMA((len(self.turns), self.chunks)),
            pltpu.SemaphoreType.DMA((self.chunks,)),
            pltpu.SemaphoreType.DMA((len(self.turns) + 1,)),
        ]
        if self.pack:
            shapes.append(pltpu.VMEM((2, height, len(self.pack) * self.rows), jnp.bfloat16))
            shapes.append(pltpu.SemaphoreType.DMA)
        return shapes

    def bind(self, number, used_ref, refs, out_ref, pack_ref, scratch, total):
        self.number, self.used_ref, self.out_ref, self.pack_ref = number, used_ref, out_ref, pack_ref
        self.plane_refs = refs[: len(self.planes)]
        self.source_refs = refs[len(self.planes) : len(self.planes) + len(self.sources)]
        self.packed_refs = refs[len(self.planes) + len(self.sources) :]
        self.left, self.right, self.held, self.left_sem, self.right_sem, self.held_sem = scratch[:6]
        self.packing = scratch[6:]
        self.chunk_depth = self.depth(total) // self.chunks
        self.members = [
            [at for at, column in enumerate(self.columns) if self.packed or column[3] == chunk]
            for chunk in range(self.chunks)
        ]

    def first_of(self, at):
        return pl.multiple_of(self.number(at), self.rows)

    def start_row(self, chunk):
        return self.number(self.count + self.members[chunk][0]) // self.chunk_depth * self.chunk_depth

    def within(self, at):
        return pl.multiple_of(self.number(at) % self.chunk_depth, self.rows)

    def held_copy(self, block, part, out, sem):
        here = self.held.at[part, pl.ds(block * self.rows, self.rows), :]
        there = self.out_ref.at[part, pl.ds(self.first_of(block), self.rows), :]
        return pltpu.make_async_copy(*((here, there) if out else (there, here)), sem)

    def start_right(self, chunk):
        for at in self.members[chunk]:
            row = at * self.rows if self.packed else self.within(self.count + at)
            for part in range(2):
                pltpu.make_async_copy(
                    self.source_refs[self.source_at[at]].at[self.columns[at][1], part],
                    self.right.at[chunk, part, pl.ds(row, self.rows), :],
                    self.right_sem.at[chunk],
                ).start()

    def start_left(self, turn, chunk):
        sem = self.left_sem.at[turn, chunk]
        first, end = self.turns[turn]
        rows, base = self.rows, 0
        for ref, (_, blocks) in zip(self.packed_refs, self.packed):
            low, high = max(first, base), min(end, base + blocks)
            if low < high:
                pltpu.make_async_copy(
                    ref.at[:, pl.ds((low - base) * rows, (high - low) * rows), :],
                    self.left.at[chunk, :, pl.ds(low * rows, (high - low) * rows), :],
                    sem,
                ).start()
            base += blocks
        if self.packed:
            return
        inner = pl.ds(pl.multiple_of(self.start_row(chunk), self.chunk_depth), self.chunk_depth)
        for block in range(first, end):
            for part in range(2):
                here = self.left.at[chunk, part, pl.ds(block * rows, rows), :]
                candidates = 1 if self.choice is None else len(self.planes) // 2
                for at in range(candidates):
                    ref = self.plane_refs[2 * (block + at) + part]
                    copy = pltpu.make_async_copy(ref.at[:, inner], here, sem)
                    if self.choice is None:
                        copy.start()
                    else:
                        pl.when(self.number(len(self.numbers()) - 1) == at)(copy.start)

    def steps(self):
        return [(self, turn, chunk) for turn in range(len(self.turns)) for chunk in range(self.chunks)]

    def start(self, turn, chunk):
        if turn == 0:
            self.start_right(chunk)
        self.start_left(turn, chunk)
        if self.packed:
            for block in range(*self.turns[turn]):
                for part in range(2):
                    self.held_copy(block, part, False, self.held_sem.at[turn]).start()

    def clear_absent(self, chunk):
        for at, (_, owner) in enumerate(self.absent):
            if owner == chunk:
                row = self.within(self.count + len(self.columns) + at)
                self.right[chunk, :, pl.ds(row, self.rows), :] = jnp.zeros(
                    (2, self.rows, TILE_SIZE), jnp.bfloat16
                )

    def wait(self, turn, chunk):
        first, end = self.turns[turn]
        height = (end - first) * self.rows
        views = [(self.left.at[chunk, :, pl.ds(0, height), :], self.left_sem.at[turn, chunk])]
        if turn == 0:
            rows = len(self.members[chunk]) * self.rows
            views.append((self.right.at[chunk, :, pl.ds(0, rows), :], self.right_sem.at[chunk]))
        if self.packed:
            views.append((self.held.at[:, pl.ds(0, height), :], self.held_sem.at[turn]))
        for view, sem in views:
            pltpu.make_async_copy(view, view, sem).wait()

    def mask(self, chunk, first, end):
        rows = self.rows
        for block in range(first, end):
            own_tile = self.number(block) // TILE_SIZE
            for offset in range(0, self.chunk_depth, TILE_SIZE):
                tile = (self.start_row(chunk) + offset) // TILE_SIZE

                @pl.when(self.used_ref[own_tile, tile] == 0)
                def _():
                    self.left[
                        chunk, :, block * rows : (block + 1) * rows, offset : offset + TILE_SIZE
                    ] = jnp.zeros((2, rows, TILE_SIZE), jnp.bfloat16)

    def write_packed(self, chunk, first, end):
        rows, (packing, sem) = self.rows, self.packing
        pack_at = self.count + len(self.columns) + len(self.absent)
        band = slice(first * rows, end * rows)
        for at, (_, owner) in enumerate(self.pack):
            if owner == chunk:
                to = slice(at * rows, (at + 1) * rows)
                packing[:, band, to] = self.left[chunk, :, band, pl.ds(self.within(pack_at + at), rows)]
                area = (slice(None), pl.ds(first * rows, (end - first) * rows), pl.ds(at * rows, rows))
                pltpu.make_async_copy(packing.at[area], self.pack_ref.at[area], sem).start()

    def products(self, chunk, band):
        by_part = ((0, 0, 1, 1), (0, 1, 1, 0))
        out = []
        for part, (a, b, c, d) in enumerate(by_part):
            first = jnp.dot(
                self.left[chunk, a, band], self.right[chunk, b], preferred_element_type=jnp.float32
            )
            second = jnp.dot(
                self.left[chunk, c, band], self.right[chunk, d], preferred_element_type=jnp.float32
            )
            out.append(first + second if part else first - second)
        return out

    def run(self, turn, chunk):
        rows, held = self.rows, self.held
        first, end = self.turns[turn]
        band = slice(first * rows, end * rows)
        if not self.packed:
            self.mask(chunk, first, end)
            if turn == 0:
                self.clear_absent(chunk)
        if self.pack:
            self.write_packed(chunk, first, end)
        sums = self.products(chunk, band)
        for part in range(2):
            if chunk == 0 and not self.packed:
                held[part, band] = sums[part]
            else:
                held[part, band] += sums[part]
            if chunk == self.chunks - 1:
                for block in range(first, end):
                    self.held_copy(block, part, True, self.held_sem.at[len(self.turns)]).start()

    def finish(self):
        if self.pack:
            pltpu.make_async_copy(self.packing[0], self.pack_ref, self.packing[1]).wait()
        pltpu.make_async_copy(self.held, self.held, self.held_sem.at[len(self.turns)]).wait()


def launch(device, base, jobs, used, span, total):
    plan = np.stack([n for job in jobs for n in job.numbers()], axis=1).astype(np.int32)
    operands = [array for job in jobs for array in job.operands()]
    operands += [] if base is None else [base]
    packing = [job for job in jobs if job.pack]
    scratch = [job.scratch(total) for job in jobs]
    out_shape = [jax.ShapeDtypeStruct((2, span, TILE_SIZE), jnp.float32)]
    for job in packing:
        shape = (2, job.count * job.rows, len(job.pack) * job.rows)
        out_shape.append(jax.ShapeDtypeStruct(shape, jnp.bfloat16))

    def kernel(device_ref, plan_ref, used_ref, *refs):
        outs = refs[len(operands) : len(operands) + len(out_shape)]
        spare = refs[len(operands) + len(out_shape) :]
        at, spare_at, plan_at = 0, 0, 0
        for job, shapes in zip(jobs, scratch):
            size = len(job.operands())
            job.bind(
                lambda n, plan_at=plan_at: plan_ref[device_ref[0], plan_at + n],
                used_ref,
                refs[at : at + size],
                outs[0],
                outs[1 + packing.index(job)] if job.pack else None,
                spare[spare_at : spare_at + len(shapes)],
                total,
            )
            at, spare_at, plan_at = at + size, spare_at + len(shapes), plan_at + len(job.numbers())
        steps = [step for job in jobs for step in job.steps()]
        for job, *step in steps[:AHEAD]:
            job.start(*step)
        for at, (job, *step) in enumerate(steps):
            job.wait(*step)
            for later, *later_step in steps[at + AHEAD : at + AHEAD + 1]:
                later.start(*later_step)
            job.run(*step)
        for job in jobs:
            job.finish()

    flops = sum(8 * job.count * job.rows * job.depth(total) * TILE_SIZE for job in jobs)
    return pl.pallas_call(
        kernel,
        out_shape=out_shape,
        grid_spec=pltpu.PrefetchScalarGridSpec(
            num_scalar_prefetch=3,
            grid=(1,),
            in_specs=[pl.BlockSpec(memory_space=pl.ANY)] * len(operands),
            out_specs=[pl.BlockSpec(memory_space=pl.ANY)] * len(out_shape),
            scratch_shapes=[shape for shapes in scratch for shape in shapes],
        ),
        input_output_aliases={} if base is None else {3 + len(operands) - 1: 0},
        cost_estimate=pl.CostEstimate(flops=flops, bytes_accessed=20 * span * total, transcendentals=0),
        compiler_params=pltpu.CompilerParams(vmem_limit_bytes=60 * 1024 * 1024),
    )(device, jnp.asarray(plan), used, *operands)


def used_tiles(aperture, lengths, rcv_index, total):
    lists = lax.dynamic_index_in_dim(aperture, rcv_index, 1, keepdims=False)
    slot = jnp.arange(lists.shape[1], dtype=jnp.int32)
    wanted = (slot[None, :] < lengths)[:, :, None]
    tiles = jnp.arange(total // TILE_SIZE, dtype=jnp.int32)
    return jnp.any(wanted & (lists[:, :, None] == tiles), axis=1).astype(jnp.int32)


def local(data, fill_mask, obliquity, aperture, lengths):
    _, rows, total = data.shape
    src_count = lax.axis_size("src")
    rcv_count = lax.axis_size("rcv")
    src_index = lax.axis_index("src")
    rcv_index = lax.axis_index("rcv")
    devices = src_count * rcv_count
    span = rows * rcv_count
    device = (src_index * rcv_count + rcv_index).reshape(1)
    phased = rows % 128 == 0 and rcv_count % 4 == 0 and rcv_count > 4

    order = ring_order(rcv_count)
    owner, mine = np.divmod(np.arange(devices), rcv_count)
    place = np.asarray([order.index(i) for i in range(rcv_count)])[mine]
    half = rcv_count // 2
    steps = (rcv_count - 1) // 2

    def origin(offset):
        return np.asarray(order)[(place + offset) % rcv_count]

    def here(numbers):
        return jnp.asarray(numbers, jnp.int32)[device[0]]

    forward = [(order[i], order[(i + 1) % rcv_count]) for i in range(rcv_count)]
    backward = [(b, a) for a, b in forward]

    def hop(planes, pairs):
        return tuple(lax.ppermute(p, "rcv", pairs) for p in planes)

    used = used_tiles(aperture, lengths, rcv_index, total)
    my_gains = -lax.dynamic_slice_in_dim(obliquity, src_index * span, span)
    gains = my_gains.reshape(rcv_count, rows, 1)

    def tiles_of(blocks, column):
        if phased:
            return cut(blocks, column, gains, device)
        out = []
        for planes, first in blocks:
            start = here(column) * TILE_SIZE
            cuts = [lax.dynamic_slice_in_dim(p, start, TILE_SIZE, 1) for p in planes]
            gain = lax.dynamic_index_in_dim(gains, here(first), 0, keepdims=True)
            out.append((jnp.stack(cuts).astype(jnp.float32) * gain).astype(jnp.bfloat16))
        return jnp.stack(out)

    columns = []

    def spread(held, origins):
        held_by = [(held, 0)]
        bit = src_count // 2
        while bit:
            swap = [(i, i ^ bit) for i in range(src_count)]
            held_by += [(lax.ppermute(x, "src", swap), mask ^ bit) for x, mask in held_by]
            bit //= 2
        for pieces, mask in held_by:
            for index, first in enumerate(origins):
                columns.append((pieces, index, (owner ^ mask) * span + first * rows, mask))

    def collect(blocks):
        tiles = tiles_of(blocks, mine)
        spread(tiles, [first for _, first in blocks])

    blocks = transposed_blocks(data, devices)
    arrived = [
        lax.all_to_all(b, ("src", "rcv"), split_axis=0, concat_axis=0, tiled=True) for b in blocks
    ]
    own, ahead, behind = [], [], []
    for part in range(2):
        own.append(fill(data, fill_mask, arrived[part], part))
        ahead.append(lax.ppermute(own[part], "rcv", forward))
        behind.append(lax.ppermute(own[part], "rcv", backward))

    rows_of = {0: (own, origin(0)), -1: (ahead, origin(-1)), 1: (behind, origin(1))}
    far = origin(half)
    if not phased:
        collect([rows_of[0]])
        collect([rows_of[-1], rows_of[1]])
        for step in range(2, steps + 1):
            ahead, behind = hop(ahead, forward), hop(behind, backward)
            rows_of[-step], rows_of[step] = (ahead, origin(-step)), (behind, origin(step))
            collect([rows_of[-step], rows_of[step]])
        if rcv_count % 2 == 0:
            last = hop(ahead[:1], forward) + hop(behind[1:], backward)
            rows_of[half] = (last, far)
            collect([rows_of[half]])
        row_buffers, row_starts, pieces, starts = [], [], [], []
        for planes, first in rows_of.values():
            row_buffers += [(planes[0], 0), (planes[1], 1)]
            row_starts += [here(first * rows)] * 2
        for array, index, first, _ in columns:
            if index == 0:
                pieces.append(array)
            starts.append(here(first))
        return product(row_buffers, row_starts, pieces, starts, used, span, total)

    quarter = rcv_count // 4
    near = [quarter - 1, quarter, rcv_count - 1 - quarter, rcv_count - quarter]

    def from_mate(offset):
        pairs = []
        for i in near:
            mate = rcv_count - 1 - i
            if (mate + offset) % rcv_count == (i + half) % rcv_count:
                pairs.append((order[mate], order[i]))
        return pairs

    collect([rows_of[0]])
    inside = [0] + [o for step in range(1, steps) for o in (-step, step)]
    outside = [-steps, steps]

    def as_rows(offsets):
        return [(rows_of[o][0], rows_of[o][1] * rows) for o in offsets]

    for step in range(2, steps + 1):
        collect([rows_of[1 - step], rows_of[step - 1]])
        moved = []
        for part in range(2):
            moved.append(lax.ppermute(ahead[part], "rcv", forward))
            moved.append(lax.ppermute(behind[part], "rcv", backward))
        ahead, behind = moved[0::2], moved[1::2]
        rows_of[-step], rows_of[step] = (ahead, origin(-step)), (behind, origin(step))
    taken = [hop(rows_of[offset][0], from_mate(offset)) for offset in (-1, 1)]
    late_from = len(columns)
    collect([rows_of[-steps], rows_of[steps]])
    across = [(order[i], order[(i + half) % rcv_count]) for i in range(rcv_count)]
    far_pieces = cut([(own, origin(0))], far, gains, device)
    far_pieces = lax.ppermute(far_pieces, "rcv", across)
    spread(far_pieces, [far])
    early, late = columns[:late_from], columns[late_from:]
    absent = pack = [(c[2], c[3]) for c in late]
    jobs = [Job(as_rows(inside), early, absent, pack=pack)]
    out, packed_inside = launch(device, None, jobs, used, span, total)
    turns = [
        [(order[(i + d) % rcv_count], order[i]) for i in range(rcv_count) if i not in near]
        for d in (-1, 1)
    ]
    last = []
    for part, plane in enumerate((ahead[0], behind[1])):
        last.append(lax.ppermute(plane, "rcv", turns[part]))
    jobs = [Job(as_rows(outside), early, absent, pack=pack)]
    out, packed_outside = launch(device, out, jobs, used, span, total)
    chosen = np.zeros(devices)
    for number, offset in enumerate((-1, 1), start=1):
        for _, target in from_mate(offset):
            chosen[mine == target] = number
    candidates = (*last, *taken[0], *taken[1])
    packed = [(packed_inside, len(inside)), (packed_outside, len(outside))]
    splits = [len(inside) // 2, len(inside)]
    jobs = [Job(as_rows(inside + outside), late, packed=packed, splits=splits)]
    out = launch(device, out, jobs, used, span, total)[0]
    jobs = [Job([(candidates, far * rows)], columns, choice=chosen)]
    return launch(device, out, jobs, used, span, total)[0]


def solution(mesh):
    placed = (
        P(None, ("src", "rcv"), None),
        P(("src", "rcv"), None),
        P(),
        P("src", None, None),
        P("src", "rcv"),
    )

    return jax.shard_map(
        local, mesh=mesh, in_specs=placed, out_specs=P(None, "src", "rcv"), check_vma=False
    )
```

```python
import jax
import jax.numpy as jnp
import numpy as np
from jax import lax
from jax.experimental import pallas as pl
from jax.experimental.pallas import tpu as pltpu
from jax.sharding import PartitionSpec as P


TILE_SIZE = 512
AHEAD = 2


def ring_order(count):
    return list(range(0, count, 2)) + list(range(1, count, 2))[::-1]


def split_kernel(data_ref, *out_refs):
    rows = data_ref.shape[1]
    for part, out_ref in enumerate(out_refs):
        for block in range(out_ref.shape[0]):
            out_ref[block] = data_ref[part, :, block * rows : (block + 1) * rows].T


def transposed_blocks(data, devices):
    _, rows, _ = data.shape
    if rows % 128:
        return tuple(jnp.transpose(p.reshape(rows, devices, rows), (1, 0, 2)) for p in data)
    group = 8
    return pl.pallas_call(
        split_kernel,
        out_shape=(jax.ShapeDtypeStruct((devices, rows, rows), data.dtype),) * 2,
        grid=(devices // group,),
        in_specs=[pl.BlockSpec((2, rows, group * rows), lambda i: (0, 0, i))],
        out_specs=(pl.BlockSpec((group, rows, rows), lambda i: (i, 0, 0)),) * 2,
    )(data)


def fill_kernel(data_ref, mask_ref, arrived_ref, out_ref):
    rows = data_ref.shape[0]
    for block in range(arrived_ref.shape[0]):
        span = slice(block * rows, (block + 1) * rows)
        out_ref[:, span] = jnp.where(
            mask_ref[:, span] == 1, data_ref[:, span], arrived_ref[block]
        )


def fill(data, mask, arrived, part):
    _, rows, total = data.shape
    devices = arrived.shape[0]
    if rows % 128:
        transposed = jnp.transpose(arrived, (2, 0, 1)).reshape(rows, total)
        return jnp.where(mask == 1, data[part], transposed)
    group = 8
    return pl.pallas_call(
        fill_kernel,
        out_shape=jax.ShapeDtypeStruct((rows, total), data.dtype),
        grid=(devices // group,),
        in_specs=[
            pl.BlockSpec((None, rows, group * rows), lambda i: (part, 0, i)),
            pl.BlockSpec((rows, group * rows), lambda i: (0, i)),
            pl.BlockSpec((group, rows, rows), lambda i: (i, 0, 0)),
        ],
        out_specs=pl.BlockSpec((rows, group * rows), lambda i: (0, i)),
    )(data, mask, arrived)


def product_kernel(rows, plan_ref, used_ref, *refs):
    (row_refs, piece_refs), out_ref, scratch = refs[0], refs[1], refs[2:]
    left, right, row_sem, piece_sem = scratch
    inner_tiles = right.shape[0]
    out_tiles = out_ref.shape[1] // TILE_SIZE

    def piece_copies():
        copies = []
        at = len(row_refs)
        for ref in piece_refs:
            for index in range(ref.shape[0]):
                first = plan_ref[at]
                tile, offset = first // TILE_SIZE, first % TILE_SIZE
                for part in range(2):
                    row = pl.multiple_of(offset + (1 - part) * TILE_SIZE, rows)
                    copies.append(
                        pltpu.make_async_copy(
                            ref.at[index, part],
                            right.at[tile, pl.ds(row, rows), :],
                            piece_sem,
                        )
                    )
                at += 1
        return copies

    def start_rows(tile):
        for index, (ref, part) in enumerate(row_refs):
            row = pl.multiple_of(plan_ref[index], rows)
            column = pl.multiple_of(tile * 2 * TILE_SIZE + part * TILE_SIZE, TILE_SIZE)
            pltpu.make_async_copy(
                ref.at[:, pl.ds(pl.multiple_of(tile * TILE_SIZE, TILE_SIZE), TILE_SIZE)],
                left.at[pl.ds(row, rows), pl.ds(column, TILE_SIZE)],
                row_sem.at[tile],
            ).start()

    for copy in piece_copies():
        copy.start()

    @pl.loop(0, inner_tiles)
    def _(tile):
        start_rows(tile)

    out_ref[...] = jnp.zeros_like(out_ref)
    pltpu.make_async_copy(
        right.at[:, pl.ds(0, 2 * TILE_SIZE), :], right.at[:, pl.ds(0, 2 * TILE_SIZE), :], piece_sem
    ).wait()

    @pl.loop(0, inner_tiles)
    def _(tile):
        columns = pl.ds(pl.multiple_of(tile * 2 * TILE_SIZE, 2 * TILE_SIZE), 2 * TILE_SIZE)
        pltpu.make_async_copy(left.at[:, columns], left.at[:, columns], row_sem.at[tile]).wait()
        right[tile, 2 * TILE_SIZE :, :] = -right[tile, :TILE_SIZE, :]

        @pl.loop(0, out_tiles)
        def _(out_tile):
            @pl.when(used_ref[out_tile, tile] == 1)
            def _():
                span = pl.ds(pl.multiple_of(out_tile * TILE_SIZE, TILE_SIZE), TILE_SIZE)
                lhs = left[span, columns]
                for part in range(2):
                    rhs = right[tile, pl.ds((1 - part) * TILE_SIZE, 2 * TILE_SIZE), :]
                    out_ref[part, span, :] += jnp.dot(lhs, rhs, preferred_element_type=jnp.float32)


def product(row_buffers, row_starts, pieces, piece_starts, used, span, total):
    rows = row_buffers[0][0].shape[0]
    parts = [part for _, part in row_buffers]
    arrays = [array for array, _ in row_buffers] + list(pieces)
    plan = jnp.stack(row_starts + piece_starts).astype(jnp.int32)

    def kernel(plan_ref, used_ref, *refs):
        ins = refs[: len(arrays)]
        row_refs = list(zip(ins[: len(parts)], parts))
        product_kernel(
            rows, plan_ref, used_ref, (row_refs, ins[len(parts) :]), *refs[len(arrays) :]
        )

    inner_tiles = total // TILE_SIZE
    return pl.pallas_call(
        kernel,
        out_shape=jax.ShapeDtypeStruct((2, span, TILE_SIZE), jnp.float32),
        grid_spec=pltpu.PrefetchScalarGridSpec(
            num_scalar_prefetch=2,
            grid=(1,),
            in_specs=[pl.BlockSpec(memory_space=pl.ANY)] * len(arrays),
            out_specs=pl.BlockSpec((2, span, TILE_SIZE), lambda i, *_: (0, 0, 0), pipeline_mode=pl.Buffered(1)),
            scratch_shapes=[
                pltpu.VMEM((span, 2 * total), jnp.bfloat16),
                pltpu.VMEM((inner_tiles, 3 * TILE_SIZE, TILE_SIZE), jnp.bfloat16),
                pltpu.SemaphoreType.DMA((inner_tiles,)),
                pltpu.SemaphoreType.DMA,
            ],
        ),
        compiler_params=pltpu.CompilerParams(vmem_limit_bytes=67_000_000),
    )(plan, used, *arrays)


def cut_kernel(device_ref, place_ref, *refs):
    ins, out_ref = refs[:-1], refs[-1]
    blocks, parts = out_ref.shape[:2]
    for block in range(blocks):
        *planes, gain = ins[(parts + 1) * block : (parts + 1) * (block + 1)]
        for part, ref in enumerate(planes):
            out_ref[block, part] = (ref[...].astype(jnp.float32) * gain[...]).astype(jnp.bfloat16)


def cut(blocks, column, gains, device, parts=(0, 1)):
    rows = blocks[0][0][0].shape[0]
    place = np.stack([column] + [first for _, first in blocks], axis=1).astype(np.int32)
    specs, operands = [], []
    for index, (planes, _) in enumerate(blocks):
        spec = pl.BlockSpec((rows, TILE_SIZE), lambda i, me, place: (0, place[me[0], 0]))
        specs += [spec] * len(parts)
        specs.append(
            pl.BlockSpec((None, rows, 1), lambda i, me, place, at=index + 1: (place[me[0], at], 0, 0))
        )
        operands += [*(planes[part] for part in parts), gains]
    shape = (len(blocks), len(parts), rows, TILE_SIZE)
    return pl.pallas_call(
        cut_kernel,
        out_shape=jax.ShapeDtypeStruct(shape, jnp.bfloat16),
        grid_spec=pltpu.PrefetchScalarGridSpec(
            num_scalar_prefetch=2,
            grid=(1,),
            in_specs=specs,
            out_specs=pl.BlockSpec(shape, lambda i, me, place: (0, 0, 0, 0)),
        ),
    )(device, jnp.asarray(place), *operands)


class Job:
    def __init__(self, row_blocks, columns, absent=(), choice=None, pack=(), packed=(), splits=()):
        self.row_blocks, self.columns, self.absent = row_blocks, columns, list(absent)
        self.choice, self.pack, self.packed = choice, list(pack), list(packed)
        self.planes, self.plane_bands = [], []
        for plane in [] if packed else [p for planes, _ in row_blocks for p in planes]:
            self.plane_bands.append([])
            row = 0
            for array in plane if isinstance(plane, tuple) else (plane,):
                self.plane_bands[-1].append((len(self.planes), row, array.shape[0]))
                self.planes.append(array)
                row += array.shape[0]
        self.sources, self.source_at = [], []
        for pieces, *_ in columns:
            apart = isinstance(pieces, tuple)
            spots = []
            for part, array in enumerate(pieces if apart else (pieces, pieces)):
                if not any(array is source for source in self.sources):
                    self.sources.append(array)
                spots.append(([array is source for source in self.sources].index(True), 0 if apart else part))
            self.source_at.append(spots)
        self.rows = self.sources[0].shape[2]
        self.count = len(row_blocks)
        self.chunks = 1 if packed else 1 + max(column[3] for column in columns)
        bounds = [0, *splits, self.count]
        self.turns = list(zip(bounds[:-1], bounds[1:]))

    def numbers(self):
        listed = [first for _, first in self.row_blocks] + [column[2] for column in self.columns]
        listed += [first for first, _ in self.absent + self.pack]
        return listed + ([] if self.choice is None else [self.choice])

    def operands(self):
        return self.planes + self.sources + [array for array, _ in self.packed]

    def depth(self, total):
        return len(self.columns) * self.rows if self.packed else total

    def scratch(self, total):
        height, depth = self.count * self.rows, self.depth(total)
        shapes = [
            pltpu.VMEM((self.chunks, 2, height, depth // self.chunks), jnp.bfloat16),
            pltpu.VMEM((self.chunks, 2, depth // self.chunks, TILE_SIZE), jnp.bfloat16),
            pltpu.VMEM((2, height, TILE_SIZE), jnp.float32),
            pltpu.SemaphoreType.DMA((len(self.turns), self.chunks)),
            pltpu.SemaphoreType.DMA((self.chunks,)),
            pltpu.SemaphoreType.DMA((len(self.turns) + 1,)),
        ]
        if self.pack:
            shapes.append(pltpu.VMEM((2, height, len(self.pack) * self.rows), jnp.bfloat16))
            shapes.append(pltpu.SemaphoreType.DMA)
        return shapes

    def bind(self, number, used_ref, refs, out_ref, pack_ref, scratch, total):
        self.number, self.used_ref, self.out_ref, self.pack_ref = number, used_ref, out_ref, pack_ref
        self.plane_refs = refs[: len(self.planes)]
        self.source_refs = refs[len(self.planes) : len(self.planes) + len(self.sources)]
        self.packed_refs = refs[len(self.planes) + len(self.sources) :]
        self.left, self.right, self.held, self.left_sem, self.right_sem, self.held_sem = scratch[:6]
        self.packing = scratch[6:]
        self.chunk_depth = self.depth(total) // self.chunks
        self.members = [
            [at for at, column in enumerate(self.columns) if self.packed or column[3] == chunk]
            for chunk in range(self.chunks)
        ]

    def first_of(self, at):
        return pl.multiple_of(self.number(at), self.rows)

    def start_row(self, chunk):
        return self.number(self.count + self.members[chunk][0]) // self.chunk_depth * self.chunk_depth

    def within(self, at):
        return pl.multiple_of(self.number(at) % self.chunk_depth, self.rows)

    def held_copy(self, block, part, out, sem):
        here = self.held.at[part, pl.ds(block * self.rows, self.rows), :]
        there = self.out_ref.at[part, pl.ds(self.first_of(block), self.rows), :]
        return pltpu.make_async_copy(*((here, there) if out else (there, here)), sem)

    def start_right(self, chunk):
        for at in self.members[chunk]:
            row = at * self.rows if self.packed else self.within(self.count + at)
            for part in range(2):
                source, part_at = self.source_at[at][part]
                pltpu.make_async_copy(
                    self.source_refs[source].at[self.columns[at][1], part_at],
                    self.right.at[chunk, part, pl.ds(row, self.rows), :],
                    self.right_sem.at[chunk],
                ).start()

    def start_left(self, turn, chunk):
        sem = self.left_sem.at[turn, chunk]
        first, end = self.turns[turn]
        rows, base = self.rows, 0
        for ref, (_, blocks) in zip(self.packed_refs, self.packed):
            low, high = max(first, base), min(end, base + blocks)
            if low < high:
                pltpu.make_async_copy(
                    ref.at[:, pl.ds((low - base) * rows, (high - low) * rows), :],
                    self.left.at[chunk, :, pl.ds(low * rows, (high - low) * rows), :],
                    sem,
                ).start()
            base += blocks
        if self.packed:
            return
        inner = pl.ds(pl.multiple_of(self.start_row(chunk), self.chunk_depth), self.chunk_depth)
        for block in range(first, end):
            for part in range(2):
                candidates = 1 if self.choice is None else len(self.plane_bands) // 2
                for at in range(candidates):
                    for index, row, size in self.plane_bands[2 * (block + at) + part]:
                        copy = pltpu.make_async_copy(
                            self.plane_refs[index].at[:, inner],
                            self.left.at[chunk, part, pl.ds(block * rows + row, size), :],
                            sem,
                        )
                        if self.choice is None:
                            copy.start()
                        else:
                            pl.when(self.number(len(self.numbers()) - 1) == at)(copy.start)

    def steps(self):
        return [(self, turn, chunk) for turn in range(len(self.turns)) for chunk in range(self.chunks)]

    def start(self, turn, chunk):
        if turn == 0:
            self.start_right(chunk)
        self.start_left(turn, chunk)
        if self.packed:
            for block in range(*self.turns[turn]):
                for part in range(2):
                    self.held_copy(block, part, False, self.held_sem.at[turn]).start()

    def clear_absent(self, chunk):
        for at, (_, owner) in enumerate(self.absent):
            if owner == chunk:
                row = self.within(self.count + len(self.columns) + at)
                self.right[chunk, :, pl.ds(row, self.rows), :] = jnp.zeros(
                    (2, self.rows, TILE_SIZE), jnp.bfloat16
                )

    def wait(self, turn, chunk):
        first, end = self.turns[turn]
        height = (end - first) * self.rows
        views = [(self.left.at[chunk, :, pl.ds(0, height), :], self.left_sem.at[turn, chunk])]
        if turn == 0:
            rows = len(self.members[chunk]) * self.rows
            views.append((self.right.at[chunk, :, pl.ds(0, rows), :], self.right_sem.at[chunk]))
        if self.packed:
            views.append((self.held.at[:, pl.ds(0, height), :], self.held_sem.at[turn]))
        for view, sem in views:
            pltpu.make_async_copy(view, view, sem).wait()

    def mask(self, chunk, first, end):
        rows = self.rows
        for block in range(first, end):
            own_tile = self.number(block) // TILE_SIZE
            for offset in range(0, self.chunk_depth, TILE_SIZE):
                tile = (self.start_row(chunk) + offset) // TILE_SIZE

                @pl.when(self.used_ref[own_tile, tile] == 0)
                def _():
                    self.left[
                        chunk, :, block * rows : (block + 1) * rows, offset : offset + TILE_SIZE
                    ] = jnp.zeros((2, rows, TILE_SIZE), jnp.bfloat16)

    def write_packed(self, chunk, first, end):
        rows, (packing, sem) = self.rows, self.packing
        pack_at = self.count + len(self.columns) + len(self.absent)
        band = slice(first * rows, end * rows)
        for at, (_, owner) in enumerate(self.pack):
            if owner == chunk:
                to = slice(at * rows, (at + 1) * rows)
                packing[:, band, to] = self.left[chunk, :, band, pl.ds(self.within(pack_at + at), rows)]
                area = (slice(None), pl.ds(first * rows, (end - first) * rows), pl.ds(at * rows, rows))
                pltpu.make_async_copy(packing.at[area], self.pack_ref.at[area], sem).start()

    def products(self, chunk, band):
        by_part = ((0, 0, 1, 1), (0, 1, 1, 0))
        out = []
        for part, (a, b, c, d) in enumerate(by_part):
            first = jnp.dot(
                self.left[chunk, a, band], self.right[chunk, b], preferred_element_type=jnp.float32
            )
            second = jnp.dot(
                self.left[chunk, c, band], self.right[chunk, d], preferred_element_type=jnp.float32
            )
            out.append(first + second if part else first - second)
        return out

    def run(self, turn, chunk):
        rows, held = self.rows, self.held
        first, end = self.turns[turn]
        band = slice(first * rows, end * rows)
        if not self.packed:
            self.mask(chunk, first, end)
            if turn == 0:
                self.clear_absent(chunk)
        if self.pack:
            self.write_packed(chunk, first, end)
        sums = self.products(chunk, band)
        for part in range(2):
            if chunk == 0 and not self.packed:
                held[part, band] = sums[part]
            else:
                held[part, band] += sums[part]
            if chunk == self.chunks - 1:
                for block in range(first, end):
                    self.held_copy(block, part, True, self.held_sem.at[len(self.turns)]).start()

    def finish(self):
        if self.pack:
            pltpu.make_async_copy(self.packing[0], self.pack_ref, self.packing[1]).wait()
        pltpu.make_async_copy(self.held, self.held, self.held_sem.at[len(self.turns)]).wait()


def launch(device, base, jobs, used, span, total):
    plan = np.stack([n for job in jobs for n in job.numbers()], axis=1).astype(np.int32)
    operands = [array for job in jobs for array in job.operands()]
    operands += [] if base is None else [base]
    packing = [job for job in jobs if job.pack]
    scratch = [job.scratch(total) for job in jobs]
    out_shape = [jax.ShapeDtypeStruct((2, span, TILE_SIZE), jnp.float32)]
    for job in packing:
        shape = (2, job.count * job.rows, len(job.pack) * job.rows)
        out_shape.append(jax.ShapeDtypeStruct(shape, jnp.bfloat16))

    def kernel(device_ref, plan_ref, used_ref, *refs):
        outs = refs[len(operands) : len(operands) + len(out_shape)]
        spare = refs[len(operands) + len(out_shape) :]
        at, spare_at, plan_at = 0, 0, 0
        for job, shapes in zip(jobs, scratch):
            size = len(job.operands())
            job.bind(
                lambda n, plan_at=plan_at: plan_ref[device_ref[0], plan_at + n],
                used_ref,
                refs[at : at + size],
                outs[0],
                outs[1 + packing.index(job)] if job.pack else None,
                spare[spare_at : spare_at + len(shapes)],
                total,
            )
            at, spare_at, plan_at = at + size, spare_at + len(shapes), plan_at + len(job.numbers())
        steps = [step for job in jobs for step in job.steps()]
        for job, *step in steps[:AHEAD]:
            job.start(*step)
        for at, (job, *step) in enumerate(steps):
            job.wait(*step)
            for later, *later_step in steps[at + AHEAD : at + AHEAD + 1]:
                later.start(*later_step)
            job.run(*step)
        for job in jobs:
            job.finish()

    flops = sum(8 * job.count * job.rows * job.depth(total) * TILE_SIZE for job in jobs)
    return pl.pallas_call(
        kernel,
        out_shape=out_shape,
        grid_spec=pltpu.PrefetchScalarGridSpec(
            num_scalar_prefetch=3,
            grid=(1,),
            in_specs=[pl.BlockSpec(memory_space=pl.ANY)] * len(operands),
            out_specs=[pl.BlockSpec(memory_space=pl.ANY)] * len(out_shape),
            scratch_shapes=[shape for shapes in scratch for shape in shapes],
        ),
        input_output_aliases={} if base is None else {3 + len(operands) - 1: 0},
        cost_estimate=pl.CostEstimate(flops=flops, bytes_accessed=20 * span * total, transcendentals=0),
        compiler_params=pltpu.CompilerParams(vmem_limit_bytes=60 * 1024 * 1024),
    )(device, jnp.asarray(plan), used, *operands)


def used_tiles(aperture, lengths, rcv_index, total):
    lists = lax.dynamic_index_in_dim(aperture, rcv_index, 1, keepdims=False)
    slot = jnp.arange(lists.shape[1], dtype=jnp.int32)
    wanted = (slot[None, :] < lengths)[:, :, None]
    tiles = jnp.arange(total // TILE_SIZE, dtype=jnp.int32)
    return jnp.any(wanted & (lists[:, :, None] == tiles), axis=1).astype(jnp.int32)


def local(data, fill_mask, obliquity, aperture, lengths):
    _, rows, total = data.shape
    src_count = lax.axis_size("src")
    rcv_count = lax.axis_size("rcv")
    src_index = lax.axis_index("src")
    rcv_index = lax.axis_index("rcv")
    devices = src_count * rcv_count
    span = rows * rcv_count
    device = (src_index * rcv_count + rcv_index).reshape(1)
    phased = rows % 128 == 0 and rcv_count % 4 == 0 and rcv_count > 4

    order = ring_order(rcv_count)
    owner, mine = np.divmod(np.arange(devices), rcv_count)
    place = np.asarray([order.index(i) for i in range(rcv_count)])[mine]
    half = rcv_count // 2
    steps = (rcv_count - 1) // 2

    def origin(offset):
        return np.asarray(order)[(place + offset) % rcv_count]

    def here(numbers):
        return jnp.asarray(numbers, jnp.int32)[device[0]]

    forward = [(order[i], order[(i + 1) % rcv_count]) for i in range(rcv_count)]
    backward = [(b, a) for a, b in forward]

    def hop(planes, pairs):
        return tuple(lax.ppermute(p, "rcv", pairs) for p in planes)

    used = used_tiles(aperture, lengths, rcv_index, total)
    my_gains = -lax.dynamic_slice_in_dim(obliquity, src_index * span, span)
    gains = my_gains.reshape(rcv_count, rows, 1)

    def tiles_of(blocks, column):
        if phased:
            return cut(blocks, column, gains, device)
        out = []
        for planes, first in blocks:
            start = here(column) * TILE_SIZE
            cuts = [lax.dynamic_slice_in_dim(p, start, TILE_SIZE, 1) for p in planes]
            gain = lax.dynamic_index_in_dim(gains, here(first), 0, keepdims=True)
            out.append((jnp.stack(cuts).astype(jnp.float32) * gain).astype(jnp.bfloat16))
        return jnp.stack(out)

    columns = []

    def exchange(held):
        held_by = [(held, 0)]
        bit = src_count // 2
        while bit:
            swap = [(i, i ^ bit) for i in range(src_count)]
            held_by += [(lax.ppermute(x, "src", swap), mask ^ bit) for x, mask in held_by]
            bit //= 2
        return held_by

    def note(held_by, origins):
        for pieces, mask in held_by:
            for index, first in enumerate(origins):
                columns.append((pieces, index, (owner ^ mask) * span + first * rows, mask))

    def collect(blocks):
        tiles = tiles_of(blocks, mine)
        note(exchange(tiles), [first for _, first in blocks])

    blocks = transposed_blocks(data, devices)
    arrived = [
        lax.all_to_all(b, ("src", "rcv"), split_axis=0, concat_axis=0, tiled=True) for b in blocks
    ]
    own, ahead, behind = [], [], []
    for part in range(2):
        own.append(fill(data, fill_mask, arrived[part], part))
        ahead.append(lax.ppermute(own[part], "rcv", forward))
        behind.append(lax.ppermute(own[part], "rcv", backward))

    rows_of = {0: (own, origin(0)), -1: (ahead, origin(-1)), 1: (behind, origin(1))}
    far = origin(half)
    if not phased:
        collect([rows_of[0]])
        collect([rows_of[-1], rows_of[1]])
        for step in range(2, steps + 1):
            ahead, behind = hop(ahead, forward), hop(behind, backward)
            rows_of[-step], rows_of[step] = (ahead, origin(-step)), (behind, origin(step))
            collect([rows_of[-step], rows_of[step]])
        if rcv_count % 2 == 0:
            last = hop(ahead[:1], forward) + hop(behind[1:], backward)
            rows_of[half] = (last, far)
            collect([rows_of[half]])
        row_buffers, row_starts, pieces, starts = [], [], [], []
        for planes, first in rows_of.values():
            row_buffers += [(planes[0], 0), (planes[1], 1)]
            row_starts += [here(first * rows)] * 2
        for array, index, first, _ in columns:
            if index == 0:
                pieces.append(array)
            starts.append(here(first))
        return product(row_buffers, row_starts, pieces, starts, used, span, total)

    quarter = rcv_count // 4
    near = [quarter - 1, quarter, rcv_count - 1 - quarter, rcv_count - quarter]

    def from_mate(offset):
        pairs = []
        for i in near:
            mate = rcv_count - 1 - i
            if (mate + offset) % rcv_count == (i + half) % rcv_count:
                pairs.append((order[mate], order[i]))
        return pairs

    collect([rows_of[0]])
    inside = [0] + [o for step in range(1, steps) for o in (-step, step)]
    outside = [-steps, steps]

    def as_rows(offsets):
        return [(rows_of[o][0], rows_of[o][1] * rows) for o in offsets]

    for step in range(2, steps + 1):
        collect([rows_of[1 - step], rows_of[step - 1]])
        moved = []
        for part in range(2):
            moved.append(lax.ppermute(ahead[part], "rcv", forward))
            moved.append(lax.ppermute(behind[part], "rcv", backward))
        ahead, behind = moved[0::2], moved[1::2]
        rows_of[-step], rows_of[step] = (ahead, origin(-step)), (behind, origin(step))
    taken = [hop(rows_of[offset][0], from_mate(offset)) for offset in (-1, 1)]
    late_from = len(columns)
    collect([rows_of[-steps], rows_of[steps]])
    far_by_part = []
    for part, pairs in enumerate((forward, backward)):
        block, receiver = rows_of[(-steps, steps)[part]], (place + (1, -1)[part]) % rcv_count
        piece = cut([block], np.asarray(order)[receiver], gains, device, (part,))
        piece = lax.ppermute(piece, "rcv", pairs)
        far_by_part.append(exchange(piece))
    note([((first, second), mask) for (first, mask), (second, _) in zip(*far_by_part)], [far])
    early, late = columns[:late_from], columns[late_from:]
    absent = pack = [(c[2], c[3]) for c in late]
    jobs = [Job(as_rows(inside), early, absent, pack=pack)]
    out, packed_inside = launch(device, None, jobs, used, span, total)
    turns = [
        [(order[(i + d) % rcv_count], order[i]) for i in range(rcv_count) if i not in near]
        for d in (-1, 1)
    ]
    last = []
    for part in range(2):
        last.append(lax.ppermute((ahead[0], behind[1])[part], "rcv", turns[part]))
    jobs = [Job(as_rows(outside), early, absent, pack=pack)]
    out, packed_outside = launch(device, out, jobs, used, span, total)
    chosen = np.zeros(devices)
    for number, offset in enumerate((-1, 1), start=1):
        for _, target in from_mate(offset):
            chosen[mine == target] = number
    candidates = (*last, *taken[0], *taken[1])
    packed = [(packed_inside, len(inside)), (packed_outside, len(outside))]
    splits = [len(inside) // 2, len(inside)]
    near_rows = Job(as_rows(inside + outside), late, packed=packed, splits=splits)
    far_rows = Job([(candidates, far * rows)], columns, choice=chosen)
    return launch(device, out, [near_rows, far_rows], used, span, total)[0]


def solution(mesh):
    placed = (
        P(None, ("src", "rcv"), None),
        P(("src", "rcv"), None),
        P(),
        P("src", None, None),
        P("src", "rcv"),
    )

    return jax.shard_map(
        local, mesh=mesh, in_specs=placed, out_specs=P(None, "src", "rcv"), check_vma=False
    )
```

```python
import jax
import jax.numpy as jnp
import numpy as np
from jax import lax
from jax.experimental import pallas as pl
from jax.experimental.pallas import tpu as pltpu
from jax.sharding import PartitionSpec as P


TILE_SIZE = 512
AHEAD = 2


def ring_order(count):
    return list(range(0, count, 2)) + list(range(1, count, 2))[::-1]


def split_kernel(data_ref, *out_refs):
    rows = data_ref.shape[1]
    for part, out_ref in enumerate(out_refs):
        for block in range(out_ref.shape[0]):
            out_ref[block] = data_ref[part, :, block * rows : (block + 1) * rows].T


def transposed_blocks(data, devices):
    _, rows, _ = data.shape
    if rows % 128:
        return tuple(jnp.transpose(p.reshape(rows, devices, rows), (1, 0, 2)) for p in data)
    group = 16
    return pl.pallas_call(
        split_kernel,
        out_shape=(jax.ShapeDtypeStruct((devices, rows, rows), data.dtype),) * 2,
        grid=(devices // group,),
        in_specs=[pl.BlockSpec((2, rows, group * rows), lambda i: (0, 0, i))],
        out_specs=(pl.BlockSpec((group, rows, rows), lambda i: (i, 0, 0)),) * 2,
    )(data)


def fill_kernel(data_ref, mask_ref, arrived_ref, out_ref):
    rows = data_ref.shape[0]
    for block in range(arrived_ref.shape[0]):
        span = slice(block * rows, (block + 1) * rows)
        out_ref[:, span] = jnp.where(
            mask_ref[:, span] == 1, data_ref[:, span], arrived_ref[block]
        )


def fill(data, mask, arrived, part):
    _, rows, total = data.shape
    devices = arrived.shape[0]
    if rows % 128:
        transposed = jnp.transpose(arrived, (2, 0, 1)).reshape(rows, total)
        return jnp.where(mask == 1, data[part], transposed)
    group = 16
    return pl.pallas_call(
        fill_kernel,
        out_shape=jax.ShapeDtypeStruct((rows, total), data.dtype),
        grid=(devices // group,),
        in_specs=[
            pl.BlockSpec((None, rows, group * rows), lambda i: (part, 0, i)),
            pl.BlockSpec((rows, group * rows), lambda i: (0, i)),
            pl.BlockSpec((group, rows, rows), lambda i: (i, 0, 0)),
        ],
        out_specs=pl.BlockSpec((rows, group * rows), lambda i: (0, i)),
    )(data, mask, arrived)


def product_kernel(rows, plan_ref, used_ref, *refs):
    (row_refs, piece_refs), out_ref, scratch = refs[0], refs[1], refs[2:]
    left, right, row_sem, piece_sem = scratch
    inner_tiles = right.shape[0]
    out_tiles = out_ref.shape[1] // TILE_SIZE

    def piece_copies():
        copies = []
        at = len(row_refs)
        for ref in piece_refs:
            for index in range(ref.shape[0]):
                first = plan_ref[at]
                tile, offset = first // TILE_SIZE, first % TILE_SIZE
                for part in range(2):
                    row = pl.multiple_of(offset + (1 - part) * TILE_SIZE, rows)
                    copies.append(
                        pltpu.make_async_copy(
                            ref.at[index, part],
                            right.at[tile, pl.ds(row, rows), :],
                            piece_sem,
                        )
                    )
                at += 1
        return copies

    def start_rows(tile):
        for index, (ref, part) in enumerate(row_refs):
            row = pl.multiple_of(plan_ref[index], rows)
            column = pl.multiple_of(tile * 2 * TILE_SIZE + part * TILE_SIZE, TILE_SIZE)
            pltpu.make_async_copy(
                ref.at[:, pl.ds(pl.multiple_of(tile * TILE_SIZE, TILE_SIZE), TILE_SIZE)],
                left.at[pl.ds(row, rows), pl.ds(column, TILE_SIZE)],
                row_sem.at[tile],
            ).start()

    for copy in piece_copies():
        copy.start()

    @pl.loop(0, inner_tiles)
    def _(tile):
        start_rows(tile)

    out_ref[...] = jnp.zeros_like(out_ref)
    pltpu.make_async_copy(
        right.at[:, pl.ds(0, 2 * TILE_SIZE), :], right.at[:, pl.ds(0, 2 * TILE_SIZE), :], piece_sem
    ).wait()

    @pl.loop(0, inner_tiles)
    def _(tile):
        columns = pl.ds(pl.multiple_of(tile * 2 * TILE_SIZE, 2 * TILE_SIZE), 2 * TILE_SIZE)
        pltpu.make_async_copy(left.at[:, columns], left.at[:, columns], row_sem.at[tile]).wait()
        right[tile, 2 * TILE_SIZE :, :] = -right[tile, :TILE_SIZE, :]

        @pl.loop(0, out_tiles)
        def _(out_tile):
            @pl.when(used_ref[out_tile, tile] == 1)
            def _():
                span = pl.ds(pl.multiple_of(out_tile * TILE_SIZE, TILE_SIZE), TILE_SIZE)
                lhs = left[span, columns]
                for part in range(2):
                    rhs = right[tile, pl.ds((1 - part) * TILE_SIZE, 2 * TILE_SIZE), :]
                    out_ref[part, span, :] += jnp.dot(lhs, rhs, preferred_element_type=jnp.float32)


def product(row_buffers, row_starts, pieces, piece_starts, used, span, total):
    rows = row_buffers[0][0].shape[0]
    parts = [part for _, part in row_buffers]
    arrays = [array for array, _ in row_buffers] + list(pieces)
    plan = jnp.stack(row_starts + piece_starts).astype(jnp.int32)

    def kernel(plan_ref, used_ref, *refs):
        ins = refs[: len(arrays)]
        row_refs = list(zip(ins[: len(parts)], parts))
        product_kernel(
            rows, plan_ref, used_ref, (row_refs, ins[len(parts) :]), *refs[len(arrays) :]
        )

    inner_tiles = total // TILE_SIZE
    return pl.pallas_call(
        kernel,
        out_shape=jax.ShapeDtypeStruct((2, span, TILE_SIZE), jnp.float32),
        grid_spec=pltpu.PrefetchScalarGridSpec(
            num_scalar_prefetch=2,
            grid=(1,),
            in_specs=[pl.BlockSpec(memory_space=pl.ANY)] * len(arrays),
            out_specs=pl.BlockSpec((2, span, TILE_SIZE), lambda i, *_: (0, 0, 0), pipeline_mode=pl.Buffered(1)),
            scratch_shapes=[
                pltpu.VMEM((span, 2 * total), jnp.bfloat16),
                pltpu.VMEM((inner_tiles, 3 * TILE_SIZE, TILE_SIZE), jnp.bfloat16),
                pltpu.SemaphoreType.DMA((inner_tiles,)),
                pltpu.SemaphoreType.DMA,
            ],
        ),
        compiler_params=pltpu.CompilerParams(vmem_limit_bytes=67_000_000),
    )(plan, used, *arrays)


def cut_kernel(device_ref, place_ref, *refs):
    planes, out_ref = refs[:-1], refs[-1]
    for block in range(out_ref.shape[0]):
        first, second, gain = planes[3 * block : 3 * block + 3]
        for part, ref in enumerate((first, second)):
            out_ref[block, part] = (ref[...].astype(jnp.float32) * gain[...]).astype(jnp.bfloat16)


def cut(blocks, column, gains, device):
    rows = blocks[0][0][0].shape[0]
    place = np.stack([column] + [first for _, first in blocks], axis=1).astype(np.int32)
    specs, operands = [], []
    for index, (planes, _) in enumerate(blocks):
        specs += [pl.BlockSpec((rows, TILE_SIZE), lambda i, me, place: (0, place[me[0], 0]))] * 2
        specs.append(
            pl.BlockSpec((None, rows, 1), lambda i, me, place, at=index + 1: (place[me[0], at], 0, 0))
        )
        operands += [planes[0], planes[1], gains]
    shape = (len(blocks), 2, rows, TILE_SIZE)
    return pl.pallas_call(
        cut_kernel,
        out_shape=jax.ShapeDtypeStruct(shape, jnp.bfloat16),
        grid_spec=pltpu.PrefetchScalarGridSpec(
            num_scalar_prefetch=2,
            grid=(1,),
            in_specs=specs,
            out_specs=pl.BlockSpec(shape, lambda i, me, place: (0, 0, 0, 0)),
        ),
    )(device, jnp.asarray(place), *operands)


class Job:
    def __init__(self, row_blocks, columns, absent=(), choice=None, pack=(), packed=(), splits=()):
        self.row_blocks, self.columns, self.absent = row_blocks, columns, list(absent)
        self.choice, self.pack, self.packed = choice, list(pack), list(packed)
        self.planes = [] if packed else [p for planes, _ in row_blocks for p in planes]
        self.sources, self.source_at = [], []
        for pieces, *_ in columns:
            if not any(pieces is source for source in self.sources):
                self.sources.append(pieces)
            self.source_at.append([pieces is source for source in self.sources].index(True))
        self.rows = columns[0][0].shape[2]
        self.count = len(row_blocks)
        self.chunks = 1 if packed else 1 + max(column[3] for column in columns)
        bounds = [0, *splits, self.count]
        self.turns = list(zip(bounds[:-1], bounds[1:]))

    def numbers(self):
        listed = [first for _, first in self.row_blocks] + [column[2] for column in self.columns]
        listed += [first for first, _ in self.absent + self.pack]
        return listed + ([] if self.choice is None else [self.choice])

    def operands(self):
        return self.planes + self.sources + [array for array, _ in self.packed]

    def depth(self, total):
        return len(self.columns) * self.rows if self.packed else total

    def scratch(self, total):
        height, depth = self.count * self.rows, self.depth(total)
        shapes = [
            pltpu.VMEM((self.chunks, 2, height, depth // self.chunks), jnp.bfloat16),
            pltpu.VMEM((self.chunks, 2, depth // self.chunks, TILE_SIZE), jnp.bfloat16),
            pltpu.VMEM((2, height, TILE_SIZE), jnp.float32),
            pltpu.SemaphoreType.DMA((len(self.turns), self.chunks)),
            pltpu.SemaphoreType.DMA((self.chunks,)),
            pltpu.SemaphoreType.DMA((len(self.turns) + 1,)),
        ]
        if self.pack:
            shapes.append(pltpu.VMEM((2, height, len(self.pack) * self.rows), jnp.bfloat16))
            shapes.append(pltpu.SemaphoreType.DMA)
        return shapes

    def bind(self, number, used_ref, refs, out_ref, pack_ref, scratch, total):
        self.number, self.used_ref, self.out_ref, self.pack_ref = number, used_ref, out_ref, pack_ref
        self.plane_refs = refs[: len(self.planes)]
        self.source_refs = refs[len(self.planes) : len(self.planes) + len(self.sources)]
        self.packed_refs = refs[len(self.planes) + len(self.sources) :]
        self.left, self.right, self.held, self.left_sem, self.right_sem, self.held_sem = scratch[:6]
        self.packing = scratch[6:]
        self.chunk_depth = self.depth(total) // self.chunks
        self.members = [
            [at for at, column in enumerate(self.columns) if self.packed or column[3] == chunk]
            for chunk in range(self.chunks)
        ]

    def first_of(self, at):
        return pl.multiple_of(self.number(at), self.rows)

    def start_row(self, chunk):
        return self.number(self.count + self.members[chunk][0]) // self.chunk_depth * self.chunk_depth

    def within(self, at):
        return pl.multiple_of(self.number(at) % self.chunk_depth, self.rows)

    def held_copy(self, block, part, out, sem):
        here = self.held.at[part, pl.ds(block * self.rows, self.rows), :]
        there = self.out_ref.at[part, pl.ds(self.first_of(block), self.rows), :]
        return pltpu.make_async_copy(*((here, there) if out else (there, here)), sem)

    def start_right(self, chunk):
        for at in self.members[chunk]:
            row = at * self.rows if self.packed else self.within(self.count + at)
            for part in range(2):
                pltpu.make_async_copy(
                    self.source_refs[self.source_at[at]].at[self.columns[at][1], part],
                    self.right.at[chunk, part, pl.ds(row, self.rows), :],
                    self.right_sem.at[chunk],
                ).start()

    def start_left(self, turn, chunk):
        sem = self.left_sem.at[turn, chunk]
        first, end = self.turns[turn]
        rows, base = self.rows, 0
        for ref, (_, blocks) in zip(self.packed_refs, self.packed):
            low, high = max(first, base), min(end, base + blocks)
            if low < high:
                pltpu.make_async_copy(
                    ref.at[:, pl.ds((low - base) * rows, (high - low) * rows), :],
                    self.left.at[chunk, :, pl.ds(low * rows, (high - low) * rows), :],
                    sem,
                ).start()
            base += blocks
        if self.packed:
            return
        inner = pl.ds(pl.multiple_of(self.start_row(chunk), self.chunk_depth), self.chunk_depth)
        for block in range(first, end):
            for part in range(2):
                here = self.left.at[chunk, part, pl.ds(block * rows, rows), :]
                candidates = 1 if self.choice is None else len(self.planes) // 2
                for at in range(candidates):
                    ref = self.plane_refs[2 * (block + at) + part]
                    copy = pltpu.make_async_copy(ref.at[:, inner], here, sem)
                    if self.choice is None:
                        copy.start()
                    else:
                        pl.when(self.number(len(self.numbers()) - 1) == at)(copy.start)

    def steps(self):
        return [(self, turn, chunk) for turn in range(len(self.turns)) for chunk in range(self.chunks)]

    def start(self, turn, chunk):
        if turn == 0:
            self.start_right(chunk)
        self.start_left(turn, chunk)
        if self.packed:
            for block in range(*self.turns[turn]):
                for part in range(2):
                    self.held_copy(block, part, False, self.held_sem.at[turn]).start()

    def clear_absent(self, chunk):
        for at, (_, owner) in enumerate(self.absent):
            if owner == chunk:
                row = self.within(self.count + len(self.columns) + at)
                self.right[chunk, :, pl.ds(row, self.rows), :] = jnp.zeros(
                    (2, self.rows, TILE_SIZE), jnp.bfloat16
                )

    def wait(self, turn, chunk):
        first, end = self.turns[turn]
        height = (end - first) * self.rows
        views = [(self.left.at[chunk, :, pl.ds(0, height), :], self.left_sem.at[turn, chunk])]
        if turn == 0:
            rows = len(self.members[chunk]) * self.rows
            views.append((self.right.at[chunk, :, pl.ds(0, rows), :], self.right_sem.at[chunk]))
        if self.packed:
            views.append((self.held.at[:, pl.ds(0, height), :], self.held_sem.at[turn]))
        for view, sem in views:
            pltpu.make_async_copy(view, view, sem).wait()

    def mask(self, chunk, first, end):
        rows = self.rows
        for block in range(first, end):
            own_tile = self.number(block) // TILE_SIZE
            for offset in range(0, self.chunk_depth, TILE_SIZE):
                tile = (self.start_row(chunk) + offset) // TILE_SIZE

                @pl.when(self.used_ref[own_tile, tile] == 0)
                def _():
                    self.left[
                        chunk, :, block * rows : (block + 1) * rows, offset : offset + TILE_SIZE
                    ] = jnp.zeros((2, rows, TILE_SIZE), jnp.bfloat16)

    def write_packed(self, chunk, first, end):
        rows, (packing, sem) = self.rows, self.packing
        pack_at = self.count + len(self.columns) + len(self.absent)
        band = slice(first * rows, end * rows)
        for at, (_, owner) in enumerate(self.pack):
            if owner == chunk:
                to = slice(at * rows, (at + 1) * rows)
                packing[:, band, to] = self.left[chunk, :, band, pl.ds(self.within(pack_at + at), rows)]
                area = (slice(None), pl.ds(first * rows, (end - first) * rows), pl.ds(at * rows, rows))
                pltpu.make_async_copy(packing.at[area], self.pack_ref.at[area], sem).start()

    def products(self, chunk, band):
        by_part = ((0, 0, 1, 1), (0, 1, 1, 0))
        out = []
        for part, (a, b, c, d) in enumerate(by_part):
            first = jnp.dot(
                self.left[chunk, a, band], self.right[chunk, b], preferred_element_type=jnp.float32
            )
            second = jnp.dot(
                self.left[chunk, c, band], self.right[chunk, d], preferred_element_type=jnp.float32
            )
            out.append(first + second if part else first - second)
        return out

    def run(self, turn, chunk):
        rows, held = self.rows, self.held
        first, end = self.turns[turn]
        band = slice(first * rows, end * rows)
        if not self.packed:
            self.mask(chunk, first, end)
            if turn == 0:
                self.clear_absent(chunk)
        if self.pack:
            self.write_packed(chunk, first, end)
        sums = self.products(chunk, band)
        for part in range(2):
            if chunk == 0 and not self.packed:
                held[part, band] = sums[part]
            else:
                held[part, band] += sums[part]
            if chunk == self.chunks - 1:
                for block in range(first, end):
                    self.held_copy(block, part, True, self.held_sem.at[len(self.turns)]).start()

    def finish(self):
        if self.pack:
            pltpu.make_async_copy(self.packing[0], self.pack_ref, self.packing[1]).wait()
        pltpu.make_async_copy(self.held, self.held, self.held_sem.at[len(self.turns)]).wait()


def launch(device, base, jobs, used, span, total):
    plan = np.stack([n for job in jobs for n in job.numbers()], axis=1).astype(np.int32)
    operands = [array for job in jobs for array in job.operands()]
    operands += [] if base is None else [base]
    packing = [job for job in jobs if job.pack]
    scratch = [job.scratch(total) for job in jobs]
    out_shape = [jax.ShapeDtypeStruct((2, span, TILE_SIZE), jnp.float32)]
    for job in packing:
        shape = (2, job.count * job.rows, len(job.pack) * job.rows)
        out_shape.append(jax.ShapeDtypeStruct(shape, jnp.bfloat16))

    def kernel(device_ref, plan_ref, used_ref, *refs):
        outs = refs[len(operands) : len(operands) + len(out_shape)]
        spare = refs[len(operands) + len(out_shape) :]
        at, spare_at, plan_at = 0, 0, 0
        for job, shapes in zip(jobs, scratch):
            size = len(job.operands())
            job.bind(
                lambda n, plan_at=plan_at: plan_ref[device_ref[0], plan_at + n],
                used_ref,
                refs[at : at + size],
                outs[0],
                outs[1 + packing.index(job)] if job.pack else None,
                spare[spare_at : spare_at + len(shapes)],
                total,
            )
            at, spare_at, plan_at = at + size, spare_at + len(shapes), plan_at + len(job.numbers())
        steps = [step for job in jobs for step in job.steps()]
        for job, *step in steps[:AHEAD]:
            job.start(*step)
        for at, (job, *step) in enumerate(steps):
            job.wait(*step)
            for later, *later_step in steps[at + AHEAD : at + AHEAD + 1]:
                later.start(*later_step)
            job.run(*step)
        for job in jobs:
            job.finish()

    flops = sum(8 * job.count * job.rows * job.depth(total) * TILE_SIZE for job in jobs)
    return pl.pallas_call(
        kernel,
        out_shape=out_shape,
        grid_spec=pltpu.PrefetchScalarGridSpec(
            num_scalar_prefetch=3,
            grid=(1,),
            in_specs=[pl.BlockSpec(memory_space=pl.ANY)] * len(operands),
            out_specs=[pl.BlockSpec(memory_space=pl.ANY)] * len(out_shape),
            scratch_shapes=[shape for shapes in scratch for shape in shapes],
        ),
        input_output_aliases={} if base is None else {3 + len(operands) - 1: 0},
        cost_estimate=pl.CostEstimate(flops=flops, bytes_accessed=20 * span * total, transcendentals=0),
        compiler_params=pltpu.CompilerParams(vmem_limit_bytes=60 * 1024 * 1024),
    )(device, jnp.asarray(plan), used, *operands)


def used_tiles(aperture, lengths, rcv_index, total):
    lists = lax.dynamic_index_in_dim(aperture, rcv_index, 1, keepdims=False)
    slot = jnp.arange(lists.shape[1], dtype=jnp.int32)
    wanted = (slot[None, :] < lengths)[:, :, None]
    tiles = jnp.arange(total // TILE_SIZE, dtype=jnp.int32)
    return jnp.any(wanted & (lists[:, :, None] == tiles), axis=1).astype(jnp.int32)


def local(data, fill_mask, obliquity, aperture, lengths):
    _, rows, total = data.shape
    src_count = lax.axis_size("src")
    rcv_count = lax.axis_size("rcv")
    src_index = lax.axis_index("src")
    rcv_index = lax.axis_index("rcv")
    devices = src_count * rcv_count
    span = rows * rcv_count
    device = (src_index * rcv_count + rcv_index).reshape(1)
    phased = rows % 128 == 0 and rcv_count % 4 == 0 and rcv_count > 4

    order = ring_order(rcv_count)
    owner, mine = np.divmod(np.arange(devices), rcv_count)
    place = np.asarray([order.index(i) for i in range(rcv_count)])[mine]
    half = rcv_count // 2
    steps = (rcv_count - 1) // 2

    def origin(offset):
        return np.asarray(order)[(place + offset) % rcv_count]

    def here(numbers):
        return jnp.asarray(numbers, jnp.int32)[device[0]]

    forward = [(order[i], order[(i + 1) % rcv_count]) for i in range(rcv_count)]
    backward = [(b, a) for a, b in forward]

    def hop(planes, pairs):
        return tuple(lax.ppermute(p, "rcv", pairs) for p in planes)

    used = used_tiles(aperture, lengths, rcv_index, total)
    my_gains = -lax.dynamic_slice_in_dim(obliquity, src_index * span, span)
    gains = my_gains.reshape(rcv_count, rows, 1)

    def tiles_of(blocks, column):
        if phased:
            return cut(blocks, column, gains, device)
        out = []
        for planes, first in blocks:
            start = here(column) * TILE_SIZE
            cuts = [lax.dynamic_slice_in_dim(p, start, TILE_SIZE, 1) for p in planes]
            gain = lax.dynamic_index_in_dim(gains, here(first), 0, keepdims=True)
            out.append((jnp.stack(cuts).astype(jnp.float32) * gain).astype(jnp.bfloat16))
        return jnp.stack(out)

    columns = []

    def spread(held, origins):
        held_by = [(held, 0)]
        bit = src_count // 2
        while bit:
            swap = [(i, i ^ bit) for i in range(src_count)]
            held_by += [(lax.ppermute(x, "src", swap), mask ^ bit) for x, mask in held_by]
            bit //= 2
        for pieces, mask in held_by:
            for index, first in enumerate(origins):
                columns.append((pieces, index, (owner ^ mask) * span + first * rows, mask))

    def collect(blocks):
        tiles = tiles_of(blocks, mine)
        spread(tiles, [first for _, first in blocks])

    blocks = transposed_blocks(data, devices)
    arrived = [
        lax.all_to_all(b, ("src", "rcv"), split_axis=0, concat_axis=0, tiled=True) for b in blocks
    ]
    own, ahead, behind = [], [], []
    for part in range(2):
        own.append(fill(data, fill_mask, arrived[part], part))
        ahead.append(lax.ppermute(own[part], "rcv", forward))
        behind.append(lax.ppermute(own[part], "rcv", backward))

    rows_of = {0: (own, origin(0)), -1: (ahead, origin(-1)), 1: (behind, origin(1))}
    far = origin(half)
    if not phased:
        collect([rows_of[0]])
        collect([rows_of[-1], rows_of[1]])
        for step in range(2, steps + 1):
            ahead, behind = hop(ahead, forward), hop(behind, backward)
            rows_of[-step], rows_of[step] = (ahead, origin(-step)), (behind, origin(step))
            collect([rows_of[-step], rows_of[step]])
        if rcv_count % 2 == 0:
            last = hop(ahead[:1], forward) + hop(behind[1:], backward)
            rows_of[half] = (last, far)
            collect([rows_of[half]])
        row_buffers, row_starts, pieces, starts = [], [], [], []
        for planes, first in rows_of.values():
            row_buffers += [(planes[0], 0), (planes[1], 1)]
            row_starts += [here(first * rows)] * 2
        for array, index, first, _ in columns:
            if index == 0:
                pieces.append(array)
            starts.append(here(first))
        return product(row_buffers, row_starts, pieces, starts, used, span, total)

    quarter = rcv_count // 4
    near = [quarter - 1, quarter, rcv_count - 1 - quarter, rcv_count - quarter]

    def from_mate(offset):
        pairs = []
        for i in near:
            mate = rcv_count - 1 - i
            if (mate + offset) % rcv_count == (i + half) % rcv_count:
                pairs.append((order[mate], order[i]))
        return pairs

    collect([rows_of[0]])
    inside = [0] + [o for step in range(1, steps) for o in (-step, step)]
    outside = [-steps, steps]

    def as_rows(offsets):
        return [(rows_of[o][0], rows_of[o][1] * rows) for o in offsets]

    for step in range(2, steps + 1):
        collect([rows_of[1 - step], rows_of[step - 1]])
        moved = []
        for part in range(2):
            moved.append(lax.ppermute(ahead[part], "rcv", forward))
            moved.append(lax.ppermute(behind[part], "rcv", backward))
        ahead, behind = moved[0::2], moved[1::2]
        rows_of[-step], rows_of[step] = (ahead, origin(-step)), (behind, origin(step))
    taken = [hop(rows_of[offset][0], from_mate(offset)) for offset in (-1, 1)]
    late_from = len(columns)
    collect([rows_of[-steps], rows_of[steps]])
    across = [(order[i], order[(i + half) % rcv_count]) for i in range(rcv_count)]
    far_pieces = cut([(own, origin(0))], far, gains, device)
    far_pieces = lax.ppermute(far_pieces, "rcv", across)
    spread(far_pieces, [far])
    early, late = columns[:late_from], columns[late_from:]
    absent = pack = [(c[2], c[3]) for c in late]
    jobs = [Job(as_rows(inside), early, absent, pack=pack)]
    out, packed_inside = launch(device, None, jobs, used, span, total)
    turns = [
        [(order[(i + d) % rcv_count], order[i]) for i in range(rcv_count) if i not in near]
        for d in (-1, 1)
    ]
    last = []
    for part, plane in enumerate((ahead[0], behind[1])):
        last.append(lax.ppermute(plane, "rcv", turns[part]))
    jobs = [Job(as_rows(outside), early, absent, pack=pack)]
    out, packed_outside = launch(device, out, jobs, used, span, total)
    chosen = np.zeros(devices)
    for number, offset in enumerate((-1, 1), start=1):
        for _, target in from_mate(offset):
            chosen[mine == target] = number
    candidates = (*last, *taken[0], *taken[1])
    packed = [(packed_inside, len(inside)), (packed_outside, len(outside))]
    splits = [len(inside) // 2, len(inside)]
    near_rows = Job(as_rows(inside + outside), late, packed=packed, splits=splits)
    far_rows = Job([(candidates, far * rows)], columns, choice=chosen)
    return launch(device, out, [near_rows, far_rows], used, span, total)[0]


def solution(mesh):
    placed = (
        P(None, ("src", "rcv"), None),
        P(("src", "rcv"), None),
        P(),
        P("src", None, None),
        P("src", "rcv"),
    )

    return jax.shard_map(
        local, mesh=mesh, in_specs=placed, out_specs=P(None, "src", "rcv"), check_vma=False
    )
```
